32 devices in a mesh: groups: 1, dev: 8 (over z, y), side: 4 (over x, core).
Axes of the slice: x: 2, y: 2, z: 4, core: 2. Of those that a mesh axis runs over, the one named last changes fastest.
Arguments:
- queries: bfloat16 [256, 4096], P(('groups', 'dev', 'side')), may hold values from -160 to 160
- kv_cache: bfloat16 [256, 192, 1024], P(('groups', 'dev', 'side')), may hold values from -4 to 4
- new_kv: bfloat16 [256, 1024], P(('groups', 'dev', 'side')), may hold values from -4 to 4
- lengths: int32 [256], P(('groups', 'dev', 'side')), may hold values from 24 to 192, as said below
- residual: bfloat16 [256, 2048], P(('groups', 'dev', 'side')), may hold values from -36 to 36
- w_out: bfloat16 [4096, 2048], P('side'), may hold values from -0.59765625 to 0.59765625
- norm_gain: float32 [2048], replicated, may hold values from 0.5 to 1.5
- expert_ids: int32 [256, 8], P(('groups', 'dev', 'side')), may hold values from 0 to 15, all different within a row; in each aligned block of 8 rows (0 to 7, 8 to 15, ...) at most 8 rows name the same one
- route_level: int32 [256, 8], P(('groups', 'dev', 'side')), may hold values from 1 to 255
- w_in: bfloat16 [32, 2048, 768], P(('dev', 'side')), may hold values from -0.125 to 0.125
- w_down: bfloat16 [32, 384, 2048], P(('dev', 'side')), may hold values from -0.4375 to 0.4375
Outputs:
- stream: bfloat16 [256, 2048], P(('groups', 'dev', 'side'))
- expert_sum: bfloat16 [256, 2048], P(('groups', 'dev', 'side'))
The draws below stay inside these ranges and needn't reach their ends.
Inputs may be any that keep to these rules, and one draw needn't show every extreme that they name: `lengths`: in each aligned block of 8 requests some request has 192 cached tokens. `expert_ids`: A row names 8 different experts. In each aligned block of 8 rows no expert is named by more than 8 rows, and in some block some expert is named by exactly 8 rows.
All inputs are finite; a program needn't handle non-finite values.
Results may differ from the reference program's by a relative error of at most 0.013.
Values may be sent and summed in bfloat16 or wider, within the bound.
No kernel may reach another device: no remote copies, remote signals or barrier semaphores. Data moves between devices by JAX's collectives and lax.ppermute only.
A program may use at most 64 MiB of HBM per device.

```python
import math
import jax
import jax.numpy as jnp
import numpy as np
from jax import lax

D = 2048
HQ = 32
KVH = 4
HD = 128
FF = 768
TOPK = 8
CACHE = 192
REQ_DEV = 8
REQ = 256
SHARDS = 32
EXPERTS = 16
FH = 384
MOST = 8


def attention_parts(key):
    base_key = jax.random.fold_in(key, 11)
    subkeys = jax.random.split(base_key, 2)
    kv_values = jnp.clip(jax.random.normal(subkeys[0], (REQ, CACHE, 2 * KVH * HD), jnp.float32), -4.0, 4.0)
    queries = jnp.clip(jax.random.normal(subkeys[1], (REQ, HQ * HD), jnp.float32), -4.0, 4.0)
    return (queries, kv_values)


def draw_queries(key, part):
    return attention_parts(key)[0].astype(jnp.bfloat16)


def draw_kv_cache(key, part):
    return attention_parts(key)[1].astype(jnp.bfloat16)


def draw_lengths(key, part):
    subkeys = jax.random.split(jax.random.fold_in(key, 31), 2)
    drawn = jax.random.randint(subkeys[0], (REQ,), CACHE // 8, CACHE + 1)
    longest = jax.random.randint(subkeys[1], (REQ // REQ_DEV,), 0, REQ_DEV)
    indices = jnp.arange(REQ)
    chosen = indices % REQ_DEV == jnp.repeat(longest, REQ_DEV, total_repeat_length=REQ)
    return jnp.where(chosen, CACHE, drawn).astype(jnp.int32)


def draw_residual(key, part):
    subkeys = jax.random.split(jax.random.fold_in(key, 23), 3)
    lower = math.log(0.3)
    upper = math.log(3.0)
    column_scale = jnp.exp(jax.random.uniform(subkeys[1], (D,), jnp.float32, lower, upper))
    row_scale = jnp.exp(jax.random.uniform(subkeys[2], (REQ,), jnp.float32, lower, upper))
    noise = jnp.clip(jax.random.normal(subkeys[0], (REQ, D), jnp.float32), -4.0, 4.0)
    return (noise * row_scale[:, None] * column_scale[None, :]).astype(jnp.bfloat16)


def with_ends(entries, own_key, smallest, largest):
    place = [jax.random.randint(jax.random.fold_in(own_key, axis), (), 0, length) for axis, length in enumerate(entries.shape)]
    widest = entries.shape.index(max(entries.shape))
    next_to = place[:widest] + [(place[widest] + 1) % entries.shape[widest]] + place[widest + 1:]
    return entries.at[tuple(place)].set(smallest).at[tuple(next_to)].set(largest)


def level_of(stream_key, extent, cuts, least, top_value):
    def one(dim, parts):
        heights = jax.random.uniform(jax.random.fold_in(jax.random.fold_in(stream_key, 6), dim), (parts,), jnp.float32, least / len(cuts), top_value / len(cuts))
        return jnp.repeat(jnp.exp(heights), extent[dim] // parts).reshape((-1,) + (1,) * (len(extent) - dim - 1))

    level = one(*cuts[0])
    for cut in cuts[1:]:
        level = level * one(*cut)
    return level


def routed_block(key, own, number, rows, amount, top, reach, slope):
    sequence = jax.random.permutation(key, amount)
    heavy_load, usual = load_shares(amount, rows * top, reach, slope, True), load_shares(amount, rows * top, reach, slope, False)
    places = jnp.arange(amount)

    def named(sizes, rotation):
        used = int((sizes > 0).sum())
        fixed = max(1, used // 4)
        shifted = fixed + (places - fixed + rotation * (used - fixed)) % max(1, amount - fixed)
        return jnp.zeros((amount,), jnp.int32).at[sequence[jnp.where(places < fixed, places, shifted)]].set(jnp.asarray(sizes, jnp.int32))

    sizes = jnp.where(number % 4 == 0, named(heavy_load, number // 4), named(usual, number - number // 4 - 1))
    mixed = jax.random.permutation(jax.random.fold_in(own, 3), amount)
    donor, receiver = mixed[0:amount // 2 * 2:2], mixed[1:amount // 2 * 2:2]
    room = jnp.minimum(sizes[donor] - 1, reach - sizes[receiver]) // 2
    room = jnp.where((donor == sequence[0]) | (receiver == sequence[0]) | (sizes[receiver] == 0), 0, jnp.maximum(room, 0))
    shifted = jax.random.randint(jax.random.fold_in(own, 4), (amount // 2,), 0, 1 << 20) % (room + 1)
    sizes = sizes.at[donor].add(-shifted).at[receiver].add(shifted)
    items = jnp.searchsorted(jnp.cumsum(sizes), jnp.arange(rows * top), side="right").astype(jnp.int32)
    grid = items.reshape(top, rows).T
    grid = grid[jax.random.permutation(jax.random.fold_in(own, 1), rows)]
    rotation = jax.random.randint(jax.random.fold_in(own, 2), (rows, 1), 0, top)
    return jnp.take_along_axis(grid, (jnp.arange(top)[None, :] + rotation) % top, axis=1)


def load_shares(count, total, limit, lean, full):
    weights = [(1 << 20) // math.isqrt(grade ** lean) + 1 for grade in range(1, count + 1)]
    largest = limit if full else min(limit, max(-(-total // count), total * weights[0] // sum(weights)))
    least = 1 if total - largest >= count - 1 else 0
    given, surplus = [largest] + [least] * (count - 1), total - largest - least * (count - 1)
    while surplus > 0:
        candidates = [i for i in range(1, count) if given[i] < largest] or [i for i in range(1, count) if given[i] < limit]
        mass, remaining = sum([weights[i] for i in candidates]), surplus
        for i in candidates:
            extra = min(limit - given[i], max(1, remaining * weights[i] // mass), surplus)
            given[i] = given[i] + extra
            surplus = surplus - extra
    return np.array(given)


def scatter_about(own_key, shape, spread, most, cuts=(), kind=jnp.bfloat16):
    result = spread * jax.random.normal(own_key, shape, jnp.float32)
    if cuts:
        result = result * level_of(own_key, shape, cuts, -0.22, 0.18)
    return jnp.clip(result, -most, most).astype(kind)


def setup_inputs(seed: int = 0, part: int = 0) -> dict:
    streams_of = jax.random.split(jax.random.key(seed), 12)
    part_splits = jax.random.split(jax.random.fold_in(streams_of[11], part), 12)
    queries = draw_queries(jax.random.fold_in(jax.random.fold_in(streams_of[11], part), 71), part)
    kv_cache = draw_kv_cache(jax.random.fold_in(jax.random.fold_in(streams_of[11], part), 71), part)
    new_kv = scatter_about(part_splits[2], (REQ, 2 * KVH * HD), 1.0, 4.0, ((0, 32),))
    lengths = draw_lengths(jax.random.fold_in(jax.random.fold_in(streams_of[11], part), 71), part)
    residual = draw_residual(jax.random.fold_in(jax.random.fold_in(streams_of[11], part), 71), part)
    w_out = scatter_about(streams_of[5], (HQ * HD, D), 0.1, 0.59765625, ((0, 4),))
    norm_gain = jnp.clip(jax.random.uniform(streams_of[6], (D,), jnp.float32, 0.5, 1.5), 0.5, 1.5)
    expert_ids_keys = jax.random.split(jax.random.fold_in(part_splits[7], 1), REQ // REQ_DEV)
    expert_ids_turns = jax.random.permutation(jax.random.fold_in(part_splits[7], 3), REQ // REQ_DEV)
    expert_ids = jax.vmap(lambda own, number: routed_block(jax.random.fold_in(part_splits[7], 2), own, number, REQ_DEV, EXPERTS, TOPK, MOST, 2))(expert_ids_keys, expert_ids_turns).reshape((REQ, TOPK))
    route_level = with_ends(jax.random.randint(part_splits[8], (REQ, TOPK), 1, 256), jax.random.fold_in(part_splits[8], 1), 1, 255).astype(jnp.int32)
    w_in = scatter_about(streams_of[9], (SHARDS, D, FF), D ** -0.5, 0.125, ((0, 32),))
    w_down = scatter_about(streams_of[10], (SHARDS, FH, D), (FF // 4) ** -0.5, 0.4375, ((0, 32),))
    return {"queries": queries, "kv_cache": kv_cache, "new_kv": new_kv, "lengths": lengths, "residual": residual, "w_out": w_out, "norm_gain": norm_gain, "expert_ids": expert_ids, "route_level": route_level, "w_in": w_in, "w_down": w_down}


def attend_block(operands):
    queries, kv_cache, new_kv, lengths = operands
    req_rows = queries.shape[0]
    group_size = HQ // KVH
    split_at = KVH * HD
    grouped_q = queries.astype(jnp.float32).reshape(req_rows, KVH, group_size, HD)
    key_rows = kv_cache[:, :, :split_at].astype(jnp.float32).reshape(req_rows, CACHE, KVH, HD)
    value_rows = kv_cache[:, :, split_at:].astype(jnp.float32).reshape(req_rows, CACHE, KVH, HD)
    new_key = new_kv[:, :split_at].astype(jnp.float32).reshape(req_rows, KVH, HD)
    new_value = new_kv[:, split_at:].astype(jnp.float32).reshape(req_rows, KVH, HD)
    scaling = 1.0 / math.sqrt(HD)
    scores = jnp.einsum('rgqd,rlgd->rgql', grouped_q, key_rows, precision=lax.Precision.HIGHEST) * scaling
    own_score = jnp.einsum('rgqd,rgd->rgq', grouped_q, new_key, precision=lax.Precision.HIGHEST) * scaling
    visible = (jnp.arange(CACHE)[None, :] < lengths[:, None])[:, None, None, :]
    scores = jnp.where(visible, scores, -jnp.inf)
    peak = jnp.maximum(lax.optimization_barrier(jnp.max(scores, axis=3)), own_score)
    weights = jnp.where(visible, jnp.exp(scores - peak[..., None]), 0.0)
    own_weight = jnp.exp(own_score - peak)
    denominator = lax.optimization_barrier(jnp.sum(weights, axis=3)) + own_weight
    probability = lax.optimization_barrier((weights / denominator[..., None]).astype(jnp.bfloat16)).astype(jnp.float32)
    own_prob = lax.optimization_barrier((own_weight / denominator).astype(jnp.bfloat16)).astype(jnp.float32)
    mixed = jnp.einsum('rgql,rlgd->rgqd', probability, value_rows, precision=lax.Precision.HIGHEST)
    mixed = mixed + own_prob[..., None] * new_value[:, :, None, :]
    return mixed.reshape(req_rows, HQ * HD).astype(jnp.bfloat16)

def reference(queries, kv_cache, new_kv, lengths, residual, w_out, norm_gain, expert_ids, route_level, w_in, w_down):
    blocks = REQ // REQ_DEV
    attended = lax.map(attend_block, (queries.reshape(blocks, REQ_DEV, HQ * HD), kv_cache.reshape(blocks, REQ_DEV, CACHE, 2 * KVH * HD), new_kv.reshape(blocks, REQ_DEV, 2 * KVH * HD), lengths.reshape(blocks, REQ_DEV)))
    attended = attended.reshape(REQ, HQ * HD)
    stream_f = residual.astype(jnp.float32) + jnp.dot(attended, w_out, preferred_element_type=jnp.float32)
    mean_square = lax.optimization_barrier(jnp.mean(stream_f * stream_f, axis=1, keepdims=True))
    normed = (stream_f * lax.rsqrt(mean_square + 1e-06) * norm_gain[None, :]).astype(jnp.bfloat16)
    shares = route_level.astype(jnp.float32)
    shares = shares / lax.optimization_barrier(jnp.sum(shares, axis=1, keepdims=True))
    rows_max = MOST * SHARDS

    def per_expert(expert_acc, expert):
        matches = expert_ids == expert
        chosen = jnp.any(matches, axis=1)
        weight = lax.optimization_barrier(jnp.sum(jnp.where(matches, shares, 0.0), axis=1))
        ordering = jnp.argsort(jnp.logical_not(chosen).astype(jnp.int32), stable=True)[:rows_max].astype(jnp.int32)
        picked = normed[ordering]
        usable = chosen[ordering]
        accum = jnp.zeros((rows_max, D), jnp.float32)
        for half_index in range(2):
            shard_index = 2 * expert + half_index
            gate_up = jnp.dot(picked, w_in[shard_index], preferred_element_type=jnp.float32)
            hidden = (jax.nn.silu(gate_up[:, :FH]) * gate_up[:, FH:]).astype(jnp.bfloat16)
            accum = accum + jnp.dot(hidden, w_down[shard_index], preferred_element_type=jnp.float32)
        rounded = lax.optimization_barrier(accum.astype(jnp.bfloat16)).astype(jnp.float32)
        weighted = jnp.where(usable[:, None], weight[ordering][:, None] * rounded, 0.0)
        return (expert_acc.at[ordering].add(weighted), None)
    expert_acc, unused = lax.scan(per_expert, jnp.zeros((REQ, D), jnp.float32), jnp.arange(EXPERTS, dtype=jnp.int32))
    return (stream_f.astype(jnp.bfloat16), expert_acc.astype(jnp.bfloat16))
```

```python
import math

import jax
import jax.numpy as jnp
from jax import lax
from jax.sharding import PartitionSpec as P

HD = 128


def swap(block, axis, bit):
    count = lax.axis_size(axis)
    return lax.ppermute(block, axis, [(i, i ^ (1 << bit)) for i in range(count)])


def attend(queries, kv_cache, new_kv, lengths):
    rows, features = queries.shape
    cache = kv_cache.shape[1]
    split_at = kv_cache.shape[2] // 2
    kv_heads = split_at // HD
    group_size = features // split_at
    grouped_q = queries.reshape(rows, kv_heads, group_size, HD)
    key_rows = kv_cache[:, :, :split_at].reshape(rows, cache, kv_heads, HD)
    value_rows = kv_cache[:, :, split_at:].reshape(rows, cache, kv_heads, HD)
    new_key = new_kv[:, :split_at].reshape(rows, kv_heads, HD)
    new_value = new_kv[:, split_at:].reshape(rows, kv_heads, HD)
    scaling = 1.0 / math.sqrt(HD)
    scores = (
        jnp.einsum("rgqd,rlgd->rgql", grouped_q, key_rows, preferred_element_type=jnp.float32)
        * scaling
    )
    own_score = (
        jnp.einsum("rgqd,rgd->rgq", grouped_q, new_key, preferred_element_type=jnp.float32)
        * scaling
    )
    visible = (jnp.arange(cache)[None, :] < lengths[:, None])[:, None, None, :]
    scores = jnp.where(visible, scores, -jnp.inf)
    peak = jnp.maximum(jnp.max(scores, axis=3), own_score)
    weights = jnp.where(visible, jnp.exp(scores - peak[..., None]), 0.0)
    own_weight = jnp.exp(own_score - peak)
    denominator = jnp.sum(weights, axis=3) + own_weight
    probability = (weights / denominator[..., None]).astype(jnp.bfloat16)
    own_prob = (own_weight / denominator).astype(jnp.bfloat16)
    mixed = jnp.einsum(
        "rgql,rlgd->rgqd", probability, value_rows, preferred_element_type=jnp.float32
    )
    mixed = (
        mixed
        + own_prob.astype(jnp.float32)[..., None] * new_value.astype(jnp.float32)[:, :, None, :]
    )
    return mixed.reshape(rows, features).astype(jnp.bfloat16)


def project(attended, w_out):
    side_bits = lax.axis_size("side").bit_length() - 1
    mine = lax.axis_index("side")
    block = attended
    for bit in reversed(range(side_bits)):
        half = block.shape[1] // 2
        own_bit = (mine >> bit) & 1
        kept = lax.dynamic_slice_in_dim(block, own_bit * half, half, 1)
        sent = lax.dynamic_slice_in_dim(block, (1 - own_bit) * half, half, 1)
        block = jnp.concatenate([kept, swap(sent, "side", bit)], axis=0)
    total = jnp.dot(block, w_out, preferred_element_type=jnp.float32)
    for bit in range(side_bits):
        half = total.shape[0] // 2
        sent = total[half:]
        if bit:
            sent = sent.astype(jnp.bfloat16)
        total = total[:half] + swap(sent, "side", bit).astype(jnp.float32)
    return total


def body(
    queries,
    kv_cache,
    new_kv,
    lengths,
    residual,
    w_out,
    norm_gain,
    expert_ids,
    route_level,
    w_in,
    w_down,
):
    rows = queries.shape[0]
    width = residual.shape[1]
    half_width = width // 2
    everyone = ("dev", "side")
    shards = lax.axis_size("dev") * lax.axis_size("side")
    experts = shards // 2
    core = lax.axis_index("side") % 2

    attended = attend(queries, kv_cache, new_kv, lengths)
    stream = residual.astype(jnp.float32) + project(attended, w_out)
    mean_square = jnp.mean(stream * stream, axis=1, keepdims=True)
    normed = (stream * lax.rsqrt(mean_square + 1e-06) * norm_gain[None, :]).astype(jnp.bfloat16)
    shares = route_level.astype(jnp.float32)
    shares = shares / jnp.sum(shares, axis=1, keepdims=True)
    chosen = expert_ids[:, :, None] == jnp.arange(experts, dtype=jnp.int32)[None, None, :]
    mixing = jnp.sum(jnp.where(chosen, shares[:, :, None], 0.0), axis=1)

    halves = normed.reshape(rows, 2, half_width).transpose(1, 0, 2)
    outbox = jnp.broadcast_to(halves[None], (experts, 2, rows, half_width))
    arrived = lax.all_to_all(
        outbox.reshape(shards, rows, half_width), everyone, split_axis=0, concat_axis=0, tiled=True
    ).reshape(shards * rows, half_width)
    other = swap(arrived, "side", 0)
    tokens = jnp.where(
        core == 0,
        jnp.concatenate([arrived, other], axis=1),
        jnp.concatenate([other, arrived], axis=1),
    )
    units = w_down.shape[1]
    gate_up = jnp.dot(tokens, w_in[0], preferred_element_type=jnp.float32)
    hidden = (jax.nn.silu(gate_up[:, :units]) * gate_up[:, units:]).astype(jnp.bfloat16)
    partial = jnp.dot(hidden, w_down[0], preferred_element_type=jnp.float32)
    kept = lax.dynamic_slice_in_dim(partial, core * half_width, half_width, 1)
    sent = lax.dynamic_slice_in_dim(partial, (1 - core) * half_width, half_width, 1)
    gained = swap(sent.astype(jnp.bfloat16), "side", 0).astype(jnp.float32)
    finished = (kept + gained).astype(jnp.bfloat16).reshape(shards, rows, half_width)
    returned = lax.all_to_all(finished, everyone, split_axis=0, concat_axis=0, tiled=True)
    returned = returned.reshape(experts, 2, rows, half_width).astype(jnp.float32)
    summed = jnp.sum(returned * mixing.T[:, None, :, None], axis=0)
    expert_sum = summed.transpose(1, 0, 2).reshape(rows, width)
    return (stream.astype(jnp.bfloat16), expert_sum.astype(jnp.bfloat16))


def solution(mesh):
    by_request = ("groups", "dev", "side")
    return jax.shard_map(
        body,
        mesh=mesh,
        in_specs=(
            P(by_request, None),
            P(by_request, None, None),
            P(by_request, None),
            P(by_request),
            P(by_request, None),
            P("side", None),
            P(),
            P(by_request, None),
            P(by_request, None),
            P(("dev", "side"), None, None),
            P(("dev", "side"), None, None),
        ),
        out_specs=(P(by_request, None), P(by_request, None)),
        check_vma=False,
    )
```

```python
import functools
import math

import jax
import jax.numpy as jnp
from jax import lax
from jax.experimental import pallas as pl
from jax.experimental.pallas import tpu as pltpu
from jax.sharding import PartitionSpec as P

HD = 128
GRANT = 16 << 20
VMEM = pl.BlockSpec(memory_space=pltpu.VMEM)
HBM = pl.BlockSpec(memory_space=pltpu.HBM)


def kernel_call(body, name, operands, outs, in_specs=None, scratch=(), cost=None):
    return pl.pallas_call(
        body,
        name=name,
        out_shape=outs,
        in_specs=in_specs or [VMEM] * len(operands),
        out_specs=jax.tree.map(lambda _: VMEM, outs, is_leaf=lambda x: hasattr(x, "shape")),
        scratch_shapes=list(scratch),
        compiler_params=pltpu.CompilerParams(vmem_limit_bytes=GRANT),
        cost_estimate=cost,
    )(*operands)


def partner(block, axis, mask):
    count = lax.axis_size(axis)
    return lax.ppermute(block, axis, [(i, i ^ mask) for i in range(count)])


def attend_kernel(
    q_hbm, kv_hbm, new_hbm, length_hbm, w_hbm, out_ref, w_ref, q_ref, kv, new_ref, lengths,
    flat, mixed_flat, sems, small_sems, w_sem,
):
    rows, cache, twice = kv.shape
    split_at = twice // 2
    kv_heads = split_at // HD
    heads = q_ref.shape[1] // HD
    group = heads // kv_heads
    small = [
        pltpu.make_async_copy(q_hbm, q_ref, small_sems.at[0]),
        pltpu.make_async_copy(new_hbm, new_ref, small_sems.at[1]),
        pltpu.make_async_copy(length_hbm, lengths, small_sems.at[2]),
    ]
    copies = [pltpu.make_async_copy(kv_hbm.at[r], kv.at[r], sems.at[r]) for r in range(rows)]
    for copy in small + copies:
        copy.start()
    w_copy = pltpu.make_async_copy(w_hbm, w_ref, w_sem)
    w_copy.start()
    for copy in small:
        copy.wait()
    for h in range(heads):
        flat[h * rows : (h + 1) * rows, :] = q_ref[:, h * HD : (h + 1) * HD].astype(jnp.float32)
    scaling = 1.0 / math.sqrt(HD)
    asked = [flat[pl.ds(r, heads, stride=rows), :] for r in range(rows)]
    place = lax.broadcasted_iota(jnp.int32, (heads, cache), 1)
    fresh = new_ref[...].astype(jnp.float32)

    def spread(r, start):
        pieces = [
            jnp.broadcast_to(
                fresh[r : r + 1, start + g * HD : start + (g + 1) * HD], (group, HD)
            )
            for g in range(kv_heads)
        ]
        return jnp.concatenate(pieces, axis=0)

    all_scores = []
    for r in range(rows):
        q = asked[r].astype(jnp.bfloat16)
        copies[r].wait()
        all_scores.append(
            jnp.concatenate(
                [
                    lax.dot_general(
                        q[g * group : (g + 1) * group],
                        kv[r, :, g * HD : (g + 1) * HD],
                        (((1,), (1,)), ((), ())),
                        preferred_element_type=jnp.float32,
                    )
                    for g in range(kv_heads)
                ],
                axis=0,
            )
        )
    probs, own_probs = [], []
    for r in range(rows):
        own = jnp.sum(asked[r] * spread(r, 0), axis=1, keepdims=True) * scaling
        scores = jnp.where(place < lengths[r], all_scores[r] * scaling, -jnp.inf)
        peak = jnp.maximum(jnp.max(scores, axis=1, keepdims=True), own)
        weights = jnp.exp(scores - peak)
        own_weight = jnp.exp(own - peak)
        denominator = jnp.sum(weights, axis=1, keepdims=True) + own_weight
        scale = 1.0 / denominator
        probs.append((weights * scale).astype(jnp.bfloat16))
        own_probs.append((own_weight * scale).astype(jnp.bfloat16).astype(jnp.float32))
    for r in range(rows):
        mixed = jnp.concatenate(
            [
                jnp.dot(
                    probs[r][g * group : (g + 1) * group],
                    kv[r, :, split_at + g * HD : split_at + (g + 1) * HD],
                    preferred_element_type=jnp.float32,
                )
                for g in range(kv_heads)
            ],
            axis=0,
        )
        mixed_flat[pl.ds(r, heads, stride=rows), :] = mixed + own_probs[r] * spread(r, split_at)
    for h in range(heads):
        out_ref[:, h * HD : (h + 1) * HD] = mixed_flat[h * rows : (h + 1) * rows, :].astype(
            jnp.bfloat16
        )
    w_copy.wait()


def attend(queries, kv_cache, new_kv, lengths, w_out):
    rows, features = queries.shape
    flat = pltpu.VMEM((rows * features // HD, HD), jnp.float32)
    return kernel_call(
        attend_kernel,
        "attend",
        (queries, kv_cache, new_kv, lengths, w_out),
        (pltpu.VMEM(queries.shape, queries.dtype), pltpu.VMEM(w_out.shape, w_out.dtype)),
        in_specs=[HBM] * 5,
        scratch=[
            pltpu.VMEM(queries.shape, queries.dtype),
            pltpu.VMEM(kv_cache.shape, kv_cache.dtype),
            pltpu.VMEM(new_kv.shape, new_kv.dtype),
            pltpu.SMEM(lengths.shape, lengths.dtype),
            flat,
            flat,
            pltpu.SemaphoreType.DMA((rows,)),
            pltpu.SemaphoreType.DMA((3,)),
            pltpu.SemaphoreType.DMA,
        ],
    )


def halves_of(first, second, upper):
    rows = first.shape[0]
    low = lax.broadcasted_iota(jnp.int32, first.shape, 0) < rows // 2
    return jnp.where(
        upper,
        jnp.where(low, pltpu.roll(first, rows // 2, 0), second),
        jnp.where(low, first, pltpu.roll(second, rows // 2, 0)),
    )


def project_kernel(block_ref, w_ref, residual_ref, kept_ref, sent_ref, total):
    side, rows, width = total.shape
    bits = side.bit_length() - 1
    mine = lax.axis_index("side")
    core = lax.rem(mine, 2)
    product = jnp.dot(block_ref[...], w_ref[...], preferred_element_type=jnp.float32)
    total[...] = product.reshape(total.shape)
    total[0] = total[0] + residual_ref[...].astype(jnp.float32)

    def of(member):
        apart = jnp.bitwise_xor(mine, member)
        q = 0
        for bit in range(bits):
            q = q + (jnp.bitwise_and(jnp.right_shift(apart, bit), 1) << (bits - 1 - bit))
        return total[q]

    for pair in range(side // 2):
        first, second = of(2 * pair), of(2 * pair + 1)
        at = slice(pair * rows, (pair + 1) * rows)
        kept_ref[at, :] = halves_of(first, second, core == 1)
        sent_ref[at, :] = halves_of(first, second, core == 0)


def project(attended, w_out, residual):
    side = lax.axis_size("side")
    bits = side.bit_length() - 1
    mine = lax.axis_index("side")
    rows, width = residual.shape
    block = attended
    for bit in reversed(range(bits)):
        half = block.shape[1] // 2
        own_bit = (mine >> bit) & 1
        kept = lax.dynamic_slice_in_dim(block, own_bit * half, half, 1)
        sent = lax.dynamic_slice_in_dim(block, (1 - own_bit) * half, half, 1)
        block = jnp.concatenate([kept, partner(sent, "side", 1 << bit)], axis=0)
    part = jax.ShapeDtypeStruct((side * rows // 2, width), jnp.float32)
    kept, sent = kernel_call(
        project_kernel,
        "project",
        (block, w_out, residual),
        (part, part),
        scratch=[pltpu.VMEM((side, rows, width), jnp.float32)],
    )
    total = kept + partner(sent, "side", 1)
    for bit in range(1, bits - 1):
        total = total + partner(total.astype(jnp.bfloat16), "side", 1 << bit).astype(jnp.float32)
    return total, partner(total.astype(jnp.bfloat16), "side", 1 << (bits - 1))


def norm_kernel(rows, total_ref, more_ref, gain_ref, normed_ref, own_ref, sent_ref):
    stream = total_ref[...] + more_ref[...].astype(jnp.float32)
    mean_square = jnp.mean(stream * stream, axis=1, keepdims=True)
    normed = stream * lax.rsqrt(mean_square + 1e-06) * gain_ref[...]
    normed_ref[...] = normed.astype(jnp.bfloat16)
    mine = lax.axis_index("side")
    core = lax.rem(mine, 2)
    pairs = stream.shape[0] // rows
    chip = lax.div(mine, 2)
    here = stream[:rows]
    for pair in range(1, pairs):
        here = jnp.where(chip == pair, stream[pair * rows : (pair + 1) * rows], here)
    upper = lax.broadcasted_iota(jnp.int32, here.shape, 0) >= rows // 2
    valid = upper == (core == 1)
    own_ref[...] = jnp.where(valid, here, 0.0).astype(jnp.bfloat16)
    sent_ref[...] = jnp.where(valid, pltpu.roll(here, rows // 2, 0), 0.0).astype(jnp.bfloat16)


def expert_kernel(
    rows, order, *refs
):
    out_ref = refs[-1]
    in_own, in_other, down_own, down_other = refs[-5:-1]
    tokens = jnp.concatenate([ref[...] for ref in refs[:-5]], axis=0)
    units = down_own.shape[0]
    half = out_ref.shape[2]
    side = lax.axis_size("side")
    dev = lax.axis_index("dev")
    hidden = []
    for w_ref in (in_own, in_other):
        gate_up = jnp.dot(tokens, w_ref[...], preferred_element_type=jnp.float32)
        gate = gate_up[:, :units]
        hidden.append((gate / (1.0 + jnp.exp(-gate)) * gate_up[:, units:]).astype(jnp.bfloat16))
    result = jnp.dot(hidden[0], down_own[...], preferred_element_type=jnp.float32) + jnp.dot(
        hidden[1], down_other[...], preferred_element_type=jnp.float32
    )
    low = lax.broadcasted_iota(jnp.int32, (rows, half), 0) < rows // 2
    pairs = side // 2
    for index, away in enumerate(order):
        base = jnp.bitwise_xor(dev, away) * side
        for pair in range(pairs):
            start = (index * pairs + pair) * rows
            left = result[start : start + rows, :half]
            right = result[start : start + rows, half:]
            out_ref[base + 2 * pair] = jnp.where(
                low, left, pltpu.roll(right, rows // 2, 0)
            ).astype(jnp.bfloat16)
            out_ref[base + 2 * pair + 1] = jnp.where(
                low, pltpu.roll(left, rows // 2, 0), right
            ).astype(jnp.bfloat16)


def mix_kernel(back_ref, mixing_ref, out_ref):
    experts2, rows, half = back_ref.shape
    mixing = mixing_ref[...]
    sums = []
    for core in range(2):
        total = jnp.zeros((rows, half), jnp.float32)
        for source in range(core, experts2, 2):
            total = total + back_ref[source].astype(jnp.float32) * mixing[:, source : source + 1]
        sums.append(total)
    low = lax.broadcasted_iota(jnp.int32, (rows, half), 0) < rows // 2
    out_ref[:, :half] = jnp.where(low, sums[0], pltpu.roll(sums[1], rows // 2, 0)).astype(
        jnp.bfloat16
    )
    out_ref[:, half:] = jnp.where(low, pltpu.roll(sums[0], rows // 2, 0), sums[1]).astype(
        jnp.bfloat16
    )


def body(
    queries,
    kv_cache,
    new_kv,
    lengths,
    residual,
    w_out,
    norm_gain,
    expert_ids,
    route_level,
    w_in,
    w_down,
):
    rows, width = residual.shape
    everyone = ("dev", "side")
    devs = lax.axis_size("dev")
    shards = devs * lax.axis_size("side")
    experts = shards // 2

    attended, w_out = attend(queries, kv_cache, new_kv, lengths, w_out)
    total, more = project(attended, w_out, residual)
    w_in, w_down, total = lax.optimization_barrier((w_in[0], w_down[0], total))
    in_other = partner(w_in, "side", 1)
    down_other = partner(w_down, "side", 1)
    like = jax.ShapeDtypeStruct(total.shape, jnp.bfloat16)
    eight = jax.ShapeDtypeStruct((rows, width), jnp.bfloat16)
    normed, own_stream, sent_stream = kernel_call(
        functools.partial(norm_kernel, rows),
        "norm",
        (total, more, norm_gain.reshape(1, width)),
        (like, eight, eight),
    )

    upper = range(2, devs, 2)
    near = [normed] + [partner(normed, "dev", away) for away in upper]
    far = partner(jnp.concatenate(near, axis=0), "dev", 1)
    stream = own_stream + partner(sent_stream, "side", 1)
    order = [0, *upper] + [1] + [away + 1 for away in upper]
    tokens = shards * rows // 2
    outbox = kernel_call(
        functools.partial(expert_kernel, rows, order),
        "experts",
        (*near, far, w_in, in_other, w_down, down_other),
        jax.ShapeDtypeStruct((shards, rows, width // 2), jnp.bfloat16),
    )
    returned = lax.all_to_all(outbox, everyone, split_axis=0, concat_axis=0, tiled=True)

    shares = route_level.astype(jnp.float32)
    shares = shares / jnp.sum(shares, axis=1, keepdims=True)
    chosen = expert_ids[:, :, None] == jnp.arange(experts, dtype=jnp.int32)[None, None, :]
    mixing = jnp.sum(jnp.where(chosen, shares[:, :, None], 0.0), axis=1)
    mixing = mixing.reshape(2, rows // 2, experts).transpose(1, 2, 0).reshape(rows // 2, shards)
    mixing = jnp.concatenate([mixing, mixing], axis=0)
    expert_sum = kernel_call(
        mix_kernel, "mix", (returned, mixing), jax.ShapeDtypeStruct((rows, width), jnp.bfloat16)
    )
    return (stream, expert_sum)


def solution(mesh):
    by_request = ("groups", "dev", "side")
    return jax.shard_map(
        body,
        mesh=mesh,
        in_specs=(
            P(by_request, None),
            P(by_request, None, None),
            P(by_request, None),
            P(by_request),
            P(by_request, None),
            P("side", None),
            P(),
            P(by_request, None),
            P(by_request, None),
            P(("dev", "side"), None, None),
            P(("dev", "side"), None, None),
        ),
        out_specs=(P(by_request, None), P(by_request, None)),
        check_vma=False,
    )
```

```python
import functools
import math

import jax
import jax.numpy as jnp
from jax import lax
from jax.experimental import pallas as pl
from jax.experimental.pallas import tpu as pltpu
from jax.sharding import PartitionSpec as P

HD = 128
GRANT = 16 << 20
VMEM = pl.BlockSpec(memory_space=pltpu.VMEM)
HBM = pl.BlockSpec(memory_space=pltpu.HBM)


def kernel_call(body, name, operands, outs, in_specs=None, scratch=(), cost=None):
    return pl.pallas_call(
        body,
        name=name,
        out_shape=outs,
        in_specs=in_specs or [VMEM] * len(operands),
        out_specs=jax.tree.map(lambda _: VMEM, outs, is_leaf=lambda x: hasattr(x, "shape")),
        scratch_shapes=list(scratch),
        compiler_params=pltpu.CompilerParams(vmem_limit_bytes=GRANT),
        cost_estimate=cost,
    )(*operands)


def in_hbm(*arrays):
    return [pltpu.with_memory_space_constraint(x, pltpu.HBM) for x in arrays]


def partner(block, axis, mask):
    count = lax.axis_size(axis)
    return lax.ppermute(block, axis, [(i, i ^ mask) for i in range(count)])


def start_all(copies):
    for copy in copies:
        copy.start()


def wait_all(copies):
    for copy in copies:
        copy.wait()


def half_copies(which, q_hbm, kv_hbm, new_hbm, q_ref, kv, new_ref, sems, kv_sems):
    rows, cache, span = kv.shape
    share = span // 2
    whole = kv_hbm.shape[2] // 2
    keys = pl.ds(pl.multiple_of(which * share, share), share)
    values = pl.ds(pl.multiple_of(whole + which * share, share), share)
    span_q = q_ref.shape[1]
    small = [
        pltpu.make_async_copy(
            q_hbm.at[:, pl.ds(pl.multiple_of(which * span_q, span_q), span_q)],
            q_ref,
            sems.at[0],
        ),
        pltpu.make_async_copy(new_hbm.at[:, keys], new_ref.at[:, :share], sems.at[1]),
        pltpu.make_async_copy(new_hbm.at[:, values], new_ref.at[:, share:], sems.at[2]),
    ]
    large = [
        (
            pltpu.make_async_copy(kv_hbm.at[r, :, keys], kv.at[r, :, :share], kv_sems.at[0, r]),
            pltpu.make_async_copy(kv_hbm.at[r, :, values], kv.at[r, :, share:], kv_sems.at[1, r]),
        )
        for r in range(rows)
    ]
    return small, large


def attend_heads(q_ref, kv, new_ref, lengths, flat, mixed_flat, key_wait, value_wait, length_wait):
    rows, cache, span = kv.shape
    share = span // 2
    kv_heads = share // HD
    heads = q_ref.shape[1] // HD
    group = heads // kv_heads
    for h in range(heads):
        flat[h * rows : (h + 1) * rows, :] = q_ref[:, h * HD : (h + 1) * HD].astype(jnp.float32)
    scaling = 1.0 / math.sqrt(HD)
    asked = [flat[pl.ds(r, heads, stride=rows), :] for r in range(rows)]
    place = lax.broadcasted_iota(jnp.int32, (heads, cache), 1)
    fresh = new_ref[...].astype(jnp.float32)

    def spread(r, start):
        pieces = [
            jnp.broadcast_to(
                fresh[r : r + 1, start + g * HD : start + (g + 1) * HD], (group, HD)
            )
            for g in range(kv_heads)
        ]
        return jnp.concatenate(pieces, axis=0)

    all_scores = []
    for r in range(rows):
        q = asked[r].astype(jnp.bfloat16)
        key_wait(r)
        all_scores.append(
            jnp.concatenate(
                [
                    lax.dot_general(
                        q[g * group : (g + 1) * group],
                        kv[r, :, g * HD : (g + 1) * HD],
                        (((1,), (1,)), ((), ())),
                        preferred_element_type=jnp.float32,
                    )
                    for g in range(kv_heads)
                ],
                axis=0,
            )
        )
    length_wait()
    probs, own_probs = [], []
    for r in range(rows):
        own = jnp.sum(asked[r] * spread(r, 0), axis=1, keepdims=True) * scaling
        scores = jnp.where(place < lengths[r], all_scores[r] * scaling, -jnp.inf)
        peak = jnp.maximum(jnp.max(scores, axis=1, keepdims=True), own)
        weights = jnp.exp(scores - peak)
        own_weight = jnp.exp(own - peak)
        denominator = jnp.sum(weights, axis=1, keepdims=True) + own_weight
        scale = 1.0 / denominator
        probs.append((weights * scale).astype(jnp.bfloat16))
        own_probs.append((own_weight * scale).astype(jnp.bfloat16).astype(jnp.float32))
    for r in range(rows):
        value_wait(r)
        mixed = jnp.concatenate(
            [
                jnp.dot(
                    probs[r][g * group : (g + 1) * group],
                    kv[r, :, share + g * HD : share + (g + 1) * HD],
                    preferred_element_type=jnp.float32,
                )
                for g in range(kv_heads)
            ],
            axis=0,
        )
        mixed_flat[pl.ds(r, heads, stride=rows), :] = mixed + own_probs[r] * spread(r, share)


def put_pieces(out_ref, mixed_flat):
    pieces, rows, columns = out_ref.shape
    heads = columns // HD
    low = lax.rem(lax.axis_index("side"), pieces)
    for d in range(pieces):
        first = jnp.bitwise_xor(low, d) * heads
        for h in range(heads):
            at = pl.multiple_of((first + h) * rows, rows)
            out_ref[d, :, h * HD : (h + 1) * HD] = mixed_flat[pl.ds(at, rows), :].astype(
                jnp.bfloat16
            )


def far_kernel(
    q_hbm, kv_hbm, new_hbm, length_hbm, out_ref, q_near, kv_near, new_near, q_ref, kv, new_ref,
    lengths, flat, mixed_flat, sems, kv_sems, near_sems, near_kv_sems, length_sem,
):
    here = lax.div(lax.axis_index("side"), lax.axis_size("side") // 2)
    length_copy = pltpu.make_async_copy(length_hbm, lengths, length_sem)
    small, large = half_copies(
        1 - here, q_hbm, kv_hbm, new_hbm, q_ref, kv, new_ref, sems, kv_sems
    )
    near_small, near_large = half_copies(
        here, q_hbm, kv_hbm, new_hbm, q_near, kv_near, new_near, near_sems, near_kv_sems
    )
    start_all(small)
    start_all([length_copy] + [pair[0] for pair in large])
    start_all([pair[1] for pair in large])
    start_all(near_small)
    for pair in near_large:
        start_all(pair)
    wait_all(small)
    attend_heads(
        q_ref, kv, new_ref, lengths, flat, mixed_flat,
        lambda r: large[r][0].wait(), lambda r: large[r][1].wait(), length_copy.wait,
    )
    put_pieces(out_ref, mixed_flat)
    wait_all(near_small)
    for pair in near_large:
        wait_all(pair)


def near_kernel(
    q_ref, kv, new_ref, length_hbm, w_hbm, out_ref, w_ref, lengths, flat, mixed_flat, length_sem,
    w_sem,
):
    length_copy = pltpu.make_async_copy(length_hbm, lengths, length_sem)
    w_copy = pltpu.make_async_copy(w_hbm, w_ref, w_sem)
    start_all([length_copy, w_copy])
    nothing = lambda r: None
    attend_heads(
        q_ref, kv, new_ref, lengths, flat, mixed_flat, nothing, nothing, length_copy.wait
    )
    put_pieces(out_ref, mixed_flat)
    w_copy.wait()


def attend(queries, kv_cache, new_kv, lengths, w_out):
    rows, features = queries.shape
    side = lax.axis_size("side")
    q_half = pltpu.VMEM((rows, features // 2), queries.dtype)
    kv_half = pltpu.VMEM((*kv_cache.shape[:2], kv_cache.shape[2] // 2), kv_cache.dtype)
    new_half = pltpu.VMEM((rows, new_kv.shape[1] // 2), new_kv.dtype)
    pieces = pltpu.VMEM((side // 2, rows, features // side), jnp.bfloat16)
    flat = pltpu.VMEM((rows * features // 2 // HD, HD), jnp.float32)
    smem = pltpu.SMEM(lengths.shape, lengths.dtype)
    dma = pltpu.SemaphoreType.DMA
    queries, kv_cache, new_kv, lengths, w_out = in_hbm(queries, kv_cache, new_kv, lengths, w_out)
    sent, q_near, kv_near, new_near = kernel_call(
        far_kernel,
        "attend_far",
        (queries, kv_cache, new_kv, lengths),
        (pieces, q_half, kv_half, new_half),
        in_specs=[HBM] * 4,
        scratch=[
            q_half, kv_half, new_half, smem, flat, flat,
            dma((3,)), dma((2, rows)), dma((3,)), dma((2, rows)), dma,
        ],
    )
    received = partner(sent, "side", side // 2)
    kept, w_near = kernel_call(
        near_kernel,
        "attend_near",
        (q_near, kv_near, new_near, lengths, w_out),
        (pieces, pltpu.VMEM(w_out.shape, w_out.dtype)),
        in_specs=[VMEM] * 3 + [HBM] * 2,
        scratch=[smem, flat, flat, dma, dma],
        cost=pl.CostEstimate(flops=8 << 20, bytes_accessed=8 << 20, transcendentals=0),
    )
    blocks = {0: kept, side // 2: received}
    bit = side // 4
    while bit:
        blocks.update({d ^ bit: partner(block, "side", bit) for d, block in blocks.items()})
        bit //= 2
    return [blocks[d] for d in range(side)], w_near


def halves_of(first, second, upper):
    rows = first.shape[0]
    low = lax.broadcasted_iota(jnp.int32, first.shape, 0) < rows // 2
    return jnp.where(
        upper,
        jnp.where(low, pltpu.roll(first, rows // 2, 0), second),
        jnp.where(low, first, pltpu.roll(second, rows // 2, 0)),
    )


def project_kernel(*refs):
    kept_ref, sent_ref, total = refs[-3:]
    w_ref, residual_ref = refs[-5:-3]
    blocks = refs[:-5]
    side, rows, width = total.shape
    mine = lax.axis_index("side")
    core = lax.rem(mine, 2)
    block = jnp.concatenate([ref[d % ref.shape[0]] for d, ref in enumerate(blocks)], axis=0)
    product = jnp.dot(block, w_ref[...], preferred_element_type=jnp.float32)
    total[...] = product.reshape(total.shape)
    total[0] = total[0] + residual_ref[...].astype(jnp.float32)
    for pair in range(side // 2):
        first = total[jnp.bitwise_xor(mine, 2 * pair)]
        second = total[jnp.bitwise_xor(mine, 2 * pair + 1)]
        at = slice(pair * rows, (pair + 1) * rows)
        kept_ref[at, :] = halves_of(first, second, core == 1)
        sent_ref[at, :] = halves_of(first, second, core == 0)


def project(blocks, w_out, residual):
    side = lax.axis_size("side")
    rows, width = residual.shape
    part = jax.ShapeDtypeStruct((side * rows // 2, width), jnp.float32)
    kept, sent = kernel_call(
        project_kernel,
        "project",
        (*blocks, w_out, residual),
        (part, part),
        scratch=[pltpu.VMEM((side, rows, width), jnp.float32)],
    )
    return kept + partner(sent, "side", 1)


def fetch_kernel(after_ref, in_hbm_ref, down_hbm_ref, in_ref, down_ref, sems):
    copies = [
        pltpu.make_async_copy(in_hbm_ref.at[0], in_ref, sems.at[0]),
        pltpu.make_async_copy(down_hbm_ref.at[0], down_ref, sems.at[1]),
    ]
    start_all(copies)
    wait_all(copies)


def fetch(after, w_in, w_down):
    return kernel_call(
        fetch_kernel,
        "fetch",
        (after, *in_hbm(w_in, w_down)),
        (pltpu.VMEM(w_in.shape[1:], w_in.dtype), pltpu.VMEM(w_down.shape[1:], w_down.dtype)),
        in_specs=[VMEM, HBM, HBM],
        scratch=[pltpu.SemaphoreType.DMA((2,))],
        cost=pl.CostEstimate(flops=0, bytes_accessed=8 << 20, transcendentals=0),
    )


def norm_kernel(rows, total_ref, more_ref, gain_ref, normed_ref, own_ref, sent_ref):
    stream = total_ref[...] + more_ref[...].astype(jnp.float32)
    mean_square = jnp.mean(stream * stream, axis=1, keepdims=True)
    normed = stream * lax.rsqrt(mean_square + 1e-06) * gain_ref[...]
    normed_ref[...] = normed.astype(jnp.bfloat16)
    mine = lax.axis_index("side")
    core = lax.rem(mine, 2)
    pairs = stream.shape[0] // rows
    chip = lax.div(mine, 2)
    here = stream[:rows]
    for pair in range(1, pairs):
        here = jnp.where(chip == pair, stream[pair * rows : (pair + 1) * rows], here)
    upper = lax.broadcasted_iota(jnp.int32, here.shape, 0) >= rows // 2
    valid = upper == (core == 1)
    own_ref[...] = jnp.where(valid, here, 0.0).astype(jnp.bfloat16)
    sent_ref[...] = jnp.where(valid, pltpu.roll(here, rows // 2, 0), 0.0).astype(jnp.bfloat16)


def expert_kernel(rows, order, *refs):
    out_ref = refs[-1]
    in_own, in_other, down_own, down_other = refs[-5:-1]
    tokens = jnp.concatenate([ref[...] for ref in refs[:-5]], axis=0)
    units = down_own.shape[0]
    half = out_ref.shape[2]
    side = lax.axis_size("side")
    dev = lax.axis_index("dev")
    hidden = []
    for w_ref in (in_own, in_other):
        gate_up = jnp.dot(tokens, w_ref[...], preferred_element_type=jnp.float32)
        gate = gate_up[:, :units]
        hidden.append((gate / (1.0 + jnp.exp(-gate)) * gate_up[:, units:]).astype(jnp.bfloat16))
    result = jnp.dot(hidden[0], down_own[...], preferred_element_type=jnp.float32) + jnp.dot(
        hidden[1], down_other[...], preferred_element_type=jnp.float32
    )
    low = lax.broadcasted_iota(jnp.int32, (rows, half), 0) < rows // 2
    pairs = side // 2
    for index, away in enumerate(order):
        base = jnp.bitwise_xor(dev, away) * side
        for pair in range(pairs):
            start = (index * pairs + pair) * rows
            left = result[start : start + rows, :half]
            right = result[start : start + rows, half:]
            out_ref[base + 2 * pair] = jnp.where(
                low, left, pltpu.roll(right, rows // 2, 0)
            ).astype(jnp.bfloat16)
            out_ref[base + 2 * pair + 1] = jnp.where(
                low, pltpu.roll(left, rows // 2, 0), right
            ).astype(jnp.bfloat16)


def mix_kernel(back_ref, mixing_ref, out_ref):
    experts2, rows, half = back_ref.shape
    mixing = mixing_ref[...]
    sums = []
    for core in range(2):
        total = jnp.zeros((rows, half), jnp.float32)
        for source in range(core, experts2, 2):
            total = total + back_ref[source].astype(jnp.float32) * mixing[:, source : source + 1]
        sums.append(total)
    low = lax.broadcasted_iota(jnp.int32, (rows, half), 0) < rows // 2
    out_ref[:, :half] = jnp.where(low, sums[0], pltpu.roll(sums[1], rows // 2, 0)).astype(
        jnp.bfloat16
    )
    out_ref[:, half:] = jnp.where(low, pltpu.roll(sums[0], rows // 2, 0), sums[1]).astype(
        jnp.bfloat16
    )


def body(
    queries,
    kv_cache,
    new_kv,
    lengths,
    residual,
    w_out,
    norm_gain,
    expert_ids,
    route_level,
    w_in,
    w_down,
):
    rows, width = residual.shape
    everyone = ("dev", "side")
    devs = lax.axis_size("dev")
    shards = devs * lax.axis_size("side")
    experts = shards // 2

    blocks, w_near = attend(queries, kv_cache, new_kv, lengths, w_out)
    total = project(blocks, w_near, residual)
    half_sum = total.astype(jnp.bfloat16)
    bit = 2
    while bit < lax.axis_size("side") // 2:
        total = total + partner(half_sum, "side", bit).astype(jnp.float32)
        half_sum = total.astype(jnp.bfloat16)
        bit *= 2
    more = partner(half_sum, "side", bit)
    w_in, w_down = fetch(half_sum, w_in, w_down)
    in_other = partner(w_in, "side", 1)
    down_other = partner(w_down, "side", 1)
    like = jax.ShapeDtypeStruct(total.shape, jnp.bfloat16)
    eight = jax.ShapeDtypeStruct((rows, width), jnp.bfloat16)
    normed, own_stream, sent_stream = kernel_call(
        functools.partial(norm_kernel, rows),
        "norm",
        (total, more, norm_gain.reshape(1, width)),
        (like, eight, eight),
    )

    upper = range(2, devs, 2)
    near = [normed] + [partner(normed, "dev", away) for away in upper]
    far = [partner(block, "dev", 1) for block in near]
    stream = own_stream + partner(sent_stream, "side", 1)
    order = [0, *upper] + [1] + [away + 1 for away in upper]
    outbox = kernel_call(
        functools.partial(expert_kernel, rows, order),
        "experts",
        (*near, *far, w_in, in_other, w_down, down_other),
        jax.ShapeDtypeStruct((shards, rows, width // 2), jnp.bfloat16),
    )
    returned = lax.all_to_all(outbox, everyone, split_axis=0, concat_axis=0, tiled=True)

    shares = route_level.astype(jnp.float32)
    shares = shares / jnp.sum(shares, axis=1, keepdims=True)
    chosen = expert_ids[:, :, None] == jnp.arange(experts, dtype=jnp.int32)[None, None, :]
    mixing = jnp.sum(jnp.where(chosen, shares[:, :, None], 0.0), axis=1)
    mixing = mixing.reshape(2, rows // 2, experts).transpose(1, 2, 0).reshape(rows // 2, shards)
    mixing = jnp.concatenate([mixing, mixing], axis=0)
    expert_sum = kernel_call(
        mix_kernel, "mix", (returned, mixing), jax.ShapeDtypeStruct((rows, width), jnp.bfloat16)
    )
    return (stream, expert_sum)


def solution(mesh):
    by_request = ("groups", "dev", "side")
    return jax.shard_map(
        body,
        mesh=mesh,
        in_specs=(
            P(by_request, None),
            P(by_request, None, None),
            P(by_request, None),
            P(by_request),
            P(by_request, None),
            P("side", None),
            P(),
            P(by_request, None),
            P(by_request, None),
            P(("dev", "side"), None, None),
            P(("dev", "side"), None, None),
        ),
        out_specs=(P(by_request, None), P(by_request, None)),
        check_vma=False,
    )
```

```python
import functools
import math

import jax
import jax.numpy as jnp
from jax import lax
from jax.experimental import pallas as pl
from jax.experimental.pallas import tpu as pltpu
from jax.sharding import PartitionSpec as P

HD = 128
GRANT = 16 << 20
VMEM = pl.BlockSpec(memory_space=pltpu.VMEM)
HBM = pl.BlockSpec(memory_space=pltpu.HBM)


def kernel_call(body, name, operands, outs, in_specs=None, scratch=(), cost=None):
    return pl.pallas_call(
        body,
        name=name,
        out_shape=outs,
        in_specs=in_specs or [VMEM] * len(operands),
        out_specs=jax.tree.map(lambda _: VMEM, outs, is_leaf=lambda x: hasattr(x, "shape")),
        scratch_shapes=list(scratch),
        compiler_params=pltpu.CompilerParams(vmem_limit_bytes=GRANT),
        cost_estimate=cost,
    )(*operands)


def in_hbm(*arrays):
    return [pltpu.with_memory_space_constraint(x, pltpu.HBM) for x in arrays]


def partner(block, axis, mask):
    count = lax.axis_size(axis)
    return lax.ppermute(block, axis, [(i, i ^ mask) for i in range(count)])


def start_all(copies):
    for copy in copies:
        copy.start()


def wait_all(copies):
    for copy in copies:
        copy.wait()


def half_copies(which, q_hbm, kv_hbm, new_hbm, q_ref, kv, new_ref, sems, kv_sems):
    rows, cache, span = kv.shape
    share = span // 2
    whole = kv_hbm.shape[2] // 2
    keys = pl.ds(pl.multiple_of(which * share, share), share)
    values = pl.ds(pl.multiple_of(whole + which * share, share), share)
    span_q = q_ref.shape[1]
    small = [
        pltpu.make_async_copy(
            q_hbm.at[:, pl.ds(pl.multiple_of(which * span_q, span_q), span_q)],
            q_ref,
            sems.at[0],
        ),
        pltpu.make_async_copy(new_hbm.at[:, keys], new_ref.at[:, :share], sems.at[1]),
        pltpu.make_async_copy(new_hbm.at[:, values], new_ref.at[:, share:], sems.at[2]),
    ]
    large = [
        (
            pltpu.make_async_copy(kv_hbm.at[r, :, keys], kv.at[r, :, :share], kv_sems.at[0, r]),
            pltpu.make_async_copy(kv_hbm.at[r, :, values], kv.at[r, :, share:], kv_sems.at[1, r]),
        )
        for r in range(rows)
    ]
    return small, large


def attend_heads(q_ref, kv, new_ref, lengths, flat, mixed_flat, key_wait, value_wait, length_wait):
    rows, cache, span = kv.shape
    share = span // 2
    kv_heads = share // HD
    heads = q_ref.shape[1] // HD
    group = heads // kv_heads
    for h in range(heads):
        flat[h * rows : (h + 1) * rows, :] = q_ref[:, h * HD : (h + 1) * HD].astype(jnp.float32)
    scaling = 1.0 / math.sqrt(HD)
    asked = [flat[pl.ds(r, heads, stride=rows), :] for r in range(rows)]
    place = lax.broadcasted_iota(jnp.int32, (heads, cache), 1)
    fresh = new_ref[...].astype(jnp.float32)

    def spread(r, start):
        pieces = [
            jnp.broadcast_to(
                fresh[r : r + 1, start + g * HD : start + (g + 1) * HD], (group, HD)
            )
            for g in range(kv_heads)
        ]
        return jnp.concatenate(pieces, axis=0)

    all_scores = []
    for r in range(rows):
        q = asked[r].astype(jnp.bfloat16)
        key_wait(r)
        all_scores.append(
            jnp.concatenate(
                [
                    lax.dot_general(
                        q[g * group : (g + 1) * group],
                        kv[r, :, g * HD : (g + 1) * HD],
                        (((1,), (1,)), ((), ())),
                        preferred_element_type=jnp.float32,
                    )
                    for g in range(kv_heads)
                ],
                axis=0,
            )
        )
    length_wait()
    probs, own_probs = [], []
    for r in range(rows):
        own = jnp.sum(asked[r] * spread(r, 0), axis=1, keepdims=True) * scaling
        scores = jnp.where(place < lengths[r], all_scores[r] * scaling, -jnp.inf)
        peak = jnp.maximum(jnp.max(scores, axis=1, keepdims=True), own)
        weights = jnp.exp(scores - peak)
        own_weight = jnp.exp(own - peak)
        denominator = jnp.sum(weights, axis=1, keepdims=True) + own_weight
        scale = 1.0 / denominator
        probs.append((weights * scale).astype(jnp.bfloat16))
        own_probs.append((own_weight * scale).astype(jnp.bfloat16).astype(jnp.float32))
    for r in range(rows):
        value_wait(r)
        mixed = jnp.concatenate(
            [
                jnp.dot(
                    probs[r][g * group : (g + 1) * group],
                    kv[r, :, share + g * HD : share + (g + 1) * HD],
                    preferred_element_type=jnp.float32,
                )
                for g in range(kv_heads)
            ],
            axis=0,
        )
        mixed_flat[pl.ds(r, heads, stride=rows), :] = mixed + own_probs[r] * spread(r, share)


def put_pieces(out_ref, mixed_flat):
    pieces, rows, columns = out_ref.shape
    heads = columns // HD // 2
    mine = lax.axis_index("side")
    core = lax.rem(mine, 2)
    low = lax.rem(lax.div(mine, 2), pieces)
    for d in range(pieces):
        chip = jnp.bitwise_xor(low, d)
        for other in range(2):
            first = (2 * chip + jnp.bitwise_xor(core, other)) * heads
            for h in range(heads):
                at = pl.multiple_of((first + h) * rows, rows)
                to = (other * heads + h) * HD
                out_ref[d, :, to : to + HD] = mixed_flat[pl.ds(at, rows), :].astype(jnp.bfloat16)


def far_kernel(
    q_hbm, kv_hbm, new_hbm, length_hbm, out_ref, q_near, kv_near, new_near, q_ref, kv, new_ref,
    lengths, flat, mixed_flat, sems, kv_sems, near_sems, near_kv_sems, length_sem,
):
    here = lax.div(lax.axis_index("side"), lax.axis_size("side") // 2)
    length_copy = pltpu.make_async_copy(length_hbm, lengths, length_sem)
    small, large = half_copies(
        1 - here, q_hbm, kv_hbm, new_hbm, q_ref, kv, new_ref, sems, kv_sems
    )
    near_small, near_large = half_copies(
        here, q_hbm, kv_hbm, new_hbm, q_near, kv_near, new_near, near_sems, near_kv_sems
    )
    start_all(small)
    start_all([length_copy] + [pair[0] for pair in large])
    start_all([pair[1] for pair in large])
    start_all(near_small)
    for pair in near_large:
        start_all(pair)
    wait_all(small)
    attend_heads(
        q_ref, kv, new_ref, lengths, flat, mixed_flat,
        lambda r: large[r][0].wait(), lambda r: large[r][1].wait(), length_copy.wait,
    )
    put_pieces(out_ref, mixed_flat)
    wait_all(near_small)
    for pair in near_large:
        wait_all(pair)


def near_kernel(
    q_ref, kv, new_ref, length_hbm, w_hbm, out_ref, w_ref, lengths, flat, mixed_flat, length_sem,
    w_sem,
):
    length_copy = pltpu.make_async_copy(length_hbm, lengths, length_sem)
    w_copy = pltpu.make_async_copy(w_hbm, w_ref, w_sem)
    start_all([length_copy, w_copy])
    nothing = lambda r: None
    attend_heads(
        q_ref, kv, new_ref, lengths, flat, mixed_flat, nothing, nothing, length_copy.wait
    )
    put_pieces(out_ref, mixed_flat)
    w_copy.wait()


def attend(queries, kv_cache, new_kv, lengths, w_out):
    rows, features = queries.shape
    chips = lax.axis_size("side") // 2
    q_half = pltpu.VMEM((rows, features // 2), queries.dtype)
    kv_half = pltpu.VMEM((*kv_cache.shape[:2], kv_cache.shape[2] // 2), kv_cache.dtype)
    new_half = pltpu.VMEM((rows, new_kv.shape[1] // 2), new_kv.dtype)
    pieces = pltpu.VMEM((chips // 2, rows, features // chips), jnp.bfloat16)
    flat = pltpu.VMEM((rows * features // 2 // HD, HD), jnp.float32)
    smem = pltpu.SMEM(lengths.shape, lengths.dtype)
    dma = pltpu.SemaphoreType.DMA
    queries, kv_cache, new_kv, lengths, w_out = in_hbm(queries, kv_cache, new_kv, lengths, w_out)
    sent, q_near, kv_near, new_near = kernel_call(
        far_kernel,
        "attend_far",
        (queries, kv_cache, new_kv, lengths),
        (pieces, q_half, kv_half, new_half),
        in_specs=[HBM] * 4,
        scratch=[
            q_half, kv_half, new_half, smem, flat, flat,
            dma((3,)), dma((2, rows)), dma((3,)), dma((2, rows)), dma,
        ],
    )
    received = partner(sent, "side", chips)
    kept, w_near = kernel_call(
        near_kernel,
        "attend_near",
        (q_near, kv_near, new_near, lengths, w_out),
        (pieces, pltpu.VMEM(w_out.shape, w_out.dtype)),
        in_specs=[VMEM] * 3 + [HBM] * 2,
        scratch=[smem, flat, flat, dma, dma],
        cost=pl.CostEstimate(flops=8 << 20, bytes_accessed=8 << 20, transcendentals=0),
    )
    blocks = {0: kept, chips // 2: received}
    bit = chips // 4
    while bit:
        blocks.update({d ^ bit: partner(block, "side", 2 * bit) for d, block in blocks.items()})
        bit //= 2
    return [blocks[d] for d in range(chips)], w_near


def project_kernel(*refs):
    kept_ref, sent_ref = refs[-2:]
    w_near, w_other, residual_ref, ids_ref, level_ref = refs[-7:-2]
    blocks = refs[:-7]
    rows, width = residual_ref.shape
    depth = w_near.shape[0]
    experts = lax.axis_size("dev") * lax.axis_size("side") // 2
    lhs = jnp.concatenate([ref[d % ref.shape[0]] for d, ref in enumerate(blocks)], axis=0)
    product = jnp.dot(lhs[:, :depth], w_near[...], preferred_element_type=jnp.float32) + jnp.dot(
        lhs[:, depth:], w_other[...], preferred_element_type=jnp.float32
    )
    level = level_ref[...].astype(jnp.float32)
    share = level / jnp.sum(level, axis=1, keepdims=True)
    spare = kept_ref.shape[1] - width
    lane = lax.broadcasted_iota(jnp.int32, (rows, spare), 1)
    ids = ids_ref[...]
    high, low = jnp.zeros((2, rows, spare), jnp.float32)
    for k in range(ids.shape[1]):
        chosen, part = ids[:, k : k + 1], share[:, k : k + 1]
        top = part.astype(jnp.bfloat16).astype(jnp.float32)
        high = high + jnp.where(lane == chosen, top, 0.0)
        low = low + jnp.where(lane == chosen + experts, part - top, 0.0)
    count = len(blocks)
    for d in range(count):
        here = product[d * rows : (d + 1) * rows]
        aside = jnp.zeros((rows, spare), jnp.float32)
        if d == 0:
            here = here + residual_ref[...].astype(jnp.float32)
            aside = high + low
        at = slice(d * rows, (d + 1) * rows)
        kept_ref[at, :width] = here
        kept_ref[at, width:] = aside
        at = slice((d ^ 1) * rows, ((d ^ 1) + 1) * rows)
        sent_ref[at, :width] = here.astype(jnp.bfloat16)
        sent_ref[at, width:] = aside.astype(jnp.bfloat16)


def project(blocks, w_near, w_other, residual, expert_ids, route_level):
    rows, width = residual.shape
    chips = len(blocks)
    experts = lax.axis_size("dev") * chips
    shape = (chips * rows, width + pl.cdiv(2 * experts, 128) * 128)
    kept, sent = kernel_call(
        project_kernel,
        "project",
        (
            *blocks,
            w_near,
            pltpu.with_memory_space_constraint(w_other, pltpu.VMEM),
            residual,
            expert_ids,
            route_level,
        ),
        (jax.ShapeDtypeStruct(shape, jnp.float32), jax.ShapeDtypeStruct(shape, jnp.bfloat16)),
    )
    bit = 1
    more = partner(sent, "side", 2 * bit)
    while 2 * bit < chips:
        kept = kept + more.astype(jnp.float32)
        bit *= 2
        swapped = [kept[(d ^ bit) * rows : ((d ^ bit) + 1) * rows] for d in range(chips)]
        more = partner(jnp.concatenate(swapped).astype(jnp.bfloat16), "side", 2 * bit)
    return kept, sent, more


def fetch_kernel(after_ref, in_hbm_ref, down_hbm_ref, in_ref, down_ref, sems):
    copies = [
        pltpu.make_async_copy(in_hbm_ref.at[0], in_ref, sems.at[0]),
        pltpu.make_async_copy(down_hbm_ref.at[0], down_ref, sems.at[1]),
    ]
    start_all(copies)
    wait_all(copies)


def fetch(after, w_in, w_down):
    return kernel_call(
        fetch_kernel,
        "fetch",
        (after, *in_hbm(w_in, w_down)),
        (pltpu.VMEM(w_in.shape[1:], w_in.dtype), pltpu.VMEM(w_down.shape[1:], w_down.dtype)),
        in_specs=[VMEM, HBM, HBM],
        scratch=[pltpu.SemaphoreType.DMA((2,))],
        cost=pl.CostEstimate(flops=0, bytes_accessed=8 << 20, transcendentals=0),
    )


def norm_kernel(total_ref, more_ref, gain_ref, normed_ref, stream_ref):
    rows, width = stream_ref.shape
    stream = total_ref[:, :width] + more_ref[:, :width].astype(jnp.float32)
    mean_square = jnp.mean(stream * stream, axis=1, keepdims=True)
    normed = stream * lax.rsqrt(mean_square + 1e-06) * gain_ref[...]
    normed_ref[:, :width] = normed.astype(jnp.bfloat16)
    aside = total_ref[:, width:] + more_ref[:, width:].astype(jnp.float32)
    normed_ref[:, width:] = aside.astype(jnp.bfloat16)
    stream_ref[...] = stream[:rows].astype(jnp.bfloat16)


def expert_kernel(rows, *refs):
    kept_ref, sent_ref = refs[-2:]
    in_own, in_other, down_own, down_other = refs[-6:-2]
    blocks = refs[:-6]
    width = kept_ref.shape[1]
    units = down_own.shape[0]
    chips = lax.axis_size("side") // 2
    experts = lax.axis_size("dev") * chips
    mine = lax.axis_index("dev") * chips + lax.div(lax.axis_index("side"), 2)
    tokens = jnp.concatenate([ref[:, :width] for ref in blocks], axis=0)
    aside = jnp.concatenate([ref[:, width:] for ref in blocks], axis=0).astype(jnp.float32)
    lane = lax.broadcasted_iota(jnp.int32, aside.shape, 1)
    picked = jnp.where((lane == mine) | (lane == mine + experts), aside, 0.0)
    share = jnp.sum(picked, axis=1, keepdims=True)
    hidden = []
    for w_ref in (in_own, in_other):
        gate_up = jnp.dot(tokens, w_ref[...], preferred_element_type=jnp.float32)
        gate = gate_up[:, :units]
        hidden.append((gate / (1.0 + jnp.exp(-gate)) * gate_up[:, units:]).astype(jnp.bfloat16))
    result = jnp.dot(hidden[0], down_own[...], preferred_element_type=jnp.float32) + jnp.dot(
        hidden[1], down_other[...], preferred_element_type=jnp.float32
    )
    result = result * share
    count = len(blocks)
    for d in range(chips):
        for i in range(count):
            start = (i * chips + d) * rows
            piece = result[start : start + rows]
            to = ((d % (chips // 2)) * count + i) * rows
            if d < chips // 2:
                kept_ref[to : to + rows, :] = piece
            else:
                sent_ref[to : to + rows, :] = piece.astype(jnp.bfloat16)


def run_experts(name, blocks, weights, rows, width):
    shape = (sum(block.shape[0] for block in blocks) // 2, width)
    return kernel_call(
        functools.partial(expert_kernel, rows),
        name,
        (*blocks, *weights),
        (jax.ShapeDtypeStruct(shape, jnp.float32), jax.ShapeDtypeStruct(shape, jnp.bfloat16)),
        cost=pl.CostEstimate(flops=1 << 30, bytes_accessed=4 << 20, transcendentals=0),
    )


def halve(total, sent, axis, mask):
    return total + partner(sent, axis, mask).astype(jnp.float32)


def homeward(kept, sent):
    bit = lax.axis_size("side") // 4
    total = halve(kept, sent, "side", 2 * bit)
    while bit > 1:
        bit //= 2
        half = total.shape[0] // 2
        total = halve(total[:half], total[half:].astype(jnp.bfloat16), "side", 2 * bit)
    half = total.shape[0] // 2
    return halve(total[:half], total[half:].astype(jnp.bfloat16), "dev", 1)


def body(
    queries,
    kv_cache,
    new_kv,
    lengths,
    residual,
    w_out,
    norm_gain,
    expert_ids,
    route_level,
    w_in,
    w_down,
):
    rows, width = residual.shape
    devs = lax.axis_size("dev")

    w_other = partner(w_out, "side", 1)
    blocks, w_near = attend(queries, kv_cache, new_kv, lengths, w_out)
    total, sent, more = project(blocks, w_near, w_other, residual, expert_ids, route_level)
    w_in, w_down = fetch(sent, w_in, w_down)
    w_in, w_down, more = lax.optimization_barrier((w_in, w_down, more))
    weights = (w_in, partner(w_in, "side", 1), w_down, partner(w_down, "side", 1))
    normed, stream = kernel_call(
        norm_kernel,
        "norm",
        (total, more, norm_gain.reshape(1, width)),
        (
            jax.ShapeDtypeStruct(total.shape, jnp.bfloat16),
            jax.ShapeDtypeStruct((rows, width), jnp.bfloat16),
        ),
    )

    upper = list(range(0, devs, 2))
    near = [normed] + [partner(normed, "dev", away) for away in upper[1:]]
    far = [partner(block, "dev", 1) for block in near]
    middle = len(upper) // 2
    home = []
    for name, group in (("early", slice(0, middle)), ("late", slice(middle, None))):
        kept, sent = run_experts(
            f"experts_{name}", near[group] + far[group], weights, rows, width
        )
        back = homeward(kept, sent)
        for index, away in enumerate(upper[group]):
            block = back[index * rows : (index + 1) * rows]
            if away:
                block = partner(block.astype(jnp.bfloat16), "dev", away).astype(jnp.float32)
            home.append(block)
    expert_sum = functools.reduce(jnp.add, home)
    return (stream, expert_sum.astype(jnp.bfloat16))


def solution(mesh):
    by_request = ("groups", "dev", "side")
    return jax.shard_map(
        body,
        mesh=mesh,
        in_specs=(
            P(by_request, None),
            P(by_request, None, None),
            P(by_request, None),
            P(by_request),
            P(by_request, None),
            P("side", None),
            P(),
            P(by_request, None),
            P(by_request, None),
            P(("dev", "side"), None, None),
            P(("dev", "side"), None, None),
        ),
        out_specs=(P(by_request, None), P(by_request, None)),
        check_vma=False,
    )
```

```python
import functools
import math

import jax
import jax.numpy as jnp
from jax import lax
from jax.experimental import pallas as pl
from jax.experimental.pallas import tpu as pltpu
from jax.sharding import PartitionSpec as P

HD = 128
GRANT = 16 << 20
VMEM = pl.BlockSpec(memory_space=pltpu.VMEM)
HBM = pl.BlockSpec(memory_space=pltpu.HBM)


def kernel_call(body, operands, outs, in_specs=None, scratch=(), cost=None):
    return pl.pallas_call(
        body,
        out_shape=outs,
        in_specs=in_specs or [VMEM] * len(operands),
        out_specs=jax.tree.map(lambda _: VMEM, outs, is_leaf=lambda x: hasattr(x, "shape")),
        scratch_shapes=list(scratch),
        compiler_params=pltpu.CompilerParams(vmem_limit_bytes=GRANT),
        cost_estimate=cost,
    )(*operands)


def in_hbm(*arrays):
    return [pltpu.with_memory_space_constraint(x, pltpu.HBM) for x in arrays]


def partner(block, axis, mask):
    count = lax.axis_size(axis)
    return lax.ppermute(block, axis, [(i, i ^ mask) for i in range(count)])


def start_all(copies):
    for copy in copies:
        copy.start()


def wait_all(copies):
    for copy in copies:
        copy.wait()


def half_copies(which, q_hbm, kv_hbm, new_hbm, q_ref, kv, new_ref, sems, kv_sems):
    rows, _, span = kv.shape
    share = span // 2
    whole = kv_hbm.shape[2] // 2
    keys = pl.ds(pl.multiple_of(which * share, share), share)
    values = pl.ds(pl.multiple_of(whole + which * share, share), share)
    span_q = q_ref.shape[1]
    small = [
        pltpu.make_async_copy(
            q_hbm.at[:, pl.ds(pl.multiple_of(which * span_q, span_q), span_q)],
            q_ref,
            sems.at[0],
        ),
        pltpu.make_async_copy(new_hbm.at[:, keys], new_ref.at[:, :share], sems.at[1]),
        pltpu.make_async_copy(new_hbm.at[:, values], new_ref.at[:, share:], sems.at[2]),
    ]
    large = [
        (
            pltpu.make_async_copy(kv_hbm.at[r, :, keys], kv.at[r, :, :share], kv_sems.at[0, r]),
            pltpu.make_async_copy(kv_hbm.at[r, :, values], kv.at[r, :, share:], kv_sems.at[1, r]),
        )
        for r in range(rows)
    ]
    return small, large


def attend_heads(q_ref, kv, new_ref, lengths, flat, mixed_flat, key_wait, value_wait, length_wait):
    rows, cache, span = kv.shape
    share = span // 2
    kv_heads = share // HD
    heads = q_ref.shape[1] // HD
    group = heads // kv_heads
    for h in range(heads):
        flat[h * rows : (h + 1) * rows, :] = q_ref[:, h * HD : (h + 1) * HD].astype(jnp.float32)
    scaling = 1.0 / math.sqrt(HD)
    asked = [flat[pl.ds(r, heads, stride=rows), :] for r in range(rows)]
    place = lax.broadcasted_iota(jnp.int32, (heads, cache), 1)
    fresh = new_ref[...].astype(jnp.float32)

    def spread(r, start):
        pieces = [
            jnp.broadcast_to(
                fresh[r : r + 1, start + g * HD : start + (g + 1) * HD], (group, HD)
            )
            for g in range(kv_heads)
        ]
        return jnp.concatenate(pieces, axis=0)

    all_scores = []
    for r in range(rows):
        q = asked[r].astype(jnp.bfloat16)
        key_wait(r)
        all_scores.append(
            jnp.concatenate(
                [
                    lax.dot_general(
                        q[g * group : (g + 1) * group],
                        kv[r, :, g * HD : (g + 1) * HD],
                        (((1,), (1,)), ((), ())),
                        preferred_element_type=jnp.float32,
                    )
                    for g in range(kv_heads)
                ],
                axis=0,
            )
        )
    length_wait()
    probs, own_probs = [], []
    for r in range(rows):
        own = jnp.sum(asked[r] * spread(r, 0), axis=1, keepdims=True) * scaling
        scores = jnp.where(place < lengths[r], all_scores[r] * scaling, -jnp.inf)
        peak = jnp.maximum(jnp.max(scores, axis=1, keepdims=True), own)
        weights = jnp.exp(scores - peak)
        own_weight = jnp.exp(own - peak)
        denominator = jnp.sum(weights, axis=1, keepdims=True) + own_weight
        scale = 1.0 / denominator
        probs.append((weights * scale).astype(jnp.bfloat16))
        own_probs.append((own_weight * scale).astype(jnp.bfloat16).astype(jnp.float32))
    for r in range(rows):
        value_wait(r)
        mixed = jnp.concatenate(
            [
                jnp.dot(
                    probs[r][g * group : (g + 1) * group],
                    kv[r, :, share + g * HD : share + (g + 1) * HD],
                    preferred_element_type=jnp.float32,
                )
                for g in range(kv_heads)
            ],
            axis=0,
        )
        mixed_flat[pl.ds(r, heads, stride=rows), :] = mixed + own_probs[r] * spread(r, share)


def put_pieces(out_ref, mixed_flat):
    pieces, rows, columns = out_ref.shape
    heads = columns // HD // 2
    mine = lax.axis_index("side")
    core = lax.rem(mine, 2)
    low = lax.rem(lax.div(mine, 2), pieces)
    for d in range(pieces):
        chip = jnp.bitwise_xor(low, d)
        for other in range(2):
            first = (2 * chip + jnp.bitwise_xor(core, other)) * heads
            for h in range(heads):
                at = pl.multiple_of((first + h) * rows, rows)
                to = (other * heads + h) * HD
                out_ref[d, :, to : to + HD] = mixed_flat[pl.ds(at, rows), :].astype(jnp.bfloat16)


def far_kernel(
    q_hbm, kv_hbm, new_hbm, length_hbm, out_ref, q_near, kv_near, new_near, q_ref, kv, new_ref,
    lengths, flat, mixed_flat, sems, kv_sems, near_sems, near_kv_sems, length_sem,
):
    here = lax.div(lax.axis_index("side"), lax.axis_size("side") // 2)
    length_copy = pltpu.make_async_copy(length_hbm, lengths, length_sem)
    small, large = half_copies(
        1 - here, q_hbm, kv_hbm, new_hbm, q_ref, kv, new_ref, sems, kv_sems
    )
    near_small, near_large = half_copies(
        here, q_hbm, kv_hbm, new_hbm, q_near, kv_near, new_near, near_sems, near_kv_sems
    )
    start_all(small)
    start_all([length_copy] + [pair[0] for pair in large])
    start_all([pair[1] for pair in large])
    start_all(near_small)
    for pair in near_large:
        start_all(pair)
    wait_all(small)
    attend_heads(
        q_ref, kv, new_ref, lengths, flat, mixed_flat,
        lambda r: large[r][0].wait(), lambda r: large[r][1].wait(), length_copy.wait,
    )
    put_pieces(out_ref, mixed_flat)
    wait_all(near_small)
    for pair in near_large:
        wait_all(pair)


def near_kernel(
    q_ref, kv, new_ref, length_hbm, w_hbm, out_ref, w_ref, lengths, flat, mixed_flat, length_sem,
    w_sem,
):
    length_copy = pltpu.make_async_copy(length_hbm, lengths, length_sem)
    w_copy = pltpu.make_async_copy(w_hbm, w_ref, w_sem)
    start_all([length_copy, w_copy])
    nothing = lambda r: None
    attend_heads(
        q_ref, kv, new_ref, lengths, flat, mixed_flat, nothing, nothing, length_copy.wait
    )
    put_pieces(out_ref, mixed_flat)
    w_copy.wait()


def attend(queries, kv_cache, new_kv, lengths, w_out):
    rows, features = queries.shape
    chips = lax.axis_size("side") // 2
    q_half = pltpu.VMEM((rows, features // 2), queries.dtype)
    kv_half = pltpu.VMEM((*kv_cache.shape[:2], kv_cache.shape[2] // 2), kv_cache.dtype)
    new_half = pltpu.VMEM((rows, new_kv.shape[1] // 2), new_kv.dtype)
    pieces = pltpu.VMEM((chips // 2, rows, features // chips), jnp.bfloat16)
    flat = pltpu.VMEM((rows * features // 2 // HD, HD), jnp.float32)
    smem = pltpu.SMEM(lengths.shape, lengths.dtype)
    dma = pltpu.SemaphoreType.DMA
    queries, kv_cache, new_kv, lengths, w_out = in_hbm(queries, kv_cache, new_kv, lengths, w_out)
    sent, q_near, kv_near, new_near = kernel_call(
        far_kernel,
        (queries, kv_cache, new_kv, lengths),
        (pieces, q_half, kv_half, new_half),
        in_specs=[HBM] * 4,
        scratch=[
            q_half, kv_half, new_half, smem, flat, flat,
            dma((3,)), dma((2, rows)), dma((3,)), dma((2, rows)), dma,
        ],
    )
    received = partner(sent, "side", chips)
    kept, w_near = kernel_call(
        near_kernel,
        (q_near, kv_near, new_near, lengths, w_out),
        (pieces, pltpu.VMEM(w_out.shape, w_out.dtype)),
        in_specs=[VMEM] * 3 + [HBM] * 2,
        scratch=[smem, flat, flat, dma, dma],
        cost=pl.CostEstimate(flops=8 << 20, bytes_accessed=8 << 20, transcendentals=0),
    )
    blocks = {0: kept, chips // 2: received}
    bit = chips // 4
    while bit:
        blocks.update({d ^ bit: partner(block, "side", 2 * bit) for d, block in blocks.items()})
        bit //= 2
    return [blocks[d] for d in range(chips)], w_near


def project_kernel(*refs):
    kept_ref, sent_ref = refs[-2:]
    w_near, w_other, residual_ref, ids_ref, level_ref = refs[-7:-2]
    blocks = refs[:-7]
    rows, width = residual_ref.shape
    depth = w_near.shape[0]
    experts = lax.axis_size("dev") * lax.axis_size("side") // 2
    lhs = jnp.concatenate([ref[d % ref.shape[0]] for d, ref in enumerate(blocks)], axis=0)
    product = jnp.dot(lhs[:, :depth], w_near[...], preferred_element_type=jnp.float32) + jnp.dot(
        lhs[:, depth:], w_other[...], preferred_element_type=jnp.float32
    )
    level = level_ref[...].astype(jnp.float32)
    share = level / jnp.sum(level, axis=1, keepdims=True)
    spare = kept_ref.shape[1] - width
    lane = lax.broadcasted_iota(jnp.int32, (rows, spare), 1)
    ids = ids_ref[...]
    high, low = jnp.zeros((2, rows, spare), jnp.float32)
    for k in range(ids.shape[1]):
        chosen, part = ids[:, k : k + 1], share[:, k : k + 1]
        top = part.astype(jnp.bfloat16).astype(jnp.float32)
        high = high + jnp.where(lane == chosen, top, 0.0)
        low = low + jnp.where(lane == chosen + experts, part - top, 0.0)
    count = len(blocks)
    for d in range(count):
        here = product[d * rows : (d + 1) * rows]
        aside = jnp.zeros((rows, spare), jnp.float32)
        if d == 0:
            here = here + residual_ref[...].astype(jnp.float32)
            aside = high + low
        at = slice(d * rows, (d + 1) * rows)
        kept_ref[at, :width] = here
        kept_ref[at, width:] = aside
        at = slice((d ^ 1) * rows, ((d ^ 1) + 1) * rows)
        sent_ref[at, :width] = here.astype(jnp.bfloat16)
        sent_ref[at, width:] = aside.astype(jnp.bfloat16)


def project(blocks, w_near, w_other, residual, expert_ids, route_level):
    rows, width = residual.shape
    chips = len(blocks)
    experts = lax.axis_size("dev") * chips
    shape = (chips * rows, width + pl.cdiv(2 * experts, 128) * 128)
    kept, sent = kernel_call(
        project_kernel,
        (
            *blocks,
            w_near,
            pltpu.with_memory_space_constraint(w_other, pltpu.VMEM),
            residual,
            expert_ids,
            route_level,
        ),
        (jax.ShapeDtypeStruct(shape, jnp.float32), jax.ShapeDtypeStruct(shape, jnp.bfloat16)),
    )
    bit = 1
    more = partner(sent, "side", 2 * bit)
    while 2 * bit < chips:
        kept = kept + more.astype(jnp.float32)
        bit *= 2
        swapped = [kept[(d ^ bit) * rows : ((d ^ bit) + 1) * rows] for d in range(chips)]
        more = partner(jnp.concatenate(swapped).astype(jnp.bfloat16), "side", 2 * bit)
    return kept, sent, more


def fetch_kernel(after_ref, in_hbm_ref, down_hbm_ref, in_ref, down_ref, sems):
    copies = [
        pltpu.make_async_copy(in_hbm_ref.at[0], in_ref, sems.at[0]),
        pltpu.make_async_copy(down_hbm_ref.at[0], down_ref, sems.at[1]),
    ]
    start_all(copies)
    wait_all(copies)


def fetch(after, w_in, w_down):
    return kernel_call(
        fetch_kernel,
        (after, *in_hbm(w_in, w_down)),
        (pltpu.VMEM(w_in.shape[1:], w_in.dtype), pltpu.VMEM(w_down.shape[1:], w_down.dtype)),
        in_specs=[VMEM, HBM, HBM],
        scratch=[pltpu.SemaphoreType.DMA((2,))],
        cost=pl.CostEstimate(flops=0, bytes_accessed=8 << 20, transcendentals=0),
    )


def norm_kernel(total_ref, more_ref, gain_ref, normed_ref, stream_ref):
    rows, width = stream_ref.shape
    stream = total_ref[:, :width] + more_ref[:, :width].astype(jnp.float32)
    mean_square = jnp.mean(stream * stream, axis=1, keepdims=True)
    normed = stream * lax.rsqrt(mean_square + 1e-06) * gain_ref[...]
    normed_ref[:, :width] = normed.astype(jnp.bfloat16)
    aside = total_ref[:, width:] + more_ref[:, width:].astype(jnp.float32)
    normed_ref[:, width:] = aside.astype(jnp.bfloat16)
    stream_ref[...] = stream[:rows].astype(jnp.bfloat16)


def expert_kernel(rows, *refs):
    kept_ref, sent_ref = refs[-2:]
    in_own, in_other, down_own, down_other = refs[-6:-2]
    blocks = refs[:-6]
    width = kept_ref.shape[1]
    units = down_own.shape[0]
    chips = lax.axis_size("side") // 2
    experts = lax.axis_size("dev") * chips
    mine = lax.axis_index("dev") * chips + lax.div(lax.axis_index("side"), 2)
    tokens = jnp.concatenate([ref[:, :width] for ref in blocks], axis=0)
    aside = jnp.concatenate([ref[:, width:] for ref in blocks], axis=0).astype(jnp.float32)
    lane = lax.broadcasted_iota(jnp.int32, aside.shape, 1)
    picked = jnp.where((lane == mine) | (lane == mine + experts), aside, 0.0)
    share = jnp.sum(picked, axis=1, keepdims=True)
    hidden = []
    for w_ref in (in_own, in_other):
        gate_up = jnp.dot(tokens, w_ref[...], preferred_element_type=jnp.float32)
        gate = gate_up[:, :units]
        hidden.append((gate / (1.0 + jnp.exp(-gate)) * gate_up[:, units:]).astype(jnp.bfloat16))
    result = jnp.dot(hidden[0], down_own[...], preferred_element_type=jnp.float32) + jnp.dot(
        hidden[1], down_other[...], preferred_element_type=jnp.float32
    )
    result = result * share
    count = tokens.shape[0] // (chips * rows)
    for d in range(chips):
        for i in range(count):
            start = (i * chips + d) * rows
            piece = result[start : start + rows]
            to = ((d % (chips // 2)) * count + i) * rows
            if d < chips // 2:
                kept_ref[to : to + rows, :] = piece
            else:
                sent_ref[to : to + rows, :] = piece.astype(jnp.bfloat16)


def run_experts(blocks, weights, rows, width):
    shape = (sum(block.shape[0] for block in blocks) // 2, width)
    return kernel_call(
        functools.partial(expert_kernel, rows),
        (*blocks, *weights),
        (jax.ShapeDtypeStruct(shape, jnp.float32), jax.ShapeDtypeStruct(shape, jnp.bfloat16)),
        cost=pl.CostEstimate(flops=1 << 30, bytes_accessed=4 << 20, transcendentals=0),
    )


def merge_kernel(kept_ref, more_ref, *out_refs):
    total = kept_ref[...] + more_ref[...].astype(jnp.float32)
    start = 0
    for ref in out_refs:
        ref[...] = total[start : start + ref.shape[0]].astype(ref.dtype)
        start += ref.shape[0]


def merge(kept, more, pieces):
    outs = tuple(jax.ShapeDtypeStruct((rows, kept.shape[1]), dtype) for rows, dtype in pieces)
    return kernel_call(merge_kernel, (kept, more), outs)


def homeward(kept, sent, aways, rows):
    bit = lax.axis_size("side") // 4
    while bit:
        more = partner(sent, "side", 2 * bit)
        half = kept.shape[0] // 2
        pieces = ((half, jnp.float32), (half, jnp.bfloat16))
        kept, sent = merge(kept, more, pieces)
        bit //= 2
    more = partner(sent, "dev", 1)
    pieces = tuple((rows, jnp.bfloat16 if away else jnp.float32) for away in aways)
    return merge(kept, more, pieces)


def dev_groups(devs):
    upper = list(range(0, devs, 2))
    return upper[: len(upper) // 2], upper[len(upper) // 2 :]


def body(
    queries,
    kv_cache,
    new_kv,
    lengths,
    residual,
    w_out,
    norm_gain,
    expert_ids,
    route_level,
    w_in,
    w_down,
):
    rows, width = residual.shape
    devs = lax.axis_size("dev")

    w_other = partner(w_out, "side", 1)
    blocks, w_near = attend(queries, kv_cache, new_kv, lengths, w_out)
    total, sent, more = project(blocks, w_near, w_other, residual, expert_ids, route_level)
    w_in, w_down = fetch(sent, w_in, w_down)
    w_in, w_down, more = lax.optimization_barrier((w_in, w_down, more))
    weights = (w_in, partner(w_in, "side", 1), w_down, partner(w_down, "side", 1))
    normed, stream = kernel_call(
        norm_kernel,
        (total, more, norm_gain.reshape(1, width)),
        (
            jax.ShapeDtypeStruct(total.shape, jnp.bfloat16),
            jax.ShapeDtypeStruct((rows, width), jnp.bfloat16),
        ),
    )

    early, late = dev_groups(devs)
    near = {0: normed}
    for away in late + early[1:]:
        near[away] = partner(normed, "dev", away)
    near_early = [near[away] for away in early]
    far_early = [partner(jnp.concatenate(near_early), "dev", 1)]
    near_late = [near[away] for away in late]
    far_late = [partner(near[away], "dev", 1) for away in late]
    home = []
    for aways, blocks in ((early, near_early + far_early), (late, near_late + far_late)):
        kept, sent = run_experts(blocks, weights, rows, width)
        for away, block in zip(aways, homeward(kept, sent, aways, rows)):
            if away:
                block = partner(block, "dev", away).astype(jnp.float32)
            home.append(block)
    expert_sum = functools.reduce(jnp.add, home)
    return (stream, expert_sum.astype(jnp.bfloat16))


def solution(mesh):
    by_request = ("groups", "dev", "side")
    return jax.shard_map(
        body,
        mesh=mesh,
        in_specs=(
            P(by_request, None),
            P(by_request, None, None),
            P(by_request, None),
            P(by_request),
            P(by_request, None),
            P("side", None),
            P(),
            P(by_request, None),
            P(by_request, None),
            P(("dev", "side"), None, None),
            P(("dev", "side"), None, None),
        ),
        out_specs=(P(by_request, None), P(by_request, None)),
        check_vma=False,
    )
```

```python
import functools
import math

import jax
import jax.numpy as jnp
from jax import lax
from jax.experimental import pallas as pl
from jax.experimental.pallas import tpu as pltpu
from jax.sharding import PartitionSpec as P

HD = 128
GRANT = 16 << 20
VMEM = pl.BlockSpec(memory_space=pltpu.VMEM)
HBM = pl.BlockSpec(memory_space=pltpu.HBM)


def kernel_call(body, operands, outs, in_specs=None, scratch=(), cost=None):
    return pl.pallas_call(
        body,
        out_shape=outs,
        in_specs=in_specs or [VMEM] * len(operands),
        out_specs=jax.tree.map(lambda _: VMEM, outs, is_leaf=lambda x: hasattr(x, "shape")),
        scratch_shapes=list(scratch),
        compiler_params=pltpu.CompilerParams(vmem_limit_bytes=GRANT),
        cost_estimate=cost,
    )(*operands)


def in_hbm(*arrays):
    return [pltpu.with_memory_space_constraint(x, pltpu.HBM) for x in arrays]


def partner(block, axis, mask):
    count = lax.axis_size(axis)
    return lax.ppermute(block, axis, [(i, i ^ mask) for i in range(count)])


def start_all(copies):
    for copy in copies:
        copy.start()


def wait_all(copies):
    for copy in copies:
        copy.wait()


def half_copies(which, q_hbm, kv_hbm, new_hbm, q_ref, kv, new_ref, sems, kv_sems):
    rows, _, span = kv.shape
    share = span // 2
    whole = kv_hbm.shape[2] // 2
    keys = pl.ds(pl.multiple_of(which * share, share), share)
    values = pl.ds(pl.multiple_of(whole + which * share, share), share)
    span_q = q_ref.shape[1]
    small = [
        pltpu.make_async_copy(
            q_hbm.at[:, pl.ds(pl.multiple_of(which * span_q, span_q), span_q)],
            q_ref,
            sems.at[0],
        ),
        pltpu.make_async_copy(new_hbm.at[:, keys], new_ref.at[:, :share], sems.at[1]),
        pltpu.make_async_copy(new_hbm.at[:, values], new_ref.at[:, share:], sems.at[2]),
    ]
    large = [
        (
            pltpu.make_async_copy(kv_hbm.at[r, :, keys], kv.at[r, :, :share], kv_sems.at[0, r]),
            pltpu.make_async_copy(kv_hbm.at[r, :, values], kv.at[r, :, share:], kv_sems.at[1, r]),
        )
        for r in range(rows)
    ]
    return small, large


def attend_heads(q_ref, kv, new_ref, lengths, flat, mixed_flat, key_wait, value_wait, length_wait):
    rows, cache, span = kv.shape
    share = span // 2
    kv_heads = share // HD
    heads = q_ref.shape[1] // HD
    group = heads // kv_heads
    for h in range(heads):
        flat[h * rows : (h + 1) * rows, :] = q_ref[:, h * HD : (h + 1) * HD].astype(jnp.float32)
    scaling = 1.0 / math.sqrt(HD)
    asked = [flat[pl.ds(r, heads, stride=rows), :] for r in range(rows)]
    place = lax.broadcasted_iota(jnp.int32, (heads, cache), 1)
    fresh = new_ref[...].astype(jnp.float32)

    def spread(r, start):
        pieces = [
            jnp.broadcast_to(
                fresh[r : r + 1, start + g * HD : start + (g + 1) * HD], (group, HD)
            )
            for g in range(kv_heads)
        ]
        return jnp.concatenate(pieces, axis=0)

    all_scores = []
    for r in range(rows):
        q = asked[r].astype(jnp.bfloat16)
        key_wait(r)
        all_scores.append(
            jnp.concatenate(
                [
                    lax.dot_general(
                        q[g * group : (g + 1) * group],
                        kv[r, :, g * HD : (g + 1) * HD],
                        (((1,), (1,)), ((), ())),
                        preferred_element_type=jnp.float32,
                    )
                    for g in range(kv_heads)
                ],
                axis=0,
            )
        )
    length_wait()
    probs, own_probs = [], []
    for r in range(rows):
        own = jnp.sum(asked[r] * spread(r, 0), axis=1, keepdims=True) * scaling
        scores = jnp.where(place < lengths[r], all_scores[r] * scaling, -jnp.inf)
        peak = jnp.maximum(jnp.max(scores, axis=1, keepdims=True), own)
        weights = jnp.exp(scores - peak)
        own_weight = jnp.exp(own - peak)
        denominator = jnp.sum(weights, axis=1, keepdims=True) + own_weight
        scale = 1.0 / denominator
        probs.append((weights * scale).astype(jnp.bfloat16))
        own_probs.append((own_weight * scale).astype(jnp.bfloat16).astype(jnp.float32))
    for r in range(rows):
        value_wait(r)
        mixed = jnp.concatenate(
            [
                jnp.dot(
                    probs[r][g * group : (g + 1) * group],
                    kv[r, :, share + g * HD : share + (g + 1) * HD],
                    preferred_element_type=jnp.float32,
                )
                for g in range(kv_heads)
            ],
            axis=0,
        )
        mixed_flat[pl.ds(r, heads, stride=rows), :] = mixed + own_probs[r] * spread(r, share)


def put_pieces(out_ref, mixed_flat):
    pieces, rows, columns = out_ref.shape
    heads = columns // HD // 2
    mine = lax.axis_index("side")
    core = lax.rem(mine, 2)
    low = lax.rem(lax.div(mine, 2), pieces)
    for d in range(pieces):
        chip = jnp.bitwise_xor(low, d)
        for other in range(2):
            first = (2 * chip + jnp.bitwise_xor(core, other)) * heads
            for h in range(heads):
                at = pl.multiple_of((first + h) * rows, rows)
                to = (other * heads + h) * HD
                out_ref[d, :, to : to + HD] = mixed_flat[pl.ds(at, rows), :].astype(jnp.bfloat16)


def far_kernel(
    q_hbm, kv_hbm, new_hbm, length_hbm, out_ref, q_near, kv_near, new_near, q_ref, kv, new_ref,
    lengths, flat, mixed_flat, sems, kv_sems, near_sems, near_kv_sems, length_sem,
):
    here = lax.div(lax.axis_index("side"), lax.axis_size("side") // 2)
    length_copy = pltpu.make_async_copy(length_hbm, lengths, length_sem)
    small, large = half_copies(
        1 - here, q_hbm, kv_hbm, new_hbm, q_ref, kv, new_ref, sems, kv_sems
    )
    near_small, near_large = half_copies(
        here, q_hbm, kv_hbm, new_hbm, q_near, kv_near, new_near, near_sems, near_kv_sems
    )
    start_all(small)
    start_all([length_copy] + [pair[0] for pair in large])
    start_all([pair[1] for pair in large])
    start_all(near_small)
    for pair in near_large:
        start_all(pair)
    wait_all(small)
    attend_heads(
        q_ref, kv, new_ref, lengths, flat, mixed_flat,
        lambda r: large[r][0].wait(), lambda r: large[r][1].wait(), length_copy.wait,
    )
    put_pieces(out_ref, mixed_flat)
    wait_all(near_small)
    for pair in near_large:
        wait_all(pair)


def near_kernel(
    q_ref, kv, new_ref, length_hbm, w_hbm, out_ref, w_ref, lengths, flat, mixed_flat, length_sem,
    w_sem,
):
    length_copy = pltpu.make_async_copy(length_hbm, lengths, length_sem)
    w_copy = pltpu.make_async_copy(w_hbm, w_ref, w_sem)
    start_all([length_copy, w_copy])
    nothing = lambda r: None
    attend_heads(
        q_ref, kv, new_ref, lengths, flat, mixed_flat, nothing, nothing, length_copy.wait
    )
    put_pieces(out_ref, mixed_flat)
    w_copy.wait()


def attend(queries, kv_cache, new_kv, lengths, w_out):
    rows, features = queries.shape
    chips = lax.axis_size("side") // 2
    q_half = pltpu.VMEM((rows, features // 2), queries.dtype)
    kv_half = pltpu.VMEM((*kv_cache.shape[:2], kv_cache.shape[2] // 2), kv_cache.dtype)
    new_half = pltpu.VMEM((rows, new_kv.shape[1] // 2), new_kv.dtype)
    pieces = pltpu.VMEM((chips // 2, rows, features // chips), jnp.bfloat16)
    flat = pltpu.VMEM((rows * features // 2 // HD, HD), jnp.float32)
    smem = pltpu.SMEM(lengths.shape, lengths.dtype)
    dma = pltpu.SemaphoreType.DMA
    queries, kv_cache, new_kv, lengths, w_out = in_hbm(queries, kv_cache, new_kv, lengths, w_out)
    sent, q_near, kv_near, new_near = kernel_call(
        far_kernel,
        (queries, kv_cache, new_kv, lengths),
        (pieces, q_half, kv_half, new_half),
        in_specs=[HBM] * 4,
        scratch=[
            q_half, kv_half, new_half, smem, flat, flat,
            dma((3,)), dma((2, rows)), dma((3,)), dma((2, rows)), dma,
        ],
    )
    received = partner(sent, "side", chips)
    kept, w_near = kernel_call(
        near_kernel,
        (q_near, kv_near, new_near, lengths, w_out),
        (pieces, pltpu.VMEM(w_out.shape, w_out.dtype)),
        in_specs=[VMEM] * 3 + [HBM] * 2,
        scratch=[smem, flat, flat, dma, dma],
        cost=pl.CostEstimate(flops=8 << 20, bytes_accessed=8 << 20, transcendentals=0),
    )
    blocks = {0: kept, chips // 2: received}
    bit = chips // 4
    while bit:
        blocks.update({d ^ bit: partner(block, "side", 2 * bit) for d, block in blocks.items()})
        bit //= 2
    return [blocks[d] for d in range(chips)], w_near


def project_kernel(*refs):
    kept_ref, sent_ref = refs[-2:]
    w_near, w_other, residual_ref, ids_ref, level_ref = refs[-7:-2]
    blocks = refs[:-7]
    rows, width = residual_ref.shape
    depth = w_near.shape[0]
    experts = lax.axis_size("dev") * lax.axis_size("side") // 2
    lhs = jnp.concatenate([ref[d % ref.shape[0]] for d, ref in enumerate(blocks)], axis=0)
    product = jnp.dot(lhs[:, :depth], w_near[...], preferred_element_type=jnp.float32) + jnp.dot(
        lhs[:, depth:], w_other[...], preferred_element_type=jnp.float32
    )
    level = level_ref[...].astype(jnp.float32)
    share = level / jnp.sum(level, axis=1, keepdims=True)
    spare = kept_ref.shape[1] - width
    lane = lax.broadcasted_iota(jnp.int32, (rows, spare), 1)
    ids = ids_ref[...]
    high, low = jnp.zeros((2, rows, spare), jnp.float32)
    for k in range(ids.shape[1]):
        chosen, part = ids[:, k : k + 1], share[:, k : k + 1]
        top = part.astype(jnp.bfloat16).astype(jnp.float32)
        high = high + jnp.where(lane == chosen, top, 0.0)
        low = low + jnp.where(lane == chosen + experts, part - top, 0.0)
    count = len(blocks)
    for d in range(count):
        here = product[d * rows : (d + 1) * rows]
        aside = jnp.zeros((rows, spare), jnp.float32)
        if d == 0:
            here = here + residual_ref[...].astype(jnp.float32)
            aside = high + low
        at = slice(d * rows, (d + 1) * rows)
        kept_ref[at, :width] = here
        kept_ref[at, width:] = aside
        at = slice((d ^ 1) * rows, ((d ^ 1) + 1) * rows)
        sent_ref[at, :width] = here.astype(jnp.bfloat16)
        sent_ref[at, width:] = aside.astype(jnp.bfloat16)


def project(blocks, w_near, w_other, residual, expert_ids, route_level):
    rows, width = residual.shape
    chips = len(blocks)
    experts = lax.axis_size("dev") * chips
    shape = (chips * rows, width + pl.cdiv(2 * experts, 128) * 128)
    kept, sent = kernel_call(
        project_kernel,
        (
            *blocks,
            w_near,
            pltpu.with_memory_space_constraint(w_other, pltpu.VMEM),
            residual,
            expert_ids,
            route_level,
        ),
        (jax.ShapeDtypeStruct(shape, jnp.float32), jax.ShapeDtypeStruct(shape, jnp.bfloat16)),
    )
    bit = 1
    more = partner(sent, "side", 2 * bit)
    while 2 * bit < chips:
        kept = kept + more.astype(jnp.float32)
        bit *= 2
        swapped = [kept[(d ^ bit) * rows : ((d ^ bit) + 1) * rows] for d in range(chips)]
        more = partner(jnp.concatenate(swapped).astype(jnp.bfloat16), "side", 2 * bit)
    return kept, sent, more


def fetch_kernel(after_ref, in_hbm_ref, down_hbm_ref, in_ref, down_ref, sems):
    copies = [
        pltpu.make_async_copy(in_hbm_ref.at[0], in_ref, sems.at[0]),
        pltpu.make_async_copy(down_hbm_ref.at[0], down_ref, sems.at[1]),
    ]
    start_all(copies)
    wait_all(copies)


def fetch(after, w_in, w_down):
    return kernel_call(
        fetch_kernel,
        (after, *in_hbm(w_in, w_down)),
        (pltpu.VMEM(w_in.shape[1:], w_in.dtype), pltpu.VMEM(w_down.shape[1:], w_down.dtype)),
        in_specs=[VMEM, HBM, HBM],
        scratch=[pltpu.SemaphoreType.DMA((2,))],
        cost=pl.CostEstimate(flops=0, bytes_accessed=8 << 20, transcendentals=0),
    )


def norm_kernel(total_ref, more_ref, gain_ref, normed_ref, stream_ref):
    rows, width = stream_ref.shape
    stream = total_ref[:, :width] + more_ref[:, :width].astype(jnp.float32)
    mean_square = jnp.mean(stream * stream, axis=1, keepdims=True)
    normed = stream * lax.rsqrt(mean_square + 1e-06) * gain_ref[...]
    normed_ref[:, :width] = normed.astype(jnp.bfloat16)
    aside = total_ref[:, width:] + more_ref[:, width:].astype(jnp.float32)
    normed_ref[:, width:] = aside.astype(jnp.bfloat16)
    stream_ref[...] = stream[:rows].astype(jnp.bfloat16)


def expert_kernel(rows, *refs):
    kept_ref, sent_ref = refs[-2:]
    in_own, in_other, down_own, down_other = refs[-6:-2]
    blocks = refs[:-6]
    width = kept_ref.shape[1]
    units = down_own.shape[0]
    chips = lax.axis_size("side") // 2
    experts = lax.axis_size("dev") * chips
    mine = lax.axis_index("dev") * chips + lax.div(lax.axis_index("side"), 2)
    tokens = jnp.concatenate([ref[:, :width] for ref in blocks], axis=0)
    aside = jnp.concatenate([ref[:, width:] for ref in blocks], axis=0).astype(jnp.float32)
    lane = lax.broadcasted_iota(jnp.int32, aside.shape, 1)
    picked = jnp.where((lane == mine) | (lane == mine + experts), aside, 0.0)
    share = jnp.sum(picked, axis=1, keepdims=True)
    hidden = []
    for w_ref in (in_own, in_other):
        gate_up = jnp.dot(tokens, w_ref[...], preferred_element_type=jnp.float32)
        gate = gate_up[:, :units]
        hidden.append((gate / (1.0 + jnp.exp(-gate)) * gate_up[:, units:]).astype(jnp.bfloat16))
    result = jnp.dot(hidden[0], down_own[...], preferred_element_type=jnp.float32) + jnp.dot(
        hidden[1], down_other[...], preferred_element_type=jnp.float32
    )
    result = result * share
    count = tokens.shape[0] // (chips * rows)
    for d in range(chips):
        for i in range(count):
            start = (i * chips + d) * rows
            piece = result[start : start + rows]
            to = ((d % (chips // 2)) * count + i) * rows
            if d < chips // 2:
                kept_ref[to : to + rows, :] = piece
            else:
                sent_ref[to : to + rows, :] = piece.astype(jnp.bfloat16)


def run_experts(blocks, weights, rows, width):
    shape = (sum(block.shape[0] for block in blocks) // 2, width)
    return kernel_call(
        functools.partial(expert_kernel, rows),
        (*blocks, *weights),
        (jax.ShapeDtypeStruct(shape, jnp.float32), jax.ShapeDtypeStruct(shape, jnp.bfloat16)),
        cost=pl.CostEstimate(flops=1 << 30, bytes_accessed=4 << 20, transcendentals=0),
    )


def merge_kernel(kept_ref, more_ref, *out_refs):
    total = kept_ref[...] + more_ref[...].astype(jnp.float32)
    start = 0
    for ref in out_refs:
        ref[...] = total[start : start + ref.shape[0]].astype(ref.dtype)
        start += ref.shape[0]


def merge(kept, more, pieces):
    outs = tuple(jax.ShapeDtypeStruct((rows, kept.shape[1]), dtype) for rows, dtype in pieces)
    return kernel_call(merge_kernel, (kept, more), outs)


def homeward(kept, sent, aways, rows):
    bit = lax.axis_size("side") // 4
    while bit:
        more = partner(sent, "side", 2 * bit)
        half = kept.shape[0] // 2
        pieces = ((half, jnp.float32), (half, jnp.bfloat16))
        kept, sent = merge(kept, more, pieces)
        bit //= 2
    more = partner(sent, "dev", 1)
    pieces = tuple((rows, jnp.bfloat16 if away else jnp.float32) for away in aways)
    return merge(kept, more, pieces)


def dev_groups(devs):
    upper = list(range(0, devs, 2))
    return upper[: len(upper) // 2], upper[len(upper) // 2 :]


def body(
    queries,
    kv_cache,
    new_kv,
    lengths,
    residual,
    w_out,
    norm_gain,
    expert_ids,
    route_level,
    w_in,
    w_down,
):
    rows, width = residual.shape
    devs = lax.axis_size("dev")

    w_other = partner(w_out, "side", 1)
    blocks, w_near = attend(queries, kv_cache, new_kv, lengths, w_out)
    total, sent, more = project(blocks, w_near, w_other, residual, expert_ids, route_level)
    w_in, w_down = fetch(sent, w_in, w_down)
    weights = (w_in, partner(w_in, "side", 1), w_down, partner(w_down, "side", 1))
    normed, stream = kernel_call(
        norm_kernel,
        (total, more, norm_gain.reshape(1, width)),
        (
            jax.ShapeDtypeStruct(total.shape, jnp.bfloat16),
            pltpu.VMEM((rows, width), jnp.bfloat16),
        ),
    )

    early, late = dev_groups(devs)
    near = {0: normed}
    for away in early[1:] + late:
        near[away] = partner(normed, "dev", away)
    home = []
    for aways in (early, late):
        blocks = [near[away] for away in aways]
        blocks += [partner(near[away], "dev", 1) for away in aways]
        kept, sent = run_experts(blocks, weights, rows, width)
        for away, block in zip(aways, homeward(kept, sent, aways, rows)):
            if away:
                block = partner(block, "dev", away).astype(jnp.float32)
            home.append(block)
    expert_sum = functools.reduce(jnp.add, home)
    return (stream, expert_sum.astype(jnp.bfloat16))


def solution(mesh):
    by_request = ("groups", "dev", "side")
    return jax.shard_map(
        body,
        mesh=mesh,
        in_specs=(
            P(by_request, None),
            P(by_request, None, None),
            P(by_request, None),
            P(by_request),
            P(by_request, None),
            P("side", None),
            P(),
            P(by_request, None),
            P(by_request, None),
            P(("dev", "side"), None, None),
            P(("dev", "side"), None, None),
        ),
        out_specs=(P(by_request, None), P(by_request, None)),
        check_vma=False,
    )
```

```python
import functools
import math

import jax
import jax.numpy as jnp
from jax import lax
from jax.experimental import pallas as pl
from jax.experimental.pallas import tpu as pltpu
from jax.sharding import PartitionSpec as P

HD = 128
GRANT = 16 << 20
VMEM = pl.BlockSpec(memory_space=pltpu.VMEM)
HBM = pl.BlockSpec(memory_space=pltpu.HBM)


def kernel_call(body, operands, outs, in_specs=None, scratch=(), cost=None):
    return pl.pallas_call(
        body,
        out_shape=outs,
        in_specs=in_specs or [VMEM] * len(operands),
        out_specs=jax.tree.map(lambda _: VMEM, outs, is_leaf=lambda x: hasattr(x, "shape")),
        scratch_shapes=list(scratch),
        compiler_params=pltpu.CompilerParams(vmem_limit_bytes=GRANT),
        cost_estimate=cost,
    )(*operands)


def in_hbm(*arrays):
    return [pltpu.with_memory_space_constraint(x, pltpu.HBM) for x in arrays]


def partner(block, axis, mask):
    count = lax.axis_size(axis)
    return lax.ppermute(block, axis, [(i, i ^ mask) for i in range(count)])


def start_all(copies):
    for copy in copies:
        copy.start()


def wait_all(copies):
    for copy in copies:
        copy.wait()


def half_copies(which, q_hbm, kv_hbm, new_hbm, q_ref, kv, new_ref, sems, kv_sems):
    _, _, span = kv.shape
    share = span // 2
    whole = kv_hbm.shape[2] // 2
    keys = pl.ds(pl.multiple_of(which * share, share), share)
    values = pl.ds(pl.multiple_of(whole + which * share, share), share)
    span_q = q_ref.shape[1]
    small = [
        pltpu.make_async_copy(
            q_hbm.at[:, pl.ds(pl.multiple_of(which * span_q, span_q), span_q)],
            q_ref,
            sems.at[0],
        ),
        pltpu.make_async_copy(new_hbm.at[:, keys], new_ref.at[:, :share], sems.at[1]),
        pltpu.make_async_copy(new_hbm.at[:, values], new_ref.at[:, share:], sems.at[2]),
    ]
    large = [
        pltpu.make_async_copy(kv_hbm.at[:, :, keys], kv.at[:, :, :share], kv_sems.at[0]),
        pltpu.make_async_copy(kv_hbm.at[:, :, values], kv.at[:, :, share:], kv_sems.at[1]),
    ]
    return small, large


def attend_heads(q_ref, kv, new_ref, lengths, flat, mixed_flat, value_wait):
    rows, cache, span = kv.shape
    share = span // 2
    kv_heads = share // HD
    heads = q_ref.shape[1] // HD
    group = heads // kv_heads
    for h in range(heads):
        flat[h * rows : (h + 1) * rows, :] = q_ref[:, h * HD : (h + 1) * HD].astype(jnp.float32)
    scaling = 1.0 / math.sqrt(HD)
    asked = [flat[pl.ds(r, heads, stride=rows), :] for r in range(rows)]
    place = lax.broadcasted_iota(jnp.int32, (heads, cache), 1)
    fresh = new_ref[...].astype(jnp.float32)

    def spread(r, start):
        pieces = [
            jnp.broadcast_to(
                fresh[r : r + 1, start + g * HD : start + (g + 1) * HD], (group, HD)
            )
            for g in range(kv_heads)
        ]
        return jnp.concatenate(pieces, axis=0)

    all_scores = []
    for r in range(rows):
        q = asked[r].astype(jnp.bfloat16)
        all_scores.append(
            jnp.concatenate(
                [
                    lax.dot_general(
                        q[g * group : (g + 1) * group],
                        kv[r, :, g * HD : (g + 1) * HD],
                        (((1,), (1,)), ((), ())),
                        preferred_element_type=jnp.float32,
                    )
                    for g in range(kv_heads)
                ],
                axis=0,
            )
        )
    probs, own_probs = [], []
    for r in range(rows):
        own = jnp.sum(asked[r] * spread(r, 0), axis=1, keepdims=True) * scaling
        scores = jnp.where(place < lengths[r], all_scores[r] * scaling, -jnp.inf)
        peak = jnp.maximum(jnp.max(scores, axis=1, keepdims=True), own)
        weights = jnp.exp(scores - peak)
        own_weight = jnp.exp(own - peak)
        denominator = jnp.sum(weights, axis=1, keepdims=True) + own_weight
        scale = 1.0 / denominator
        probs.append((weights * scale).astype(jnp.bfloat16))
        own_probs.append((own_weight * scale).astype(jnp.bfloat16).astype(jnp.float32))
    value_wait()
    for r in range(rows):
        mixed = jnp.concatenate(
            [
                jnp.dot(
                    probs[r][g * group : (g + 1) * group],
                    kv[r, :, share + g * HD : share + (g + 1) * HD],
                    preferred_element_type=jnp.float32,
                )
                for g in range(kv_heads)
            ],
            axis=0,
        )
        mixed_flat[pl.ds(r, heads, stride=rows), :] = mixed + own_probs[r] * spread(r, share)


def put_pieces(out_ref, mixed_flat):
    pieces, rows, columns = out_ref.shape
    heads = columns // HD // 2
    mine = lax.axis_index("side")
    core = lax.rem(mine, 2)
    low = lax.rem(lax.div(mine, 2), pieces)
    for d in range(pieces):
        chip = jnp.bitwise_xor(low, d)
        for other in range(2):
            first = (2 * chip + jnp.bitwise_xor(core, other)) * heads
            for h in range(heads):
                at = pl.multiple_of((first + h) * rows, rows)
                to = (other * heads + h) * HD
                out_ref[d, :, to : to + HD] = mixed_flat[pl.ds(at, rows), :].astype(jnp.bfloat16)


def half_kernel(
    away, q_hbm, kv_hbm, new_hbm, length_hbm, out_ref, q_ref, kv, new_ref, lengths, flat,
    mixed_flat, sems, kv_sems, length_sem,
):
    here = lax.div(lax.axis_index("side"), lax.axis_size("side") // 2)
    length_copy = pltpu.make_async_copy(length_hbm, lengths, length_sem)
    small, large = half_copies(
        jnp.bitwise_xor(here, away), q_hbm, kv_hbm, new_hbm, q_ref, kv, new_ref, sems, kv_sems
    )
    start_all([*small, length_copy, *large])
    wait_all([*small, length_copy, large[0]])
    attend_heads(q_ref, kv, new_ref, lengths, flat, mixed_flat, large[1].wait)
    put_pieces(out_ref, mixed_flat)


def attend(queries, kv_cache, new_kv, lengths):
    rows, features = queries.shape
    chips = lax.axis_size("side") // 2
    q_half = pltpu.VMEM((rows, features // 2), queries.dtype)
    kv_half = pltpu.VMEM((*kv_cache.shape[:2], kv_cache.shape[2] // 2), kv_cache.dtype)
    new_half = pltpu.VMEM((rows, new_kv.shape[1] // 2), new_kv.dtype)
    pieces = pltpu.VMEM((chips // 2, rows, features // chips), jnp.bfloat16)
    flat = pltpu.VMEM((rows * features // 2 // HD, HD), jnp.float32)
    smem = pltpu.SMEM(lengths.shape, lengths.dtype)
    dma = pltpu.SemaphoreType.DMA
    queries, kv_cache, new_kv, lengths = in_hbm(queries, kv_cache, new_kv, lengths)

    def half(away):
        return kernel_call(
            functools.partial(half_kernel, away),
            (queries, kv_cache, new_kv, lengths),
            pieces,
            in_specs=[HBM] * 4,
            scratch=[
                q_half, kv_half, new_half, smem, flat, flat, dma((3,)), dma((2,)), dma,
            ],
            cost=pl.CostEstimate(flops=8 << 20, bytes_accessed=6 << 20, transcendentals=0),
        )

    received = partner(half(1), "side", chips)
    kept = half(0)
    blocks = {0: kept, chips // 2: received}
    bit = chips // 4
    while bit:
        blocks.update({d ^ bit: partner(block, "side", 2 * bit) for d, block in blocks.items()})
        bit //= 2
    return [blocks[d] for d in range(chips)]


def project_kernel(*refs):
    kept_ref, sent_ref = refs[-2:]
    w_near, w_other, residual_ref, ids_ref, level_ref = refs[-7:-2]
    blocks = refs[:-7]
    rows, width = residual_ref.shape
    depth = w_near.shape[0]
    experts = lax.axis_size("dev") * lax.axis_size("side") // 2
    lhs = jnp.concatenate([ref[d % ref.shape[0]] for d, ref in enumerate(blocks)], axis=0)
    product = jnp.dot(lhs[:, :depth], w_near[...], preferred_element_type=jnp.float32) + jnp.dot(
        lhs[:, depth:], w_other[...], preferred_element_type=jnp.float32
    )
    level = level_ref[...].astype(jnp.float32)
    share = level / jnp.sum(level, axis=1, keepdims=True)
    spare = kept_ref.shape[1] - width
    lane = lax.broadcasted_iota(jnp.int32, (rows, spare), 1)
    ids = ids_ref[...]
    high, low = jnp.zeros((2, rows, spare), jnp.float32)
    for k in range(ids.shape[1]):
        chosen, part = ids[:, k : k + 1], share[:, k : k + 1]
        top = part.astype(jnp.bfloat16).astype(jnp.float32)
        high = high + jnp.where(lane == chosen, top, 0.0)
        low = low + jnp.where(lane == chosen + experts, part - top, 0.0)
    count = len(blocks)
    for d in range(count):
        here = product[d * rows : (d + 1) * rows]
        aside = jnp.zeros((rows, spare), jnp.float32)
        if d == 0:
            here = here + residual_ref[...].astype(jnp.float32)
            aside = high + low
        at = slice(d * rows, (d + 1) * rows)
        kept_ref[at, :width] = here
        kept_ref[at, width:] = aside
        at = slice((d ^ 1) * rows, ((d ^ 1) + 1) * rows)
        sent_ref[at, :width] = here.astype(jnp.bfloat16)
        sent_ref[at, width:] = aside.astype(jnp.bfloat16)


def project(blocks, w_near, w_other, residual, expert_ids, route_level):
    rows, width = residual.shape
    chips = len(blocks)
    experts = lax.axis_size("dev") * chips
    shape = (chips * rows, width + pl.cdiv(2 * experts, 128) * 128)
    kept, sent = kernel_call(
        project_kernel,
        (
            *blocks,
            pltpu.with_memory_space_constraint(w_near, pltpu.VMEM),
            pltpu.with_memory_space_constraint(w_other, pltpu.VMEM),
            residual,
            expert_ids,
            route_level,
        ),
        (jax.ShapeDtypeStruct(shape, jnp.float32), jax.ShapeDtypeStruct(shape, jnp.bfloat16)),
    )
    bit = 1
    more = partner(sent, "side", 2 * bit)
    while 2 * bit < chips:
        kept = kept + more.astype(jnp.float32)
        bit *= 2
        swapped = [kept[(d ^ bit) * rows : ((d ^ bit) + 1) * rows] for d in range(chips)]
        more = partner(jnp.concatenate(swapped).astype(jnp.bfloat16), "side", 2 * bit)
    return kept, sent, more


def norm_kernel(total_ref, more_ref, gain_ref, normed_ref, stream_ref):
    rows, width = stream_ref.shape
    stream = total_ref[:, :width] + more_ref[:, :width].astype(jnp.float32)
    mean_square = jnp.mean(stream * stream, axis=1, keepdims=True)
    normed = stream * lax.rsqrt(mean_square + 1e-06) * gain_ref[...]
    normed_ref[:, :width] = normed.astype(jnp.bfloat16)
    aside = total_ref[:, width:] + more_ref[:, width:].astype(jnp.float32)
    normed_ref[:, width:] = aside.astype(jnp.bfloat16)
    stream_ref[...] = stream[:rows].astype(jnp.bfloat16)


def expert_kernel(rows, *refs):
    kept_ref, sent_ref = refs[-2:]
    in_own, in_other, down_own, down_other = refs[-6:-2]
    blocks = refs[:-6]
    width = kept_ref.shape[1]
    units = down_own.shape[0]
    chips = lax.axis_size("side") // 2
    experts = lax.axis_size("dev") * chips
    mine = lax.axis_index("dev") * chips + lax.div(lax.axis_index("side"), 2)
    tokens = jnp.concatenate([ref[:, :width] for ref in blocks], axis=0)
    aside = jnp.concatenate([ref[:, width:] for ref in blocks], axis=0).astype(jnp.float32)
    lane = lax.broadcasted_iota(jnp.int32, aside.shape, 1)
    picked = jnp.where((lane == mine) | (lane == mine + experts), aside, 0.0)
    share = jnp.sum(picked, axis=1, keepdims=True)
    hidden = []
    for w_ref in (in_own, in_other):
        gate_up = jnp.dot(tokens, w_ref[...], preferred_element_type=jnp.float32)
        gate = gate_up[:, :units]
        hidden.append((gate / (1.0 + jnp.exp(-gate)) * gate_up[:, units:]).astype(jnp.bfloat16))
    result = jnp.dot(hidden[0], down_own[...], preferred_element_type=jnp.float32) + jnp.dot(
        hidden[1], down_other[...], preferred_element_type=jnp.float32
    )
    result = result * share
    count = tokens.shape[0] // (chips * rows)
    for d in range(chips):
        for i in range(count):
            start = (i * chips + d) * rows
            piece = result[start : start + rows]
            to = ((d % (chips // 2)) * count + i) * rows
            if d < chips // 2:
                kept_ref[to : to + rows, :] = piece
            else:
                sent_ref[to : to + rows, :] = piece.astype(jnp.bfloat16)


def run_experts(blocks, weights, rows, width):
    shape = (sum(block.shape[0] for block in blocks) // 2, width)
    return kernel_call(
        functools.partial(expert_kernel, rows),
        (*blocks, *weights),
        (jax.ShapeDtypeStruct(shape, jnp.float32), jax.ShapeDtypeStruct(shape, jnp.bfloat16)),
        cost=pl.CostEstimate(flops=1 << 30, bytes_accessed=4 << 20, transcendentals=0),
    )


def merge_kernel(kept_ref, more_ref, *out_refs):
    total = kept_ref[...] + more_ref[...].astype(jnp.float32)
    start = 0
    for ref in out_refs:
        ref[...] = total[start : start + ref.shape[0]].astype(ref.dtype)
        start += ref.shape[0]


def merge(kept, more, pieces):
    outs = tuple(jax.ShapeDtypeStruct((rows, kept.shape[1]), dtype) for rows, dtype in pieces)
    return kernel_call(merge_kernel, (kept, more), outs)


def homeward(kept, sent, aways, rows):
    bit = lax.axis_size("side") // 4
    while bit:
        more = partner(sent, "side", 2 * bit)
        half = kept.shape[0] // 2
        pieces = ((half, jnp.float32), (half, jnp.bfloat16))
        kept, sent = merge(kept, more, pieces)
        bit //= 2
    more = partner(sent, "dev", 1)
    pieces = tuple((rows, jnp.bfloat16 if away else jnp.float32) for away in aways)
    return merge(kept, more, pieces)


def dev_groups(devs):
    upper = list(range(0, devs, 2))
    return upper[: len(upper) // 2], upper[len(upper) // 2 :]


def body(
    queries,
    kv_cache,
    new_kv,
    lengths,
    residual,
    w_out,
    norm_gain,
    expert_ids,
    route_level,
    w_in,
    w_down,
):
    rows, width = residual.shape
    devs = lax.axis_size("dev")

    w_other = partner(w_out, "side", 1)
    in_other = partner(w_in[0], "side", 1)
    down_other = partner(w_down[0], "side", 1)
    blocks = attend(queries, kv_cache, new_kv, lengths)
    total, sent, more = project(blocks, w_out, w_other, residual, expert_ids, route_level)
    weights = [
        pltpu.with_memory_space_constraint(x, pltpu.VMEM)
        for x in (w_in[0], in_other, w_down[0], down_other)
    ]
    normed, stream = kernel_call(
        norm_kernel,
        (total, more, norm_gain.reshape(1, width)),
        (
            jax.ShapeDtypeStruct(total.shape, jnp.bfloat16),
            pltpu.VMEM((rows, width), jnp.bfloat16),
        ),
    )

    early, late = dev_groups(devs)
    near = {0: normed}
    for away in early[1:] + late:
        near[away] = partner(normed, "dev", away)
    home = []
    for aways in (early, late):
        blocks = [near[away] for away in aways]
        blocks += [partner(near[away], "dev", 1) for away in aways]
        kept, sent = run_experts(blocks, weights, rows, width)
        for away, block in zip(aways, homeward(kept, sent, aways, rows)):
            if away:
                block = partner(block, "dev", away).astype(jnp.float32)
            home.append(block)
    expert_sum = functools.reduce(jnp.add, home)
    return (stream, expert_sum.astype(jnp.bfloat16))


def solution(mesh):
    by_request = ("groups", "dev", "side")
    return jax.shard_map(
        body,
        mesh=mesh,
        in_specs=(
            P(by_request, None),
            P(by_request, None, None),
            P(by_request, None),
            P(by_request),
            P(by_request, None),
            P("side", None),
            P(),
            P(by_request, None),
            P(by_request, None),
            P(("dev", "side"), None, None),
            P(("dev", "side"), None, None),
        ),
        out_specs=(P(by_request, None), P(by_request, None)),
        check_vma=False,
    )
```

```python
import functools
import math

import jax
import jax.numpy as jnp
from jax import lax
from jax.experimental import pallas as pl
from jax.experimental.pallas import tpu as pltpu
from jax.sharding import PartitionSpec as P

HD = 128
GRANT = 16 << 20
VMEM = pl.BlockSpec(memory_space=pltpu.VMEM)
HBM = pl.BlockSpec(memory_space=pltpu.HBM)


def kernel_call(body, operands, outs, in_specs=None, scratch=(), cost=None):
    return pl.pallas_call(
        body,
        out_shape=outs,
        in_specs=in_specs or [VMEM] * len(operands),
        out_specs=jax.tree.map(lambda _: VMEM, outs, is_leaf=lambda x: hasattr(x, "shape")),
        scratch_shapes=list(scratch),
        compiler_params=pltpu.CompilerParams(vmem_limit_bytes=GRANT),
        cost_estimate=cost,
    )(*operands)


def in_hbm(*arrays):
    return [pltpu.with_memory_space_constraint(x, pltpu.HBM) for x in arrays]


def partner(block, axis, mask):
    count = lax.axis_size(axis)
    return lax.ppermute(block, axis, [(i, i ^ mask) for i in range(count)])


def across(block, over_dev, over_side):
    side = lax.axis_size("side")
    mask = over_dev * side + 2 * over_side + 1
    count = lax.axis_size("dev") * side
    return lax.ppermute(block, ("dev", "side"), [(i, i ^ mask) for i in range(count)])


def start_all(copies):
    for copy in copies:
        copy.start()


def wait_all(copies):
    for copy in copies:
        copy.wait()


def half_copies(which, q_hbm, kv_hbm, new_hbm, q_ref, kv, new_ref, sems, kv_sems):
    _, _, span = kv.shape
    share = span // 2
    whole = kv_hbm.shape[2] // 2
    keys = pl.ds(pl.multiple_of(which * share, share), share)
    values = pl.ds(pl.multiple_of(whole + which * share, share), share)
    span_q = q_ref.shape[1]
    small = [
        pltpu.make_async_copy(
            q_hbm.at[:, pl.ds(pl.multiple_of(which * span_q, span_q), span_q)],
            q_ref,
            sems.at[0],
        ),
        pltpu.make_async_copy(new_hbm.at[:, keys], new_ref.at[:, :share], sems.at[1]),
        pltpu.make_async_copy(new_hbm.at[:, values], new_ref.at[:, share:], sems.at[2]),
    ]
    large = [
        pltpu.make_async_copy(kv_hbm.at[:, :, keys], kv.at[:, :, :share], kv_sems.at[0]),
        pltpu.make_async_copy(kv_hbm.at[:, :, values], kv.at[:, :, share:], kv_sems.at[1]),
    ]
    return small, large


def attend_heads(q_ref, kv, new_ref, lengths, flat, mixed_flat, value_wait):
    rows, cache, span = kv.shape
    share = span // 2
    kv_heads = share // HD
    heads = q_ref.shape[1] // HD
    group = heads // kv_heads
    for h in range(heads):
        flat[h * rows : (h + 1) * rows, :] = q_ref[:, h * HD : (h + 1) * HD].astype(jnp.float32)
    scaling = 1.0 / math.sqrt(HD)
    asked = [flat[pl.ds(r, heads, stride=rows), :] for r in range(rows)]
    place = lax.broadcasted_iota(jnp.int32, (heads, cache), 1)
    fresh = new_ref[...].astype(jnp.float32)

    def spread(r, start):
        pieces = [
            jnp.broadcast_to(
                fresh[r : r + 1, start + g * HD : start + (g + 1) * HD], (group, HD)
            )
            for g in range(kv_heads)
        ]
        return jnp.concatenate(pieces, axis=0)

    all_scores = []
    for r in range(rows):
        q = asked[r].astype(jnp.bfloat16)
        all_scores.append(
            jnp.concatenate(
                [
                    lax.dot_general(
                        q[g * group : (g + 1) * group],
                        kv[r, :, g * HD : (g + 1) * HD],
                        (((1,), (1,)), ((), ())),
                        preferred_element_type=jnp.float32,
                    )
                    for g in range(kv_heads)
                ],
                axis=0,
            )
        )
    probs, own_probs = [], []
    for r in range(rows):
        own = jnp.sum(asked[r] * spread(r, 0), axis=1, keepdims=True) * scaling
        scores = jnp.where(place < lengths[r], all_scores[r] * scaling, -jnp.inf)
        peak = jnp.maximum(jnp.max(scores, axis=1, keepdims=True), own)
        weights = jnp.exp(scores - peak)
        own_weight = jnp.exp(own - peak)
        denominator = jnp.sum(weights, axis=1, keepdims=True) + own_weight
        scale = 1.0 / denominator
        probs.append((weights * scale).astype(jnp.bfloat16))
        own_probs.append((own_weight * scale).astype(jnp.bfloat16).astype(jnp.float32))
    value_wait()
    for r in range(rows):
        mixed = jnp.concatenate(
            [
                jnp.dot(
                    probs[r][g * group : (g + 1) * group],
                    kv[r, :, share + g * HD : share + (g + 1) * HD],
                    preferred_element_type=jnp.float32,
                )
                for g in range(kv_heads)
            ],
            axis=0,
        )
        mixed_flat[pl.ds(r, heads, stride=rows), :] = mixed + own_probs[r] * spread(r, share)


def put_pieces(out_ref, mixed_flat, away):
    pieces, rows, columns = out_ref.shape
    heads = columns // HD // 2
    mine = lax.axis_index("side")
    core = lax.rem(mine, 2)
    low = lax.rem(lax.div(mine, 2), pieces)
    for d in range(pieces):
        chip = jnp.bitwise_xor(low, d)
        for other in range(2):
            flips = (other + away + d.bit_count()) % 2
            first = (2 * chip + jnp.bitwise_xor(core, flips)) * heads
            for h in range(heads):
                at = pl.multiple_of((first + h) * rows, rows)
                to = (other * heads + h) * HD
                out_ref[d, :, to : to + HD] = mixed_flat[pl.ds(at, rows), :].astype(jnp.bfloat16)


def half_kernel(
    away, q_hbm, kv_hbm, new_hbm, length_hbm, out_ref, q_ref, kv, new_ref, lengths, flat,
    mixed_flat, sems, kv_sems, length_sem,
):
    here = lax.div(lax.axis_index("side"), lax.axis_size("side") // 2)
    length_copy = pltpu.make_async_copy(length_hbm, lengths, length_sem)
    small, large = half_copies(
        jnp.bitwise_xor(here, away), q_hbm, kv_hbm, new_hbm, q_ref, kv, new_ref, sems, kv_sems
    )
    start_all([*small, length_copy, *large])
    wait_all([*small, length_copy, large[0]])
    attend_heads(q_ref, kv, new_ref, lengths, flat, mixed_flat, large[1].wait)
    put_pieces(out_ref, mixed_flat, away)


def attend(queries, kv_cache, new_kv, lengths):
    rows, features = queries.shape
    chips = lax.axis_size("side") // 2
    q_half = pltpu.VMEM((rows, features // 2), queries.dtype)
    kv_half = pltpu.VMEM((*kv_cache.shape[:2], kv_cache.shape[2] // 2), kv_cache.dtype)
    new_half = pltpu.VMEM((rows, new_kv.shape[1] // 2), new_kv.dtype)
    pieces = pltpu.VMEM((chips // 2, rows, features // chips), jnp.bfloat16)
    flat = pltpu.VMEM((rows * features // 2 // HD, HD), jnp.float32)
    smem = pltpu.SMEM(lengths.shape, lengths.dtype)
    dma = pltpu.SemaphoreType.DMA
    queries, kv_cache, new_kv, lengths = in_hbm(queries, kv_cache, new_kv, lengths)

    def half(away):
        return kernel_call(
            functools.partial(half_kernel, away),
            (queries, kv_cache, new_kv, lengths),
            pieces,
            in_specs=[HBM] * 4,
            scratch=[
                q_half, kv_half, new_half, smem, flat, flat, dma((3,)), dma((2,)), dma,
            ],
            cost=pl.CostEstimate(flops=8 << 20, bytes_accessed=6 << 20, transcendentals=0),
        )

    received = across(half(1), 0, chips // 2)
    kept = half(0)
    blocks = {0: kept, chips // 2: received}
    bit = chips // 4
    while bit:
        blocks.update({d ^ bit: across(block, 0, bit) for d, block in blocks.items()})
        bit //= 2
    return [blocks[d] for d in range(chips)]


def project_kernel(*refs):
    kept_ref, sent_ref = refs[-2:]
    w_near, w_other, residual_ref, ids_ref, level_ref = refs[-7:-2]
    blocks = refs[:-7]
    rows, width = residual_ref.shape
    depth = w_near.shape[0]
    experts = lax.axis_size("dev") * lax.axis_size("side") // 2
    lhs = jnp.concatenate([ref[d % ref.shape[0]] for d, ref in enumerate(blocks)], axis=0)
    product = jnp.dot(lhs[:, :depth], w_near[...], preferred_element_type=jnp.float32) + jnp.dot(
        lhs[:, depth:], w_other[...], preferred_element_type=jnp.float32
    )
    level = level_ref[...].astype(jnp.float32)
    share = level / jnp.sum(level, axis=1, keepdims=True)
    spare = kept_ref.shape[1] - width
    lane = lax.broadcasted_iota(jnp.int32, (rows, spare), 1)
    ids = ids_ref[...]
    high, low = jnp.zeros((2, rows, spare), jnp.float32)
    for k in range(ids.shape[1]):
        chosen, part = ids[:, k : k + 1], share[:, k : k + 1]
        top = part.astype(jnp.bfloat16).astype(jnp.float32)
        high = high + jnp.where(lane == chosen, top, 0.0)
        low = low + jnp.where(lane == chosen + experts, part - top, 0.0)
    count = len(blocks)
    for d in range(count):
        here = product[d * rows : (d + 1) * rows]
        aside = jnp.zeros((rows, spare), jnp.float32)
        if d == 0:
            here = here + residual_ref[...].astype(jnp.float32)
            aside = high + low
        at = slice(d * rows, (d + 1) * rows)
        kept_ref[at, :width] = here
        kept_ref[at, width:] = aside
        at = slice((d ^ 1) * rows, ((d ^ 1) + 1) * rows)
        sent_ref[at, :width] = here.astype(jnp.bfloat16)
        sent_ref[at, width:] = aside.astype(jnp.bfloat16)


def project(blocks, w_near, w_other, residual, expert_ids, route_level):
    rows, width = residual.shape
    chips = len(blocks)
    experts = lax.axis_size("dev") * chips
    shape = (chips * rows, width + pl.cdiv(2 * experts, 128) * 128)
    kept, sent = kernel_call(
        project_kernel,
        (
            *blocks,
            pltpu.with_memory_space_constraint(w_near, pltpu.VMEM),
            pltpu.with_memory_space_constraint(w_other, pltpu.VMEM),
            residual,
            expert_ids,
            route_level,
        ),
        (jax.ShapeDtypeStruct(shape, jnp.float32), jax.ShapeDtypeStruct(shape, jnp.bfloat16)),
    )
    bit = 1
    more = across(sent, 0, bit)
    while 2 * bit < chips:
        kept = kept + more.astype(jnp.float32)
        bit *= 2
        swapped = [kept[(d ^ bit) * rows : ((d ^ bit) + 1) * rows] for d in range(chips)]
        more = across(jnp.concatenate(swapped).astype(jnp.bfloat16), 0, bit)
    return kept, sent, more


def norm_kernel(total_ref, more_ref, gain_ref, normed_ref, stream_ref):
    rows, width = stream_ref.shape
    stream = total_ref[:, :width] + more_ref[:, :width].astype(jnp.float32)
    mean_square = jnp.mean(stream * stream, axis=1, keepdims=True)
    normed = stream * lax.rsqrt(mean_square + 1e-06) * gain_ref[...]
    normed_ref[:, :width] = normed.astype(jnp.bfloat16)
    aside = total_ref[:, width:] + more_ref[:, width:].astype(jnp.float32)
    normed_ref[:, width:] = aside.astype(jnp.bfloat16)
    stream_ref[...] = stream[:rows].astype(jnp.bfloat16)


def expert_kernel(rows, *refs):
    kept_ref, sent_ref = refs[-2:]
    in_own, in_other, down_own, down_other = refs[-6:-2]
    blocks = refs[:-6]
    width = kept_ref.shape[1]
    units = down_own.shape[0]
    chips = lax.axis_size("side") // 2
    experts = lax.axis_size("dev") * chips
    mine = lax.axis_index("dev") * chips + lax.div(lax.axis_index("side"), 2)
    tokens = jnp.concatenate([ref[:, :width] for ref in blocks], axis=0)
    aside = jnp.concatenate([ref[:, width:] for ref in blocks], axis=0).astype(jnp.float32)
    lane = lax.broadcasted_iota(jnp.int32, aside.shape, 1)
    picked = jnp.where((lane == mine) | (lane == mine + experts), aside, 0.0)
    share = jnp.sum(picked, axis=1, keepdims=True)
    hidden = []
    for w_ref in (in_own, in_other):
        gate_up = jnp.dot(tokens, w_ref[...], preferred_element_type=jnp.float32)
        gate = gate_up[:, :units]
        hidden.append((gate / (1.0 + jnp.exp(-gate)) * gate_up[:, units:]).astype(jnp.bfloat16))
    result = jnp.dot(hidden[0], down_own[...], preferred_element_type=jnp.float32) + jnp.dot(
        hidden[1], down_other[...], preferred_element_type=jnp.float32
    )
    result = result * share
    count = tokens.shape[0] // (chips * rows)
    for d in range(chips):
        for i in range(count):
            start = (i * chips + d) * rows
            piece = result[start : start + rows]
            to = ((d % (chips // 2)) * count + i) * rows
            if d < chips // 2:
                kept_ref[to : to + rows, :] = piece
            else:
                sent_ref[to : to + rows, :] = piece.astype(jnp.bfloat16)


def run_experts(blocks, weights, rows, width):
    shape = (sum(block.shape[0] for block in blocks) // 2, width)
    return kernel_call(
        functools.partial(expert_kernel, rows),
        (*blocks, *weights),
        (jax.ShapeDtypeStruct(shape, jnp.float32), jax.ShapeDtypeStruct(shape, jnp.bfloat16)),
        cost=pl.CostEstimate(flops=1 << 30, bytes_accessed=4 << 20, transcendentals=0),
    )


def merge_kernel(kept_ref, more_ref, *out_refs):
    total = kept_ref[...] + more_ref[...].astype(jnp.float32)
    start = 0
    for ref in out_refs:
        ref[...] = total[start : start + ref.shape[0]].astype(ref.dtype)
        start += ref.shape[0]


def merge(kept, more, pieces):
    outs = tuple(jax.ShapeDtypeStruct((rows, kept.shape[1]), dtype) for rows, dtype in pieces)
    return kernel_call(merge_kernel, (kept, more), outs)


def homeward(kept, sent, aways, rows):
    bit = lax.axis_size("side") // 4
    while bit:
        more = across(sent, 0, bit)
        half = kept.shape[0] // 2
        pieces = ((half, jnp.float32), (half, jnp.bfloat16))
        kept, sent = merge(kept, more, pieces)
        bit //= 2
    more = across(sent, 1, 0)
    pieces = tuple((rows, jnp.bfloat16 if away else jnp.float32) for away in aways)
    return merge(kept, more, pieces)


def dev_groups(devs):
    far = list(range(devs - 2, 0, -2))
    middle = len(far) // 2
    return [0] + far[:middle], far[middle:]


def body(
    queries,
    kv_cache,
    new_kv,
    lengths,
    residual,
    w_out,
    norm_gain,
    expert_ids,
    route_level,
    w_in,
    w_down,
):
    rows, width = residual.shape
    devs = lax.axis_size("dev")

    w_other = partner(w_out, "side", 1)
    in_other = partner(w_in[0], "side", 1)
    down_other = partner(w_down[0], "side", 1)
    blocks = attend(queries, kv_cache, new_kv, lengths)
    total, sent, more = project(blocks, w_out, w_other, residual, expert_ids, route_level)
    weights = [
        pltpu.with_memory_space_constraint(x, pltpu.VMEM)
        for x in (w_in[0], in_other, w_down[0], down_other)
    ]
    normed, stream = kernel_call(
        norm_kernel,
        (total, more, norm_gain.reshape(1, width)),
        (
            jax.ShapeDtypeStruct(total.shape, jnp.bfloat16),
            pltpu.VMEM((rows, width), jnp.bfloat16),
        ),
    )

    early, late = dev_groups(devs)
    near = {0: normed}
    for away in early + late:
        if away:
            near[away] = across(normed, away, 0)
    home = []
    for aways in (early, late):
        blocks = [near[away] for away in aways]
        blocks += [across(near[away], 1, 0) for away in aways]
        kept, sent = run_experts(blocks, weights, rows, width)
        for away, block in zip(aways, homeward(kept, sent, aways, rows)):
            if away:
                block = across(block, away, 0).astype(jnp.float32)
            home.append(block)
    expert_sum = functools.reduce(jnp.add, home)
    return (stream, expert_sum.astype(jnp.bfloat16))


def solution(mesh):
    by_request = ("groups", "dev", "side")
    return jax.shard_map(
        body,
        mesh=mesh,
        in_specs=(
            P(by_request, None),
            P(by_request, None, None),
            P(by_request, None),
            P(by_request),
            P(by_request, None),
            P("side", None),
            P(),
            P(by_request, None),
            P(by_request, None),
            P(("dev", "side"), None, None),
            P(("dev", "side"), None, None),
        ),
        out_specs=(P(by_request, None), P(by_request, None)),
        check_vma=False,
    )
```

```python
import functools
import math

import jax
import jax.numpy as jnp
from jax import lax
from jax.experimental import pallas as pl
from jax.experimental.pallas import tpu as pltpu
from jax.sharding import PartitionSpec as P

HD = 128
GRANT = 16 << 20
VMEM = pl.BlockSpec(memory_space=pltpu.VMEM)
HBM = pl.BlockSpec(memory_space=pltpu.HBM)


def kernel_call(body, operands, outs, in_specs=None, scratch=(), cost=None):
    return pl.pallas_call(
        body,
        out_shape=outs,
        in_specs=in_specs or [VMEM] * len(operands),
        out_specs=jax.tree.map(lambda _: VMEM, outs, is_leaf=lambda x: hasattr(x, "shape")),
        scratch_shapes=list(scratch),
        compiler_params=pltpu.CompilerParams(vmem_limit_bytes=GRANT),
        cost_estimate=cost,
    )(*operands)


def in_hbm(*arrays):
    return [pltpu.with_memory_space_constraint(x, pltpu.HBM) for x in arrays]


def partner(block, axis, mask):
    count = lax.axis_size(axis)
    return lax.ppermute(block, axis, [(i, i ^ mask) for i in range(count)])


def across(block, over_dev, over_side):
    side = lax.axis_size("side")
    mask = over_dev * side + 2 * over_side + 1
    count = lax.axis_size("dev") * side
    return lax.ppermute(block, ("dev", "side"), [(i, i ^ mask) for i in range(count)])


def device_class(dev, member):
    ones = dev & 1
    for bit in range((lax.axis_size("side") - 1).bit_length()):
        ones = ones + ((member >> bit) & 1)
    return ones & 1


def apart(block, distances):
    devs, side = lax.axis_size("dev"), lax.axis_size("side")
    route = []
    for dev in range(devs):
        for member in range(side):
            over_dev, over_side = distances[device_class(dev, member)]
            here = dev * side + member
            route.append((here, here ^ (over_dev * side + 2 * over_side + 1)))
    return lax.ppermute(block, ("dev", "side"), route)


def start_all(copies):
    for copy in copies:
        copy.start()


def wait_all(copies):
    for copy in copies:
        copy.wait()


def half_copies(which, q_hbm, kv_hbm, new_hbm, q_ref, kv, new_ref, sems, kv_sems):
    _, _, span = kv.shape
    share = span // 2
    whole = kv_hbm.shape[2] // 2
    keys = pl.ds(pl.multiple_of(which * share, share), share)
    values = pl.ds(pl.multiple_of(whole + which * share, share), share)
    span_q = q_ref.shape[1]
    small = [
        pltpu.make_async_copy(
            q_hbm.at[:, pl.ds(pl.multiple_of(which * span_q, span_q), span_q)],
            q_ref,
            sems.at[0],
        ),
        pltpu.make_async_copy(new_hbm.at[:, keys], new_ref.at[:, :share], sems.at[1]),
        pltpu.make_async_copy(new_hbm.at[:, values], new_ref.at[:, share:], sems.at[2]),
    ]
    large = [
        pltpu.make_async_copy(kv_hbm.at[:, :, keys], kv.at[:, :, :share], kv_sems.at[0]),
        pltpu.make_async_copy(kv_hbm.at[:, :, values], kv.at[:, :, share:], kv_sems.at[1]),
    ]
    return small, large


def attend_heads(q_ref, kv, new_ref, lengths, flat, mixed_flat, value_wait):
    rows, cache, span = kv.shape
    share = span // 2
    kv_heads = share // HD
    heads = q_ref.shape[1] // HD
    group = heads // kv_heads
    for h in range(heads):
        flat[h * rows : (h + 1) * rows, :] = q_ref[:, h * HD : (h + 1) * HD].astype(jnp.float32)
    scaling = 1.0 / math.sqrt(HD)
    asked = [flat[pl.ds(r, heads, stride=rows), :] for r in range(rows)]
    place = lax.broadcasted_iota(jnp.int32, (heads, cache), 1)
    fresh = new_ref[...].astype(jnp.float32)

    def spread(r, start):
        pieces = [
            jnp.broadcast_to(
                fresh[r : r + 1, start + g * HD : start + (g + 1) * HD], (group, HD)
            )
            for g in range(kv_heads)
        ]
        return jnp.concatenate(pieces, axis=0)

    all_scores = []
    for r in range(rows):
        q = asked[r].astype(jnp.bfloat16)
        all_scores.append(
            jnp.concatenate(
                [
                    lax.dot_general(
                        q[g * group : (g + 1) * group],
                        kv[r, :, g * HD : (g + 1) * HD],
                        (((1,), (1,)), ((), ())),
                        preferred_element_type=jnp.float32,
                    )
                    for g in range(kv_heads)
                ],
                axis=0,
            )
        )
    probs, own_probs = [], []
    for r in range(rows):
        own = jnp.sum(asked[r] * spread(r, 0), axis=1, keepdims=True) * scaling
        scores = jnp.where(place < lengths[r], all_scores[r] * scaling, -jnp.inf)
        peak = jnp.maximum(jnp.max(scores, axis=1, keepdims=True), own)
        weights = jnp.exp(scores - peak)
        own_weight = jnp.exp(own - peak)
        denominator = jnp.sum(weights, axis=1, keepdims=True) + own_weight
        scale = 1.0 / denominator
        probs.append((weights * scale).astype(jnp.bfloat16))
        own_probs.append((own_weight * scale).astype(jnp.bfloat16).astype(jnp.float32))
    value_wait()
    for r in range(rows):
        mixed = jnp.concatenate(
            [
                jnp.dot(
                    probs[r][g * group : (g + 1) * group],
                    kv[r, :, share + g * HD : share + (g + 1) * HD],
                    preferred_element_type=jnp.float32,
                )
                for g in range(kv_heads)
            ],
            axis=0,
        )
        mixed_flat[pl.ds(r, heads, stride=rows), :] = mixed + own_probs[r] * spread(r, share)


def put_pieces(out_ref, mixed_flat, away):
    pieces, rows, columns = out_ref.shape
    heads = columns // HD // 2
    mine = lax.axis_index("side")
    core = lax.rem(mine, 2)
    low = lax.rem(lax.div(mine, 2), pieces)
    for d in range(pieces):
        chip = jnp.bitwise_xor(low, d)
        for other in range(2):
            flips = (other + away + d.bit_count()) % 2
            first = (2 * chip + jnp.bitwise_xor(core, flips)) * heads
            for h in range(heads):
                at = pl.multiple_of((first + h) * rows, rows)
                to = (other * heads + h) * HD
                out_ref[d, :, to : to + HD] = mixed_flat[pl.ds(at, rows), :].astype(jnp.bfloat16)


def half_kernel(
    away, q_hbm, kv_hbm, new_hbm, length_hbm, out_ref, q_ref, kv, new_ref, lengths, flat,
    mixed_flat, sems, kv_sems, length_sem,
):
    here = lax.div(lax.axis_index("side"), lax.axis_size("side") // 2)
    length_copy = pltpu.make_async_copy(length_hbm, lengths, length_sem)
    small, large = half_copies(
        jnp.bitwise_xor(here, away), q_hbm, kv_hbm, new_hbm, q_ref, kv, new_ref, sems, kv_sems
    )
    start_all([*small, length_copy, *large])
    wait_all([*small, length_copy, large[0]])
    attend_heads(q_ref, kv, new_ref, lengths, flat, mixed_flat, large[1].wait)
    put_pieces(out_ref, mixed_flat, away)


def attend(queries, kv_cache, new_kv, lengths):
    rows, features = queries.shape
    chips = lax.axis_size("side") // 2
    q_half = pltpu.VMEM((rows, features // 2), queries.dtype)
    kv_half = pltpu.VMEM((*kv_cache.shape[:2], kv_cache.shape[2] // 2), kv_cache.dtype)
    new_half = pltpu.VMEM((rows, new_kv.shape[1] // 2), new_kv.dtype)
    pieces = pltpu.VMEM((chips // 2, rows, features // chips), jnp.bfloat16)
    flat = pltpu.VMEM((rows * features // 2 // HD, HD), jnp.float32)
    smem = pltpu.SMEM(lengths.shape, lengths.dtype)
    dma = pltpu.SemaphoreType.DMA
    queries, kv_cache, new_kv, lengths = in_hbm(queries, kv_cache, new_kv, lengths)

    def half(away):
        return kernel_call(
            functools.partial(half_kernel, away),
            (queries, kv_cache, new_kv, lengths),
            pieces,
            in_specs=[HBM] * 4,
            scratch=[
                q_half, kv_half, new_half, smem, flat, flat, dma((3,)), dma((2,)), dma,
            ],
            cost=pl.CostEstimate(flops=8 << 20, bytes_accessed=6 << 20, transcendentals=0),
        )

    received = across(half(1), 0, chips // 2)
    kept = half(0)
    blocks = {0: kept, chips // 2: received}
    bit = chips // 4
    while bit:
        blocks.update({d ^ bit: across(block, 0, bit) for d, block in blocks.items()})
        bit //= 2
    return [blocks[d] for d in range(chips)]


def project_kernel(*refs):
    kept_ref, sent_ref = refs[-2:]
    w_near, w_other, residual_ref, ids_ref, level_ref = refs[-7:-2]
    blocks = refs[:-7]
    rows, width = residual_ref.shape
    depth = w_near.shape[0]
    experts = lax.axis_size("dev") * lax.axis_size("side") // 2
    lhs = jnp.concatenate([ref[d % ref.shape[0]] for d, ref in enumerate(blocks)], axis=0)
    product = jnp.dot(lhs[:, :depth], w_near[...], preferred_element_type=jnp.float32) + jnp.dot(
        lhs[:, depth:], w_other[...], preferred_element_type=jnp.float32
    )
    level = level_ref[...].astype(jnp.float32)
    share = level / jnp.sum(level, axis=1, keepdims=True)
    spare = kept_ref.shape[1] - width
    lane = lax.broadcasted_iota(jnp.int32, (rows, spare), 1)
    ids = ids_ref[...]
    high, low = jnp.zeros((2, rows, spare), jnp.float32)
    for k in range(ids.shape[1]):
        chosen, part = ids[:, k : k + 1], share[:, k : k + 1]
        top = part.astype(jnp.bfloat16).astype(jnp.float32)
        high = high + jnp.where(lane == chosen, top, 0.0)
        low = low + jnp.where(lane == chosen + experts, part - top, 0.0)
    count = len(blocks)
    for d in range(count):
        here = product[d * rows : (d + 1) * rows]
        aside = jnp.zeros((rows, spare), jnp.float32)
        if d == 0:
            here = here + residual_ref[...].astype(jnp.float32)
            aside = high + low
        at = slice(d * rows, (d + 1) * rows)
        kept_ref[at, :width] = here
        kept_ref[at, width:] = aside
        at = slice((d ^ 1) * rows, ((d ^ 1) + 1) * rows)
        sent_ref[at, :width] = here.astype(jnp.bfloat16)
        sent_ref[at, width:] = aside.astype(jnp.bfloat16)


def project(blocks, w_near, w_other, residual, expert_ids, route_level):
    rows, width = residual.shape
    chips = len(blocks)
    experts = lax.axis_size("dev") * chips
    shape = (chips * rows, width + pl.cdiv(2 * experts, 128) * 128)
    kept, sent = kernel_call(
        project_kernel,
        (
            *blocks,
            pltpu.with_memory_space_constraint(w_near, pltpu.VMEM),
            pltpu.with_memory_space_constraint(w_other, pltpu.VMEM),
            residual,
            expert_ids,
            route_level,
        ),
        (jax.ShapeDtypeStruct(shape, jnp.float32), jax.ShapeDtypeStruct(shape, jnp.bfloat16)),
    )
    bit = 1
    more = across(sent, 0, bit)
    while 2 * bit < chips:
        kept = kept + more.astype(jnp.float32)
        bit *= 2
        swapped = [kept[(d ^ bit) * rows : ((d ^ bit) + 1) * rows] for d in range(chips)]
        more = across(jnp.concatenate(swapped).astype(jnp.bfloat16), 0, bit)
    return kept, sent, more


def norm_kernel(total_ref, more_ref, gain_ref, normed_ref, stream_ref):
    rows, width = stream_ref.shape
    stream = total_ref[:, :width] + more_ref[:, :width].astype(jnp.float32)
    mean_square = jnp.mean(stream * stream, axis=1, keepdims=True)
    normed = stream * lax.rsqrt(mean_square + 1e-06) * gain_ref[...]
    normed_ref[:, :width] = normed.astype(jnp.bfloat16)
    aside = total_ref[:, width:] + more_ref[:, width:].astype(jnp.float32)
    normed_ref[:, width:] = aside.astype(jnp.bfloat16)
    stream_ref[...] = stream[:rows].astype(jnp.bfloat16)


def expert_kernel(rows, *refs):
    kept_ref, sent_ref, result = refs[-3:]
    in_own, in_other, down_own, down_other = refs[-7:-3]
    blocks = refs[:-7]
    width = kept_ref.shape[1]
    units = down_own.shape[0]
    chips = lax.axis_size("side") // 2
    experts = lax.axis_size("dev") * chips
    mine = lax.axis_index("dev") * chips + lax.div(lax.axis_index("side"), 2)
    tokens = jnp.concatenate([ref[:, :width] for ref in blocks], axis=0)
    aside = jnp.concatenate([ref[:, width:] for ref in blocks], axis=0).astype(jnp.float32)
    lane = lax.broadcasted_iota(jnp.int32, aside.shape, 1)
    picked = jnp.where((lane == mine) | (lane == mine + experts), aside, 0.0)
    share = jnp.sum(picked, axis=1, keepdims=True)
    hidden = []
    for w_ref in (in_own, in_other):
        gate_up = jnp.dot(tokens, w_ref[...], preferred_element_type=jnp.float32)
        gate = gate_up[:, :units]
        hidden.append((gate / (1.0 + jnp.exp(-gate)) * gate_up[:, units:]).astype(jnp.bfloat16))
    total = jnp.dot(hidden[0], down_own[...], preferred_element_type=jnp.float32) + jnp.dot(
        hidden[1], down_other[...], preferred_element_type=jnp.float32
    )
    result[...] = total * share
    kind = device_class(lax.axis_index("dev"), lax.axis_index("side"))
    nearby = len(blocks) // 2
    slots = 2 * nearby * chips
    for slot in range(slots):
        index, upper = slot % nearby, slot // nearby
        starts = []
        for chip, far in ((upper // 2, upper % 2), (upper % chips, upper // chips)):
            starts.append(((far * nearby + index) * chips + chip) * rows)
        start = pl.multiple_of(jnp.where(kind == 0, starts[0], starts[1]), rows)
        piece = result[pl.ds(start, rows), :]
        to = slot % (slots // 2) * rows
        if slot < slots // 2:
            kept_ref[to : to + rows, :] = piece
        else:
            sent_ref[to : to + rows, :] = piece.astype(jnp.bfloat16)


def run_experts(blocks, weights, rows, width):
    count = sum(block.shape[0] for block in blocks)
    shape = (count // 2, width)
    return kernel_call(
        functools.partial(expert_kernel, rows),
        (*blocks, *weights),
        (jax.ShapeDtypeStruct(shape, jnp.float32), jax.ShapeDtypeStruct(shape, jnp.bfloat16)),
        scratch=[pltpu.VMEM((count, width), jnp.float32)],
        cost=pl.CostEstimate(flops=1 << 30, bytes_accessed=4 << 20, transcendentals=0),
    )


def merge_kernel(kept_ref, more_ref, *out_refs):
    total = kept_ref[...] + more_ref[...].astype(jnp.float32)
    start = 0
    for ref in out_refs:
        ref[...] = total[start : start + ref.shape[0]].astype(ref.dtype)
        start += ref.shape[0]


def merge(kept, more, pieces):
    outs = tuple(jax.ShapeDtypeStruct((rows, kept.shape[1]), dtype) for rows, dtype in pieces)
    return kernel_call(merge_kernel, (kept, more), outs)


def homeward(kept, sent, aways, rows):
    over_side = []
    chips = lax.axis_size("side") // 2
    while chips > 1:
        chips //= 2
        over_side.append((0, chips))
    first, second = over_side + [(1, 0)], [(1, 0)] + over_side
    for step, distances in enumerate(zip(first, second)):
        more = apart(sent, distances)
        half = kept.shape[0] // 2
        pieces = ((half, jnp.float32), (half, jnp.bfloat16))
        if step + 1 == len(first):
            pieces = tuple((rows, jnp.bfloat16 if away else jnp.float32) for away in aways)
        parts = merge(kept, more, pieces)
        kept, sent = parts[0], parts[-1]
    return parts


def dev_groups(devs):
    far = list(range(devs - 2, 0, -2))
    middle = len(far) // 2
    return [0] + far[:middle], far[middle:]


def body(
    queries,
    kv_cache,
    new_kv,
    lengths,
    residual,
    w_out,
    norm_gain,
    expert_ids,
    route_level,
    w_in,
    w_down,
):
    rows, width = residual.shape
    devs = lax.axis_size("dev")

    w_other = partner(w_out, "side", 1)
    in_other = partner(w_in[0], "side", 1)
    down_other = partner(w_down[0], "side", 1)
    blocks = attend(queries, kv_cache, new_kv, lengths)
    total, sent, more = project(blocks, w_out, w_other, residual, expert_ids, route_level)
    weights = [
        pltpu.with_memory_space_constraint(x, pltpu.VMEM)
        for x in (w_in[0], in_other, w_down[0], down_other)
    ]
    normed, stream = kernel_call(
        norm_kernel,
        (total, more, norm_gain.reshape(1, width)),
        (
            jax.ShapeDtypeStruct(total.shape, jnp.bfloat16),
            pltpu.VMEM((rows, width), jnp.bfloat16),
        ),
    )

    early, late = dev_groups(devs)
    near = {0: normed}
    for away in early + late:
        if away:
            near[away] = across(normed, away, 0)
    home = []
    for aways in (early, late):
        blocks = [near[away] for away in aways]
        blocks += [across(near[away], 1, 0) for away in aways]
        kept, sent = run_experts(blocks, weights, rows, width)
        for away, block in zip(aways, homeward(kept, sent, aways, rows)):
            if away:
                block = across(block, away, 0).astype(jnp.float32)
            home.append(block)
    expert_sum = functools.reduce(jnp.add, home)
    return (stream, expert_sum.astype(jnp.bfloat16))


def solution(mesh):
    by_request = ("groups", "dev", "side")
    return jax.shard_map(
        body,
        mesh=mesh,
        in_specs=(
            P(by_request, None),
            P(by_request, None, None),
            P(by_request, None),
            P(by_request),
            P(by_request, None),
            P("side", None),
            P(),
            P(by_request, None),
            P(by_request, None),
            P(("dev", "side"), None, None),
            P(("dev", "side"), None, None),
        ),
        out_specs=(P(by_request, None), P(by_request, None)),
        check_vma=False,
    )
```

```python
import functools
import math

import jax
import jax.numpy as jnp
from jax import lax
from jax.experimental import pallas as pl
from jax.experimental.pallas import tpu as pltpu
from jax.sharding import PartitionSpec as P

HD = 128
GRANT = 16 << 20
VMEM = pl.BlockSpec(memory_space=pltpu.VMEM)
HBM = pl.BlockSpec(memory_space=pltpu.HBM)


def kernel_call(body, operands, outs, in_specs=None, scratch=(), cost=None):
    return pl.pallas_call(
        body,
        out_shape=outs,
        in_specs=in_specs or [VMEM] * len(operands),
        out_specs=jax.tree.map(lambda _: VMEM, outs, is_leaf=lambda x: hasattr(x, "shape")),
        scratch_shapes=list(scratch),
        compiler_params=pltpu.CompilerParams(vmem_limit_bytes=GRANT),
        cost_estimate=cost,
    )(*operands)


def in_hbm(*arrays):
    return [pltpu.with_memory_space_constraint(x, pltpu.HBM) for x in arrays]


def partner(block, axis, mask):
    count = lax.axis_size(axis)
    return lax.ppermute(block, axis, [(i, i ^ mask) for i in range(count)])


def across(block, over_dev, over_side):
    side = lax.axis_size("side")
    mask = over_dev * side + 2 * over_side + 1
    count = lax.axis_size("dev") * side
    return lax.ppermute(block, ("dev", "side"), [(i, i ^ mask) for i in range(count)])


def device_class(dev, member):
    ones = dev & 1
    for bit in range((lax.axis_size("side") - 1).bit_length()):
        ones = ones + ((member >> bit) & 1)
    return ones & 1


def apart(block, distances):
    devs, side = lax.axis_size("dev"), lax.axis_size("side")
    route = []
    for dev in range(devs):
        for member in range(side):
            over_dev, over_side = distances[device_class(dev, member)]
            here = dev * side + member
            route.append((here, here ^ (over_dev * side + 2 * over_side + 1)))
    return lax.ppermute(block, ("dev", "side"), route)


def start_all(copies):
    for copy in copies:
        copy.start()


def wait_all(copies):
    for copy in copies:
        copy.wait()


def half_copies(which, q_hbm, kv_hbm, new_hbm, q_ref, kv, new_ref, sems, kv_sems):
    _, _, span = kv.shape
    share = span // 2
    whole = kv_hbm.shape[2] // 2
    keys = pl.ds(pl.multiple_of(which * share, share), share)
    values = pl.ds(pl.multiple_of(whole + which * share, share), share)
    span_q = q_ref.shape[1]
    small = [
        pltpu.make_async_copy(
            q_hbm.at[:, pl.ds(pl.multiple_of(which * span_q, span_q), span_q)],
            q_ref,
            sems.at[0],
        ),
        pltpu.make_async_copy(new_hbm.at[:, keys], new_ref.at[:, :share], sems.at[1]),
        pltpu.make_async_copy(new_hbm.at[:, values], new_ref.at[:, share:], sems.at[2]),
    ]
    large = [
        pltpu.make_async_copy(kv_hbm.at[:, :, keys], kv.at[:, :, :share], kv_sems.at[0]),
        pltpu.make_async_copy(kv_hbm.at[:, :, values], kv.at[:, :, share:], kv_sems.at[1]),
    ]
    return small, large


def attend_heads(q_ref, kv, new_ref, lengths, flat, mixed_flat, value_wait):
    rows, cache, span = kv.shape
    share = span // 2
    kv_heads = share // HD
    heads = q_ref.shape[1] // HD
    group = heads // kv_heads
    for h in range(heads):
        flat[h * rows : (h + 1) * rows, :] = q_ref[:, h * HD : (h + 1) * HD].astype(jnp.float32)
    scaling = 1.0 / math.sqrt(HD)
    asked = [flat[pl.ds(r, heads, stride=rows), :] for r in range(rows)]
    place = lax.broadcasted_iota(jnp.int32, (heads, cache), 1)
    fresh = new_ref[...].astype(jnp.float32)

    def spread(r, start):
        pieces = [
            jnp.broadcast_to(
                fresh[r : r + 1, start + g * HD : start + (g + 1) * HD], (group, HD)
            )
            for g in range(kv_heads)
        ]
        return jnp.concatenate(pieces, axis=0)

    all_scores = []
    for r in range(rows):
        q = asked[r].astype(jnp.bfloat16)
        all_scores.append(
            jnp.concatenate(
                [
                    lax.dot_general(
                        q[g * group : (g + 1) * group],
                        kv[r, :, g * HD : (g + 1) * HD],
                        (((1,), (1,)), ((), ())),
                        preferred_element_type=jnp.float32,
                    )
                    for g in range(kv_heads)
                ],
                axis=0,
            )
        )
    probs, own_probs = [], []
    for r in range(rows):
        own = jnp.sum(asked[r] * spread(r, 0), axis=1, keepdims=True) * scaling
        scores = jnp.where(place < lengths[r], all_scores[r] * scaling, -jnp.inf)
        peak = jnp.maximum(jnp.max(scores, axis=1, keepdims=True), own)
        weights = jnp.exp(scores - peak)
        own_weight = jnp.exp(own - peak)
        denominator = jnp.sum(weights, axis=1, keepdims=True) + own_weight
        scale = 1.0 / denominator
        probs.append((weights * scale).astype(jnp.bfloat16))
        own_probs.append((own_weight * scale).astype(jnp.bfloat16).astype(jnp.float32))
    value_wait()
    for r in range(rows):
        mixed = jnp.concatenate(
            [
                jnp.dot(
                    probs[r][g * group : (g + 1) * group],
                    kv[r, :, share + g * HD : share + (g + 1) * HD],
                    preferred_element_type=jnp.float32,
                )
                for g in range(kv_heads)
            ],
            axis=0,
        )
        mixed_flat[pl.ds(r, heads, stride=rows), :] = mixed + own_probs[r] * spread(r, share)


def put_pieces(out_ref, mixed_flat, away):
    pieces, rows, columns = out_ref.shape
    heads = columns // HD // 2
    mine = lax.axis_index("side")
    core = lax.rem(mine, 2)
    low = lax.rem(lax.div(mine, 2), pieces)
    for d in range(pieces):
        chip = jnp.bitwise_xor(low, d)
        for other in range(2):
            flips = (other + away + d.bit_count()) % 2
            first = (2 * chip + jnp.bitwise_xor(core, flips)) * heads
            for h in range(heads):
                at = pl.multiple_of((first + h) * rows, rows)
                to = (other * heads + h) * HD
                out_ref[d, :, to : to + HD] = mixed_flat[pl.ds(at, rows), :].astype(jnp.bfloat16)


def half_kernel(
    away, q_hbm, kv_hbm, new_hbm, length_hbm, out_ref, q_ref, kv, new_ref, lengths, flat,
    mixed_flat, sems, kv_sems, length_sem,
):
    here = lax.div(lax.axis_index("side"), lax.axis_size("side") // 2)
    length_copy = pltpu.make_async_copy(length_hbm, lengths, length_sem)
    small, large = half_copies(
        jnp.bitwise_xor(here, away), q_hbm, kv_hbm, new_hbm, q_ref, kv, new_ref, sems, kv_sems
    )
    start_all([*small, length_copy, *large])
    wait_all([*small, length_copy, large[0]])
    attend_heads(q_ref, kv, new_ref, lengths, flat, mixed_flat, large[1].wait)
    put_pieces(out_ref, mixed_flat, away)


def attend(queries, kv_cache, new_kv, lengths):
    rows, features = queries.shape
    chips = lax.axis_size("side") // 2
    q_half = pltpu.VMEM((rows, features // 2), queries.dtype)
    kv_half = pltpu.VMEM((*kv_cache.shape[:2], kv_cache.shape[2] // 2), kv_cache.dtype)
    new_half = pltpu.VMEM((rows, new_kv.shape[1] // 2), new_kv.dtype)
    pieces = pltpu.VMEM((chips // 2, rows, features // chips), jnp.bfloat16)
    flat = pltpu.VMEM((rows * features // 2 // HD, HD), jnp.float32)
    smem = pltpu.SMEM(lengths.shape, lengths.dtype)
    dma = pltpu.SemaphoreType.DMA
    queries, kv_cache, new_kv, lengths = in_hbm(queries, kv_cache, new_kv, lengths)

    def half(away):
        return kernel_call(
            functools.partial(half_kernel, away),
            (queries, kv_cache, new_kv, lengths),
            pieces,
            in_specs=[HBM] * 4,
            scratch=[
                q_half, kv_half, new_half, smem, flat, flat, dma((3,)), dma((2,)), dma,
            ],
            cost=pl.CostEstimate(flops=8 << 20, bytes_accessed=6 << 20, transcendentals=0),
        )

    received = across(half(1), 0, chips // 2)
    kept = half(0)
    blocks = {0: kept, chips // 2: received}
    bit = chips // 4
    while bit:
        blocks.update({d ^ bit: across(block, 0, bit) for d, block in blocks.items()})
        bit //= 2
    return [blocks[d] for d in range(chips)]


def project_kernel(*refs):
    kept_ref, sent_ref = refs[-2:]
    w_near, w_other, residual_ref, ids_ref, level_ref = refs[-7:-2]
    blocks = refs[:-7]
    rows, width = residual_ref.shape
    depth = w_near.shape[0]
    experts = lax.axis_size("dev") * lax.axis_size("side") // 2
    lhs = jnp.concatenate([ref[d % ref.shape[0]] for d, ref in enumerate(blocks)], axis=0)
    product = jnp.dot(lhs[:, :depth], w_near[...], preferred_element_type=jnp.float32) + jnp.dot(
        lhs[:, depth:], w_other[...], preferred_element_type=jnp.float32
    )
    level = level_ref[...].astype(jnp.float32)
    share = level / jnp.sum(level, axis=1, keepdims=True)
    spare = kept_ref.shape[1] - width
    lane = lax.broadcasted_iota(jnp.int32, (rows, spare), 1)
    ids = ids_ref[...]
    high, low = jnp.zeros((2, rows, spare), jnp.float32)
    for k in range(ids.shape[1]):
        chosen, part = ids[:, k : k + 1], share[:, k : k + 1]
        top = part.astype(jnp.bfloat16).astype(jnp.float32)
        high = high + jnp.where(lane == chosen, top, 0.0)
        low = low + jnp.where(lane == chosen + experts, part - top, 0.0)
    count = len(blocks)
    for d in range(count):
        here = product[d * rows : (d + 1) * rows]
        aside = jnp.zeros((rows, spare), jnp.float32)
        if d == 0:
            here = here + residual_ref[...].astype(jnp.float32)
            aside = high + low
        at = slice(d * rows, (d + 1) * rows)
        kept_ref[at, :width] = here
        kept_ref[at, width:] = aside
        at = slice((d ^ 1) * rows, ((d ^ 1) + 1) * rows)
        sent_ref[at, :width] = here.astype(jnp.bfloat16)
        sent_ref[at, width:] = aside.astype(jnp.bfloat16)


def project(blocks, w_near, w_other, residual, expert_ids, route_level):
    rows, width = residual.shape
    chips = len(blocks)
    experts = lax.axis_size("dev") * chips
    shape = (chips * rows, width + pl.cdiv(2 * experts, 128) * 128)
    kept, sent = kernel_call(
        project_kernel,
        (
            *blocks,
            pltpu.with_memory_space_constraint(w_near, pltpu.VMEM),
            pltpu.with_memory_space_constraint(w_other, pltpu.VMEM),
            residual,
            expert_ids,
            route_level,
        ),
        (jax.ShapeDtypeStruct(shape, jnp.float32), jax.ShapeDtypeStruct(shape, jnp.bfloat16)),
    )
    bit = 1
    more = across(sent, 0, bit)
    while 2 * bit < chips:
        kept = kept + more.astype(jnp.float32)
        bit *= 2
        swapped = [kept[(d ^ bit) * rows : ((d ^ bit) + 1) * rows] for d in range(chips)]
        more = across(jnp.concatenate(swapped).astype(jnp.bfloat16), 0, bit)
    return kept, sent, more


def norm_kernel(total_ref, more_ref, gain_ref, normed_ref, stream_ref):
    rows, width = stream_ref.shape
    stream = total_ref[:, :width] + more_ref[:, :width].astype(jnp.float32)
    mean_square = jnp.mean(stream * stream, axis=1, keepdims=True)
    normed = stream * lax.rsqrt(mean_square + 1e-06) * gain_ref[...]
    normed_ref[:, :width] = normed.astype(jnp.bfloat16)
    aside = total_ref[:, width:] + more_ref[:, width:].astype(jnp.float32)
    normed_ref[:, width:] = aside.astype(jnp.bfloat16)
    stream_ref[...] = stream[:rows].astype(jnp.bfloat16)


def expert_kernel(rows, turn, *refs):
    kept_ref, sent_ref, result = refs[-3:]
    in_own, in_other, down_own, down_other = refs[-7:-3]
    blocks = refs[:-7]
    width = kept_ref.shape[1]
    units = down_own.shape[0]
    chips = lax.axis_size("side") // 2
    experts = lax.axis_size("dev") * chips
    mine = lax.axis_index("dev") * chips + lax.div(lax.axis_index("side"), 2)
    tokens = jnp.concatenate([ref[:, :width] for ref in blocks], axis=0)
    aside = jnp.concatenate([ref[:, width:] for ref in blocks], axis=0).astype(jnp.float32)
    lane = lax.broadcasted_iota(jnp.int32, aside.shape, 1)
    picked = jnp.where((lane == mine) | (lane == mine + experts), aside, 0.0)
    share = jnp.sum(picked, axis=1, keepdims=True)
    hidden = []
    for w_ref in (in_own, in_other):
        gate_up = jnp.dot(tokens, w_ref[...], preferred_element_type=jnp.float32)
        gate = gate_up[:, :units]
        hidden.append((gate / (1.0 + jnp.exp(-gate)) * gate_up[:, units:]).astype(jnp.bfloat16))
    total = jnp.dot(hidden[0], down_own[...], preferred_element_type=jnp.float32) + jnp.dot(
        hidden[1], down_other[...], preferred_element_type=jnp.float32
    )
    result[...] = total * share
    kind = device_class(lax.axis_index("dev"), lax.axis_index("side")) ^ turn
    nearby = len(blocks) // 2
    slots = 2 * nearby * chips
    for slot in range(slots):
        index, upper = slot % nearby, slot // nearby
        starts = []
        for chip, far in ((upper // 2, upper % 2), (upper % chips, upper // chips)):
            starts.append(((far * nearby + index) * chips + chip) * rows)
        start = pl.multiple_of(jnp.where(kind == 0, starts[0], starts[1]), rows)
        piece = result[pl.ds(start, rows), :]
        to = slot % (slots // 2) * rows
        if slot < slots // 2:
            kept_ref[to : to + rows, :] = piece
        else:
            sent_ref[to : to + rows, :] = piece.astype(jnp.bfloat16)


def run_experts(name, blocks, weights, rows, width):
    count = sum(block.shape[0] for block in blocks)
    shape = (count // 2, width)
    return kernel_call(
        functools.partial(expert_kernel, rows, int(name == "experts_late")),
        (*blocks, *weights),
        (jax.ShapeDtypeStruct(shape, jnp.float32), jax.ShapeDtypeStruct(shape, jnp.bfloat16)),
        scratch=[pltpu.VMEM((count, width), jnp.float32)],
        cost=pl.CostEstimate(flops=1 << 30, bytes_accessed=4 << 20, transcendentals=0),
    )


def merge_kernel(kept_ref, more_ref, *out_refs):
    total = kept_ref[...] + more_ref[...].astype(jnp.float32)
    start = 0
    for ref in out_refs:
        ref[...] = total[start : start + ref.shape[0]].astype(ref.dtype)
        start += ref.shape[0]


def merge(kept, more, pieces):
    outs = tuple(jax.ShapeDtypeStruct((rows, kept.shape[1]), dtype) for rows, dtype in pieces)
    return kernel_call(merge_kernel, (kept, more), outs)


def homeward(kept, sent, group, aways, rows):
    over_side = []
    chips = lax.axis_size("side") // 2
    while chips > 1:
        chips //= 2
        over_side.append((0, chips))
    first, second = over_side + [(1, 0)], [(1, 0)] + over_side
    if group == "late":
        first, second = second, first
    for step, distances in enumerate(zip(first, second)):
        more = apart(sent, distances)
        half = kept.shape[0] // 2
        pieces = ((half, jnp.float32), (half, jnp.bfloat16))
        if step + 1 == len(first):
            pieces = tuple((rows, jnp.bfloat16 if away else jnp.float32) for away in aways)
        parts = merge(kept, more, pieces)
        kept, sent = parts[0], parts[-1]
    return parts


def dev_groups(devs):
    far = list(range(devs - 2, 0, -2))
    middle = len(far) // 2
    return [0] + far[:middle], far[middle:]


def body(
    queries,
    kv_cache,
    new_kv,
    lengths,
    residual,
    w_out,
    norm_gain,
    expert_ids,
    route_level,
    w_in,
    w_down,
):
    rows, width = residual.shape
    devs = lax.axis_size("dev")

    w_other = partner(w_out, "side", 1)
    in_other = partner(w_in[0], "side", 1)
    down_other = partner(w_down[0], "side", 1)
    blocks = attend(queries, kv_cache, new_kv, lengths)
    total, sent, more = project(blocks, w_out, w_other, residual, expert_ids, route_level)
    weights = [
        pltpu.with_memory_space_constraint(x, pltpu.VMEM)
        for x in (w_in[0], in_other, w_down[0], down_other)
    ]
    normed, stream = kernel_call(
        norm_kernel,
        (total, more, norm_gain.reshape(1, width)),
        (
            jax.ShapeDtypeStruct(total.shape, jnp.bfloat16),
            pltpu.VMEM((rows, width), jnp.bfloat16),
        ),
    )

    early, late = dev_groups(devs)
    near = {0: normed}
    for away in early + late:
        if away:
            near[away] = across(normed, away, 0)
    home = []
    for group, aways in (("early", early), ("late", late)):
        blocks = [near[away] for away in aways]
        blocks += [across(near[away], 1, 0) for away in aways]
        kept, sent = run_experts(f"experts_{group}", blocks, weights, rows, width)
        for away, block in zip(aways, homeward(kept, sent, group, aways, rows)):
            if away:
                block = across(block, away, 0).astype(jnp.float32)
            home.append(block)
    expert_sum = functools.reduce(jnp.add, home)
    return (stream, expert_sum.astype(jnp.bfloat16))


def solution(mesh):
    by_request = ("groups", "dev", "side")
    return jax.shard_map(
        body,
        mesh=mesh,
        in_specs=(
            P(by_request, None),
            P(by_request, None, None),
            P(by_request, None),
            P(by_request),
            P(by_request, None),
            P("side", None),
            P(),
            P(by_request, None),
            P(by_request, None),
            P(("dev", "side"), None, None),
            P(("dev", "side"), None, None),
        ),
        out_specs=(P(by_request, None), P(by_request, None)),
        check_vma=False,
    )
```

```python
import functools
import math

import jax
import jax.numpy as jnp
from jax import lax
from jax.experimental import pallas as pl
from jax.experimental.pallas import tpu as pltpu
from jax.sharding import PartitionSpec as P

HD = 128
GRANT = 16 << 20
VMEM = pl.BlockSpec(memory_space=pltpu.VMEM)
HBM = pl.BlockSpec(memory_space=pltpu.HBM)


def kernel_call(body, operands, outs, in_specs=None, scratch=(), cost=None):
    return pl.pallas_call(
        body,
        out_shape=outs,
        in_specs=in_specs or [VMEM] * len(operands),
        out_specs=jax.tree.map(lambda _: VMEM, outs, is_leaf=lambda x: hasattr(x, "shape")),
        scratch_shapes=list(scratch),
        compiler_params=pltpu.CompilerParams(vmem_limit_bytes=GRANT),
        cost_estimate=cost,
    )(*operands)


def in_hbm(*arrays):
    return [pltpu.with_memory_space_constraint(x, pltpu.HBM) for x in arrays]


def partner(block, axis, mask):
    count = lax.axis_size(axis)
    return lax.ppermute(block, axis, [(i, i ^ mask) for i in range(count)])


def across(block, over_dev, over_side):
    side = lax.axis_size("side")
    mask = over_dev * side + 2 * over_side + 1
    count = lax.axis_size("dev") * side
    return lax.ppermute(block, ("dev", "side"), [(i, i ^ mask) for i in range(count)])


def device_class(dev, member):
    ones = dev & 1
    for bit in range((lax.axis_size("side") - 1).bit_length()):
        ones = ones + ((member >> bit) & 1)
    return ones & 1


def apart(block, distances):
    devs, side = lax.axis_size("dev"), lax.axis_size("side")
    route = []
    for dev in range(devs):
        for member in range(side):
            over_dev, over_side = distances[device_class(dev, member)]
            here = dev * side + member
            route.append((here, here ^ (over_dev * side + 2 * over_side + 1)))
    return lax.ppermute(block, ("dev", "side"), route)


def start_all(copies):
    for copy in copies:
        copy.start()


def wait_all(copies):
    for copy in copies:
        copy.wait()


def half_copies(which, q_hbm, kv_hbm, new_hbm, q_ref, kv, new_ref, sems, kv_sems):
    _, _, span = kv.shape
    share = span // 2
    whole = kv_hbm.shape[2] // 2
    keys = pl.ds(pl.multiple_of(which * share, share), share)
    values = pl.ds(pl.multiple_of(whole + which * share, share), share)
    span_q = q_ref.shape[1]
    small = [
        pltpu.make_async_copy(
            q_hbm.at[:, pl.ds(pl.multiple_of(which * span_q, span_q), span_q)],
            q_ref,
            sems.at[0],
        ),
        pltpu.make_async_copy(new_hbm.at[:, keys], new_ref.at[:, :share], sems.at[1]),
        pltpu.make_async_copy(new_hbm.at[:, values], new_ref.at[:, share:], sems.at[2]),
    ]
    large = [
        pltpu.make_async_copy(kv_hbm.at[:, :, keys], kv.at[:, :, :share], kv_sems.at[0]),
        pltpu.make_async_copy(kv_hbm.at[:, :, values], kv.at[:, :, share:], kv_sems.at[1]),
    ]
    return small, large


def attend_heads(q_ref, kv, new_ref, lengths, flat, mixed_flat, value_wait):
    rows, cache, span = kv.shape
    share = span // 2
    kv_heads = share // HD
    heads = q_ref.shape[1] // HD
    group = heads // kv_heads
    for h in range(heads):
        flat[h * rows : (h + 1) * rows, :] = q_ref[:, h * HD : (h + 1) * HD].astype(jnp.float32)
    scaling = 1.0 / math.sqrt(HD)
    asked = [flat[pl.ds(r, heads, stride=rows), :] for r in range(rows)]
    place = lax.broadcasted_iota(jnp.int32, (heads, cache), 1)
    fresh = new_ref[...].astype(jnp.float32)

    def spread(r, start):
        pieces = [
            jnp.broadcast_to(
                fresh[r : r + 1, start + g * HD : start + (g + 1) * HD], (group, HD)
            )
            for g in range(kv_heads)
        ]
        return jnp.concatenate(pieces, axis=0)

    all_scores = []
    for r in range(rows):
        q = asked[r].astype(jnp.bfloat16)
        all_scores.append(
            jnp.concatenate(
                [
                    lax.dot_general(
                        q[g * group : (g + 1) * group],
                        kv[r, :, g * HD : (g + 1) * HD],
                        (((1,), (1,)), ((), ())),
                        preferred_element_type=jnp.float32,
                    )
                    for g in range(kv_heads)
                ],
                axis=0,
            )
        )
    probs, own_probs = [], []
    for r in range(rows):
        own = jnp.sum(asked[r] * spread(r, 0), axis=1, keepdims=True) * scaling
        scores = jnp.where(place < lengths[r], all_scores[r] * scaling, -jnp.inf)
        peak = jnp.maximum(jnp.max(scores, axis=1, keepdims=True), own)
        weights = jnp.exp(scores - peak)
        own_weight = jnp.exp(own - peak)
        denominator = jnp.sum(weights, axis=1, keepdims=True) + own_weight
        scale = 1.0 / denominator
        probs.append((weights * scale).astype(jnp.bfloat16))
        own_probs.append((own_weight * scale).astype(jnp.bfloat16).astype(jnp.float32))
    value_wait()
    for r in range(rows):
        mixed = jnp.concatenate(
            [
                jnp.dot(
                    probs[r][g * group : (g + 1) * group],
                    kv[r, :, share + g * HD : share + (g + 1) * HD],
                    preferred_element_type=jnp.float32,
                )
                for g in range(kv_heads)
            ],
            axis=0,
        )
        mixed_flat[pl.ds(r, heads, stride=rows), :] = mixed + own_probs[r] * spread(r, share)


def put_pieces(out_ref, mixed_flat, away):
    pieces, rows, columns = out_ref.shape
    heads = columns // HD // 2
    mine = lax.axis_index("side")
    core = lax.rem(mine, 2)
    low = lax.rem(lax.div(mine, 2), pieces)
    for d in range(pieces):
        chip = jnp.bitwise_xor(low, d)
        for other in range(2):
            flips = (other + away + d.bit_count()) % 2
            first = (2 * chip + jnp.bitwise_xor(core, flips)) * heads
            for h in range(heads):
                at = pl.multiple_of((first + h) * rows, rows)
                to = (other * heads + h) * HD
                out_ref[d, :, to : to + HD] = mixed_flat[pl.ds(at, rows), :].astype(jnp.bfloat16)


def half_kernel(
    away, q_hbm, kv_hbm, new_hbm, length_hbm, out_ref, q_ref, kv, new_ref, lengths, flat,
    mixed_flat, sems, kv_sems, length_sem,
):
    here = lax.div(lax.axis_index("side"), lax.axis_size("side") // 2)
    length_copy = pltpu.make_async_copy(length_hbm, lengths, length_sem)
    small, large = half_copies(
        jnp.bitwise_xor(here, away), q_hbm, kv_hbm, new_hbm, q_ref, kv, new_ref, sems, kv_sems
    )
    start_all([*small, length_copy, *large])
    wait_all([*small, length_copy, large[0]])
    attend_heads(q_ref, kv, new_ref, lengths, flat, mixed_flat, large[1].wait)
    put_pieces(out_ref, mixed_flat, away)


def attend(queries, kv_cache, new_kv, lengths):
    rows, features = queries.shape
    chips = lax.axis_size("side") // 2
    q_half = pltpu.VMEM((rows, features // 2), queries.dtype)
    kv_half = pltpu.VMEM((*kv_cache.shape[:2], kv_cache.shape[2] // 2), kv_cache.dtype)
    new_half = pltpu.VMEM((rows, new_kv.shape[1] // 2), new_kv.dtype)
    pieces = pltpu.VMEM((chips // 2, rows, features // chips), jnp.bfloat16)
    flat = pltpu.VMEM((rows * features // 2 // HD, HD), jnp.float32)
    smem = pltpu.SMEM(lengths.shape, lengths.dtype)
    dma = pltpu.SemaphoreType.DMA
    queries, kv_cache, new_kv, lengths = in_hbm(queries, kv_cache, new_kv, lengths)

    def half(away):
        return kernel_call(
            functools.partial(half_kernel, away),
            (queries, kv_cache, new_kv, lengths),
            pieces,
            in_specs=[HBM] * 4,
            scratch=[
                q_half, kv_half, new_half, smem, flat, flat, dma((3,)), dma((2,)), dma,
            ],
            cost=pl.CostEstimate(flops=8 << 20, bytes_accessed=6 << 20, transcendentals=0),
        )

    received = across(half(1), 0, chips // 2)
    kept = half(0)
    blocks = {0: kept, chips // 2: received}
    bit = chips // 4
    while bit:
        blocks.update({d ^ bit: across(block, 0, bit) for d, block in blocks.items()})
        bit //= 2
    return [blocks[d] for d in range(chips)]


def project_kernel(*refs):
    kept_ref, sent_ref = refs[-2:]
    w_near, w_other, residual_ref, ids_ref, level_ref = refs[-7:-2]
    blocks = refs[:-7]
    rows, width = residual_ref.shape
    depth = w_near.shape[0]
    experts = lax.axis_size("dev") * lax.axis_size("side") // 2
    lhs = jnp.concatenate([ref[d % ref.shape[0]] for d, ref in enumerate(blocks)], axis=0)
    product = jnp.dot(lhs[:, :depth], w_near[...], preferred_element_type=jnp.float32) + jnp.dot(
        lhs[:, depth:], w_other[...], preferred_element_type=jnp.float32
    )
    level = level_ref[...].astype(jnp.float32)
    share = level / jnp.sum(level, axis=1, keepdims=True)
    spare = kept_ref.shape[1] - width
    lane = lax.broadcasted_iota(jnp.int32, (rows, spare), 1)
    ids = ids_ref[...]
    high, low = jnp.zeros((2, rows, spare), jnp.float32)
    for k in range(ids.shape[1]):
        chosen, part = ids[:, k : k + 1], share[:, k : k + 1]
        top = part.astype(jnp.bfloat16).astype(jnp.float32)
        high = high + jnp.where(lane == chosen, top, 0.0)
        low = low + jnp.where(lane == chosen + experts, part - top, 0.0)
    count = len(blocks)
    for d in range(count):
        here = product[d * rows : (d + 1) * rows]
        aside = jnp.zeros((rows, spare), jnp.float32)
        if d == 0:
            here = here + residual_ref[...].astype(jnp.float32)
            aside = high + low
        at = slice(d * rows, (d + 1) * rows)
        kept_ref[at, :width] = here
        kept_ref[at, width:] = aside
        at = slice((d ^ 1) * rows, ((d ^ 1) + 1) * rows)
        sent_ref[at, :width] = here.astype(jnp.bfloat16)
        sent_ref[at, width:] = aside.astype(jnp.bfloat16)


def project(blocks, w_near, w_other, residual, expert_ids, route_level):
    rows, width = residual.shape
    chips = len(blocks)
    experts = lax.axis_size("dev") * chips
    shape = (chips * rows, width + pl.cdiv(2 * experts, 128) * 128)
    kept, sent = kernel_call(
        project_kernel,
        (
            *blocks,
            pltpu.with_memory_space_constraint(w_near, pltpu.VMEM),
            pltpu.with_memory_space_constraint(w_other, pltpu.VMEM),
            residual,
            expert_ids,
            route_level,
        ),
        (jax.ShapeDtypeStruct(shape, jnp.float32), jax.ShapeDtypeStruct(shape, jnp.bfloat16)),
    )
    bit = 1
    more = across(sent, 0, bit)
    while 2 * bit < chips:
        kept = kept + more.astype(jnp.float32)
        bit *= 2
        swapped = [kept[(d ^ bit) * rows : ((d ^ bit) + 1) * rows] for d in range(chips)]
        more = across(jnp.concatenate(swapped).astype(jnp.bfloat16), 0, bit)
    return kept, sent, more


def norm_kernel(total_ref, more_ref, gain_ref, normed_ref, stream_ref):
    rows, width = stream_ref.shape
    stream = total_ref[:, :width] + more_ref[:, :width].astype(jnp.float32)
    mean_square = jnp.mean(stream * stream, axis=1, keepdims=True)
    normed = stream * lax.rsqrt(mean_square + 1e-06) * gain_ref[...]
    normed_ref[:, :width] = normed.astype(jnp.bfloat16)
    aside = total_ref[:, width:] + more_ref[:, width:].astype(jnp.float32)
    normed_ref[:, width:] = aside.astype(jnp.bfloat16)
    stream_ref[...] = stream[:rows].astype(jnp.bfloat16)


def expert_kernel(rows, turn, *refs):
    kept_ref, sent_ref = refs[-2:]
    in_own, in_other, down_own, down_other = refs[-6:-2]
    blocks = refs[:-6]
    width = kept_ref.shape[1]
    units = down_own.shape[0]
    chips = lax.axis_size("side") // 2
    experts = lax.axis_size("dev") * chips
    mine = lax.axis_index("dev") * chips + lax.div(lax.axis_index("side"), 2)
    tokens = jnp.concatenate([ref[:, :width] for ref in blocks], axis=0)
    aside = jnp.concatenate([ref[:, width:] for ref in blocks], axis=0).astype(jnp.float32)
    lane = lax.broadcasted_iota(jnp.int32, aside.shape, 1)
    picked = jnp.where((lane == mine) | (lane == mine + experts), aside, 0.0)
    share = jnp.sum(picked, axis=1, keepdims=True)
    hidden = []
    for w_ref in (in_own, in_other):
        gate_up = jnp.dot(tokens, w_ref[...], preferred_element_type=jnp.float32)
        gate = gate_up[:, :units]
        hidden.append((gate / (1.0 + jnp.exp(-gate)) * gate_up[:, units:]).astype(jnp.bfloat16))
    total = jnp.dot(hidden[0], down_own[...], preferred_element_type=jnp.float32) + jnp.dot(
        hidden[1], down_other[...], preferred_element_type=jnp.float32
    )
    total = total * share
    kind = device_class(lax.axis_index("dev"), lax.axis_index("side")) ^ turn
    nearby = len(blocks) // 2
    slots = 2 * nearby * chips
    for slot in range(slots):
        index, upper = slot % nearby, slot // nearby
        starts = []
        for chip, far in ((upper // 2, upper % 2), (upper % chips, upper // chips)):
            starts.append(((far * nearby + index) * chips + chip) * rows)
        first, second = (total[start : start + rows] for start in starts)
        piece = jnp.where(kind == 0, first, second)
        to = slot % (slots // 2) * rows
        if slot < slots // 2:
            kept_ref[to : to + rows, :] = piece
        else:
            sent_ref[to : to + rows, :] = piece.astype(jnp.bfloat16)


def run_experts(name, blocks, weights, rows, width):
    count = sum(block.shape[0] for block in blocks)
    shape = (count // 2, width)
    return kernel_call(
        functools.partial(expert_kernel, rows, int(name == "experts_late")),
        (*blocks, *weights),
        (jax.ShapeDtypeStruct(shape, jnp.float32), jax.ShapeDtypeStruct(shape, jnp.bfloat16)),
        cost=pl.CostEstimate(flops=1 << 30, bytes_accessed=4 << 20, transcendentals=0),
    )


def merge_kernel(kept_ref, more_ref, *out_refs):
    total = kept_ref[...] + more_ref[...].astype(jnp.float32)
    start = 0
    for ref in out_refs:
        ref[...] = total[start : start + ref.shape[0]].astype(ref.dtype)
        start += ref.shape[0]


def merge(kept, more, pieces):
    outs = tuple(jax.ShapeDtypeStruct((rows, kept.shape[1]), dtype) for rows, dtype in pieces)
    return kernel_call(merge_kernel, (kept, more), outs)


def homeward(kept, sent, group, aways, rows):
    over_side = []
    chips = lax.axis_size("side") // 2
    while chips > 1:
        chips //= 2
        over_side.append((0, chips))
    first, second = over_side + [(1, 0)], [(1, 0)] + over_side
    if group == "late":
        first, second = second, first
    for step, distances in enumerate(zip(first, second)):
        more = apart(sent, distances)
        half = kept.shape[0] // 2
        pieces = ((half, jnp.float32), (half, jnp.bfloat16))
        if step + 1 == len(first):
            pieces = tuple((rows, jnp.bfloat16 if away else jnp.float32) for away in aways)
        parts = merge(kept, more, pieces)
        kept, sent = parts[0], parts[-1]
    return parts


def dev_groups(devs):
    far = list(range(devs - 2, 0, -2))
    middle = len(far) // 2
    return [0] + far[:middle], far[middle:]


def body(
    queries,
    kv_cache,
    new_kv,
    lengths,
    residual,
    w_out,
    norm_gain,
    expert_ids,
    route_level,
    w_in,
    w_down,
):
    rows, width = residual.shape
    devs = lax.axis_size("dev")

    w_other = partner(w_out, "side", 1)
    in_other = partner(w_in[0], "side", 1)
    down_other = partner(w_down[0], "side", 1)
    blocks = attend(queries, kv_cache, new_kv, lengths)
    total, sent, more = project(blocks, w_out, w_other, residual, expert_ids, route_level)
    weights = [
        pltpu.with_memory_space_constraint(x, pltpu.VMEM)
        for x in (w_in[0], in_other, w_down[0], down_other)
    ]
    normed, stream = kernel_call(
        norm_kernel,
        (total, more, norm_gain.reshape(1, width)),
        (
            jax.ShapeDtypeStruct(total.shape, jnp.bfloat16),
            pltpu.VMEM((rows, width), jnp.bfloat16),
        ),
    )

    early, late = dev_groups(devs)
    near = {0: normed}
    for away in early + late:
        if away:
            near[away] = across(normed, away, 0)
    home = []
    for group, aways in (("early", early), ("late", late)):
        blocks = [near[away] for away in aways]
        blocks += [across(near[away], 1, 0) for away in aways]
        kept, sent = run_experts(f"experts_{group}", blocks, weights, rows, width)
        for away, block in zip(aways, homeward(kept, sent, group, aways, rows)):
            if away:
                block = across(block, away, 0).astype(jnp.float32)
            home.append(block)
    expert_sum = functools.reduce(jnp.add, home)
    return (stream, expert_sum.astype(jnp.bfloat16))


def solution(mesh):
    by_request = ("groups", "dev", "side")
    return jax.shard_map(
        body,
        mesh=mesh,
        in_specs=(
            P(by_request, None),
            P(by_request, None, None),
            P(by_request, None),
            P(by_request),
            P(by_request, None),
            P("side", None),
            P(),
            P(by_request, None),
            P(by_request, None),
            P(("dev", "side"), None, None),
            P(("dev", "side"), None, None),
        ),
        out_specs=(P(by_request, None), P(by_request, None)),
        check_vma=False,
    )
```
